32 devices in a mesh: section: 2 (over core), dp: 4 (over z), tensor: 4 (over y, x).
Axes of the slice: x: 2, y: 2, z: 4, core: 2. Of those that a mesh axis runs over, the one named last changes fastest.
Arguments:
- tokens: bfloat16 [32, 160, 768], P(('dp', 'tensor')), may hold values from -1.7265625 to 1.7265625
- cotangent: bfloat16 [32, 160, 768], P(('dp', 'tensor')), may hold values from -6 to 6
- lengths: int32 [32], P('dp'), may hold values from 80 to 160, as said below
- chain_type: int32 [32], P('dp'), may hold values 0 or 1
- qkv_weight: bfloat16 [2, 2, 768, 3, 768], P('section', None, None, None, 'tensor'), may hold values from -0.21875 to 0.21875
- qkv_bias: float32 [2, 2, 2, 768], P('section', None, None, 'tensor'), may hold values from -0.8 to 0.8
- out_weight: bfloat16 [2, 2, 768, 768], P('section', None, 'tensor'), may hold values from -0.625 to 0.625
- out_bias: float32 [2, 2, 768], P('section'), may hold values from -0.8 to 0.8
- ffn_in: bfloat16 [2, 2, 768, 3072], P('section', None, None, 'tensor'), may hold values from -0.21875 to 0.21875
- ffn_in_bias: float32 [2, 2, 3072], P('section', None, 'tensor'), may hold values from -0.8 to 0.8
- ffn_out: bfloat16 [2, 2, 3072, 768], P('section', None, 'tensor'), may hold values from -0.109375 to 0.109375
- ffn_out_bias: float32 [2, 2, 768], P('section'), may hold values from -0.8 to 0.8
- norm_gain: float32 [2, 2, 2, 768], P('section'), may hold values from 0.5 to 1.5
- norm_bias: float32 [2, 2, 2, 768], P('section'), may hold values from -0.8 to 0.8
Outputs:
- acts: bfloat16 [2, 32, 160, 768], P('section', ('dp', 'tensor'))
- in_grad: float32 [2, 32, 160, 768], P('section', ('dp', 'tensor'))
- qkv_weight_grad: float32 [2, 2, 768, 3, 768], P('section', None, 'dp', None, 'tensor')
- qkv_bias_grad: float32 [2, 2, 2, 768], P('section', None, None, 'tensor')
- out_weight_grad: float32 [2, 2, 768, 768], P('section', None, 'tensor', 'dp')
- out_bias_grad: float32 [2, 2, 768], P('section')
- ffn_in_grad: float32 [2, 2, 768, 3072], P('section', None, 'dp', 'tensor')
- ffn_in_bias_grad: float32 [2, 2, 3072], P('section', None, 'tensor')
- ffn_out_grad: float32 [2, 2, 3072, 768], P('section', None, 'tensor', 'dp')
- ffn_out_bias_grad: float32 [2, 2, 768], P('section')
- norm_gain_grad: float32 [2, 2, 2, 768], P('section')
- norm_bias_grad: float32 [2, 2, 2, 768], P('section')
The draws below stay inside these ranges and needn't reach their ends.
Inputs may be any that keep to these rules, and one draw needn't show every extreme that they name: `lengths`: real tokens of a chain; the other positions of its 160 are padding. `chain_type`: 0 for a heavy chain, 1 for a light chain.
All inputs are finite; a program needn't handle non-finite values. No bound on the sum of `chain_type` on one device may be relied on, other than what follows from the above.
Results may differ from the reference program's by a relative error of at most 0.02.
Values may be sent and summed in bfloat16 or wider, within the bound.
No kernel may reach another device: no remote copies, remote signals or barrier semaphores. Data moves between devices by JAX's collectives and lax.ppermute only.
A program may use at most 192 MiB of HBM per device.

```python
import math
import jax
import jax.numpy as jnp
from jax import lax

D = 768
HEADS = 12
HEAD_DIM = 64
FF = 3072
LENGTH = 160
TYPES = 2
LAYERS = 2
CHAINS = 32
N_DP = 4


def draw_lengths(key, part):
    drawn = jax.random.randint(key, (CHAINS,), LENGTH // 2, LENGTH + 1)
    pinned = jnp.arange(CHAINS) % 5 == 0
    return jnp.where(pinned, LENGTH, drawn).astype(jnp.int32)


def touch_ends(array, own_key, least, largest):
    place = [jax.random.randint(jax.random.fold_in(own_key, axis), (), 0, length) for axis, length in enumerate(array.shape)]
    longest = array.shape.index(max(array.shape))
    beside = place[:longest] + [(place[longest] + 1) % array.shape[longest]] + place[longest + 1:]
    return array.at[tuple(place)].set(least).at[tuple(beside)].set(largest)


def strengthened(values, key, source, target, parts, factor):
    owner, partner = [(jnp.arange(values.shape[axis_at]) // (values.shape[axis_at] // parts)).reshape([-1 if axis == axis_at else 1 for axis in range(values.ndim)]) for axis_at in (source, target)]
    chosen = jax.random.permutation(key, parts)[partner]
    strong = (owner == chosen) | (owner == (partner + parts // 2) % parts)
    return jnp.where(strong, factor * values, values)


def block_scale(own_key, extent, split, smallest, high):
    level, own = 1.0, jax.random.fold_in(own_key, 6)
    for position, blocks in split:
        draws = jnp.exp(jax.random.uniform(jax.random.fold_in(own, position), (blocks,), jnp.float32, smallest / len(split), high / len(split)))
        level = level * jnp.repeat(draws, extent[position] // blocks).reshape([-1 if axis == position else 1 for axis in range(len(extent))])
    return level


def noise(rng, dims, scale, most, cuts=(), kind=jnp.bfloat16):
    values = jax.random.normal(rng, dims, jnp.float32) * scale
    if len(cuts) > 0:
        values = block_scale(rng, dims, cuts, -0.22, 0.18) * values
    return jnp.clip(values, min=-most, max=most).astype(kind)


def heavy_noise(stream_key, shape, scale, reach, pieces, heavy, kind=jnp.bfloat16):
    array = scale * jax.random.normal(stream_key, shape, jnp.float32)
    if pieces:
        array = array * block_scale(stream_key, shape, pieces, -0.22, 0.18)
    return jnp.clip(strengthened(array, jax.random.fold_in(stream_key, 3), *heavy), -reach, reach).astype(kind)


def setup_inputs(seed: int = 0) -> dict:
    seeds = jax.random.split(jax.random.key(seed), 15)
    tokens = jnp.clip(jax.random.uniform(seeds[0], (CHAINS, LENGTH, D), jnp.float32, -1.7265625, 1.7265625) * block_scale(seeds[0], (CHAINS, LENGTH, D), ((0, 16),), -0.4, 0.0), -1.7265625, 1.7265625).astype(jnp.bfloat16)
    cotangent = heavy_noise(seeds[1], (CHAINS, LENGTH, D), 1.0, 6.0, ((0, 16),), (0, 2, 16, 2.0))
    lengths = draw_lengths(jax.random.fold_in(seeds[14], 71), 0)
    chain_type = touch_ends((jax.random.randint(seeds[3], (CHAINS,), 0, 3) < 1).astype(jnp.int32), jax.random.fold_in(seeds[3], 1), 0, 1)
    qkv_weight = noise(seeds[4], (LAYERS, TYPES, D, 3, D), D ** -0.5, 0.21875, ((0, 2), (4, 4)))
    qkv_bias = jnp.clip(jax.random.uniform(seeds[5], (LAYERS, TYPES, 2, D), jnp.float32, -0.8, 0.8) * block_scale(seeds[5], (LAYERS, TYPES, 2, D), ((0, 2), (3, 4)), -0.4, 0.0), -0.8, 0.8)
    out_weight = noise(seeds[6], (LAYERS, TYPES, D, D), (D // 8) ** -0.5, 0.625, ((0, 2), (2, 4)))
    out_bias = jnp.clip(jax.random.uniform(seeds[7], (LAYERS, TYPES, D), jnp.float32, -0.8, 0.8) * block_scale(seeds[7], (LAYERS, TYPES, D), ((0, 2),), -0.4, 0.0), -0.8, 0.8)
    ffn_in = noise(seeds[8], (LAYERS, TYPES, D, FF), D ** -0.5, 0.21875, ((0, 2), (3, 4)))
    ffn_in_bias = jnp.clip(jax.random.uniform(seeds[9], (LAYERS, TYPES, FF), jnp.float32, -0.8, 0.8) * block_scale(seeds[9], (LAYERS, TYPES, FF), ((0, 2), (2, 4)), -0.4, 0.0), -0.8, 0.8)
    ffn_out = noise(seeds[10], (LAYERS, TYPES, FF, D), FF ** -0.5, 0.109375, ((0, 2), (2, 4)))
    ffn_out_bias = jnp.clip(jax.random.uniform(seeds[11], (LAYERS, TYPES, D), jnp.float32, -0.8, 0.8) * block_scale(seeds[11], (LAYERS, TYPES, D), ((0, 2),), -0.4, 0.0), -0.8, 0.8)
    norm_gain = jnp.clip(1.0 + 0.1 * jax.random.normal(seeds[12], (LAYERS, TYPES, 2, D), jnp.float32), 0.5, 1.5)
    norm_bias = jnp.clip(jax.random.uniform(seeds[13], (LAYERS, TYPES, 2, D), jnp.float32, -0.8, 0.8) * block_scale(seeds[13], (LAYERS, TYPES, 2, D), ((0, 2),), -0.4, 0.0), -0.8, 0.8)
    return {"tokens": tokens, "cotangent": cotangent, "lengths": lengths, "chain_type": chain_type, "qkv_weight": qkv_weight, "qkv_bias": qkv_bias, "out_weight": out_weight, "out_bias": out_bias, "ffn_in": ffn_in, "ffn_in_bias": ffn_in_bias, "ffn_out": ffn_out, "ffn_out_bias": ffn_out_bias, "norm_gain": norm_gain, "norm_bias": norm_bias}


HIGH = lax.Precision.HIGHEST

@jax.custom_vjp
def low(v):
    return lax.optimization_barrier(v.astype(jnp.bfloat16)).astype(jnp.float32)

@jax.custom_vjp
def low_back(v):
    return v

def low_keep(v):
    return (low(v), None)

def low_pass(kept, grad):
    return (grad,)

def back_keep(v):
    return (v, None)

def back_low(kept, grad):
    return (low(grad),)
low.defvjp(low_keep, low_pass)
low_back.defvjp(back_keep, back_low)

def pick(select, table):
    return jnp.einsum('ct,t...->c...', select, table, precision=HIGH)

def typed(select, spec, left, table):
    running = jnp.zeros((), jnp.float32)
    for type_index in range(TYPES):
        type_term = jnp.einsum(spec, left, table[type_index], precision=HIGH)
        shape = (-1,) + (1,) * (type_term.ndim - 1)
        running = running + select[:, type_index].reshape(shape) * type_term
    return running

def normalize(values, gain, shift):
    center = values - lax.optimization_barrier(jnp.mean(values, axis=-1, keepdims=True))
    spread = lax.optimization_barrier(jnp.mean(center * center, axis=-1, keepdims=True))
    return center * lax.rsqrt(spread + 1e-06) * gain + shift

def layer(inputs, select, keep, params):
    qkv_w, qkv_b, out_w, out_b, in_w, in_b, back_w, back_b, gains, shifts = params
    chains = inputs.shape[0]
    proj = typed(select, 'cld,dke->clke', inputs, qkv_w)
    bias_rows = pick(select, qkv_b)
    heads_shape = (chains, LENGTH, HEADS, HEAD_DIM)
    query_rows = low_back(low(proj[:, :, 0] + bias_rows[:, None, 0])).reshape(heads_shape)
    key_rows = low_back(low(proj[:, :, 1])).reshape(heads_shape)
    value_rows = low_back(low(proj[:, :, 2] + bias_rows[:, None, 1])).reshape(heads_shape)
    scores = jnp.einsum('cqhe,ckhe->chqk', query_rows, key_rows, precision=HIGH) * (1.0 / math.sqrt(HEAD_DIM))
    scores = jnp.where(keep[:, None, None, :], scores, -1000000000.0)
    scores = low_back(scores)
    attn_probs = low(jax.nn.softmax(scores, axis=-1))
    attended = jnp.einsum('chqk,ckhe->cqhe', attn_probs, value_rows, precision=HIGH).reshape(chains, LENGTH, D)
    attended = low_back(low(attended))
    mixed = inputs + low_back(typed(select, 'cle,ed->cld', attended, out_w)) + pick(select, out_b)[:, None]
    gain_rows = pick(select, gains)
    shift_rows = pick(select, shifts)
    normed = normalize(mixed, gain_rows[:, None, 0], shift_rows[:, None, 0])
    pre_act = low_back(typed(select, 'cld,df->clf', low(normed), in_w) + pick(select, in_b)[:, None])
    hidden = low(jax.nn.gelu(pre_act, approximate=False))
    summed = normed + low_back(typed(select, 'clf,fd->cld', hidden, back_w)) + pick(select, back_b)[:, None]
    return normalize(summed, gain_rows[:, None, 1], shift_rows[:, None, 1])

def reference(tokens, cotangent, lengths, chain_type, qkv_weight, qkv_bias, out_weight, out_bias, ffn_in, ffn_in_bias, ffn_out, ffn_out_bias, norm_gain, norm_bias):
    groups = N_DP
    block_size = CHAINS // groups
    select = (chain_type[:, None] == jnp.arange(TYPES)[None, :]).astype(jnp.float32)
    keep = jnp.arange(LENGTH)[None, :] < lengths[:, None]
    params = tuple((weight.astype(jnp.float32) for weight in (qkv_weight, qkv_bias, out_weight, out_bias, ffn_in, ffn_in_bias, ffn_out, ffn_out_bias, norm_gain, norm_bias)))

    def forward(inputs, offset, *weights):

        def block_fn(carry, items):
            block_in, block_off, block_sel, block_keep = items
            first_out = low(layer(block_in, block_sel, block_keep, tuple((weight[0] for weight in weights))))
            second_out = layer(low_back(first_out) + block_off, block_sel, block_keep, tuple((weight[1] for weight in weights)))
            return (carry, (first_out, second_out))
        items = (inputs.reshape(groups, block_size, LENGTH, D), offset.reshape(groups, block_size, LENGTH, D), select.reshape(groups, block_size, TYPES), keep.reshape(groups, block_size, LENGTH))
        _, (first_out, second_out) = lax.scan(jax.checkpoint(block_fn), jnp.zeros((), jnp.float32), items)
        return (second_out.reshape(CHAINS, LENGTH, D), first_out.reshape(CHAINS, LENGTH, D))
    zero_off = jnp.zeros((CHAINS, LENGTH, D), jnp.float32)
    second_out, vjp_fn, first_out = jax.vjp(forward, tokens.astype(jnp.float32), zero_off, *params, has_aux=True)
    grads = vjp_fn(cotangent.astype(jnp.float32))
    acts = jnp.stack([first_out, second_out]).astype(jnp.bfloat16)
    in_grad = jnp.stack([grads[0], grads[1]])
    return (acts, in_grad, grads[2], grads[3], grads[4], grads[5], grads[6], grads[7], grads[8], grads[9], grads[10], grads[11])
```

```python
import functools
import math

import jax
import jax.numpy as jnp
from jax import lax
from jax.experimental import pallas as pl
from jax.experimental.pallas import tpu as pltpu
from jax.sharding import PartitionSpec as P

HEAD_DIM = 64
TYPES = 2
LAYERS = 2
SPLIT = 1
EPS = 1e-06
HALF_ROOT = 0.7071067811865476
DENSITY = 0.3989422804014327
SCALE = 1.0 / math.sqrt(HEAD_DIM)
MIB = 1 << 20

F32 = jnp.float32
BF16 = jnp.bfloat16

OUT_B, BACK_B, GAIN1, GAIN2, SHIFT1, SHIFT2, IN_B, QKV_B = range(0, 16, 2)


def dot(a, b):
    return jnp.dot(a, b, preferred_element_type=F32)


def dot_nt(a, b):
    return lax.dot_general(a, b, (((1,), (1,)), ((), ())), preferred_element_type=F32)


def dot_tn(a, b):
    return lax.dot_general(a, b, (((0,), (0,)), ((), ())), preferred_element_type=F32)


def nested(structure, flat):
    leaves, tree = jax.tree.flatten(structure)
    return jax.tree.unflatten(tree, flat)


def run(name, body, meta, ins, outs, flops=0, limit=16):
    flat_in, flat_out = jax.tree.leaves(ins), jax.tree.leaves(outs)

    def kernel(meta_ref, *refs):
        body(meta_ref, nested(ins, refs[: len(flat_in)]), nested(outs, refs[len(flat_in) :]))

    vmem = pl.BlockSpec(memory_space=pltpu.VMEM)
    moved = sum(math.prod(a.shape) * a.dtype.itemsize for a in flat_in + flat_out)
    results = pl.pallas_call(
        kernel,
        name=name,
        in_specs=[pl.BlockSpec(memory_space=pltpu.SMEM)] + [vmem] * len(flat_in),
        out_specs=[vmem] * len(flat_out),
        out_shape=flat_out,
        compiler_params=pltpu.CompilerParams(vmem_limit_bytes=limit * MIB),
        cost_estimate=pl.CostEstimate(flops=int(flops), bytes_accessed=moved, transcendentals=0),
    )(meta, *flat_in)
    return nested(outs, results)


def arr(shape, dtype=BF16):
    return jax.ShapeDtypeStruct(tuple(shape), dtype)


class Ids:
    def __init__(self, meta, dims):
        self.meta, self.dims = meta, dims
        self.section, self.tensor, self.dp = meta[0], meta[1], meta[2]

    def chain(self, slot):
        return (self.tensor ^ slot) * self.dims.per_chip + self.section

    def kind(self, slot):
        return self.meta[3 + self.chain(slot)]

    def length(self, slot):
        return self.meta[3 + self.dims.group + self.chain(slot)]


def on_weights(ids, layer, own, other, go):
    pl.when(ids.section == layer)(lambda: go(*own))
    pl.when(ids.section != layer)(lambda: go(*other))


class Dims:
    pass


def attention_forward(dims, layer, meta, rows, own, other, small):
    r, slots, length, width = dims.r, dims.slots, dims.length, dims.width

    def body(meta_ref, ins, outs):
        rows, own, other, small = ins
        parts, qkv, att = outs
        ids = Ids(meta_ref, dims)

        def go(qkv_w, out_w):
            for k in range(slots):
                kind = ids.kind(k)
                bias = small[pl.ds(QKV_B + kind, 1), : 3 * width]
                for h in range(SPLIT):
                    qkv[k, h * r : (h + 1) * r, :] = (dot(rows[h][k][...], qkv_w[kind]) + bias).astype(BF16)
                keep = lax.broadcasted_iota(jnp.int32, (1, length), 1) < ids.length(k)
                for c in range(0, width, HEAD_DIM):
                    query = qkv[k, :, c : c + HEAD_DIM]
                    key = qkv[k, :, width + c : width + c + HEAD_DIM]
                    value = qkv[k, :, 2 * width + c : 2 * width + c + HEAD_DIM]
                    scores = jnp.where(keep, dot_nt(query, key) * SCALE, -1e9)
                    expd = jnp.exp(scores - jnp.max(scores, axis=-1, keepdims=True))
                    probs = (expd * (1.0 / jnp.sum(expd, axis=-1, keepdims=True))).astype(BF16)
                    att[k, :, c : c + HEAD_DIM] = dot(probs, value).astype(BF16)
                for h in range(SPLIT):
                    parts[h][k][...] = dot(att[k, h * r : (h + 1) * r, :], out_w[kind]).astype(BF16)

        on_weights(ids, layer, own, other, go)

    outs = (
        [[arr((r, dims.d))] * slots for _ in range(SPLIT)],
        arr((slots, length, 3 * width)),
        arr((slots, length, width)),
    )
    flops = 2 * slots * length * dims.d * 4 * width
    return run(f"attn_fwd{layer}", body, meta, (rows, own, other, small), outs, flops)


def attention_backward(dims, layer, meta, grads, qkv, own, other):
    r, slots, length, width = dims.r, dims.slots, dims.length, dims.width

    def body(meta_ref, ins, outs):
        grads, qkv, own, other = ins
        parts, dqkv = outs
        ids = Ids(meta_ref, dims)

        def go(qkv_w, out_w):
            for k in range(slots):
                kind = ids.kind(k)
                keep = lax.broadcasted_iota(jnp.int32, (1, length), 1) < ids.length(k)
                datt = jnp.concatenate(
                    [dot_nt(grads[h][k][...], out_w[kind]).astype(BF16) for h in range(SPLIT)], axis=0
                )
                for c in range(0, width, HEAD_DIM):
                    query = qkv[k, :, c : c + HEAD_DIM]
                    key = qkv[k, :, width + c : width + c + HEAD_DIM]
                    value = qkv[k, :, 2 * width + c : 2 * width + c + HEAD_DIM]
                    da = datt[:, c : c + HEAD_DIM]
                    scores = jnp.where(keep, dot_nt(query, key) * SCALE, -1e9)
                    expd = jnp.exp(scores - jnp.max(scores, axis=-1, keepdims=True))
                    probs = expd * (1.0 / jnp.sum(expd, axis=-1, keepdims=True))
                    dprobs = dot_nt(da, value)
                    dscores = (
                        probs * (dprobs - jnp.sum(probs * dprobs, axis=-1, keepdims=True))
                    ).astype(BF16)
                    dqkv[k, :, c : c + HEAD_DIM] = (dot(dscores, key) * SCALE).astype(BF16)
                    dqkv[k, :, width + c : width + c + HEAD_DIM] = (
                        dot_tn(dscores, query) * SCALE
                    ).astype(BF16)
                    dqkv[k, :, 2 * width + c : 2 * width + c + HEAD_DIM] = dot_tn(
                        probs.astype(BF16), da
                    ).astype(BF16)
                for h in range(SPLIT):
                    parts[h][k][...] = dot_nt(dqkv[k, h * r : (h + 1) * r, :], qkv_w[kind]).astype(BF16)

        on_weights(ids, layer, own, other, go)

    outs = (
        [[arr((r, dims.d))] * slots for _ in range(SPLIT)],
        arr((slots, length, 3 * width)),
    )
    flops = 2 * slots * length * dims.d * 4 * width
    return run(f"attn_bwd{layer}", body, meta, (grads, qkv, own, other), outs, flops)


def typed_sum(ids, left, right, kind, slots):
    chosen = [
        jnp.where(ids.kind(k) == kind, right[k], jnp.zeros_like(right[k])) for k in range(slots)
    ]
    return dot_tn(jnp.concatenate(left, axis=0), jnp.concatenate(chosen, axis=0))


def joined(refs, k):
    return jnp.concatenate([refs[h][k][...] for h in range(SPLIT)], axis=0)


def row_sums(ids, slots, rows, out, cols):
    for kind in range(TYPES):
        total = jnp.zeros((1, cols), F32)
        for k in range(slots):
            here = jnp.sum(rows(k).astype(F32), axis=0, keepdims=True)
            total = total + jnp.where(ids.kind(k) == kind, here, 0.0)
        out[kind : kind + 1, :cols] = total


def attention_weights(dims, layer, meta, rows, dqkv, grads, att):
    slots, width, d = dims.slots, dims.width, dims.d

    def body(meta_ref, ins, outs):
        rows, dqkv, grads, att = ins
        total, bias = outs
        ids = Ids(meta_ref, dims)
        left = [joined(rows, k) for k in range(slots)]
        back = [joined(grads, k) for k in range(slots)]
        for kind in range(TYPES):
            total[kind, :, : 3 * width] = typed_sum(
                ids, left, [dqkv[k] for k in range(slots)], kind, slots
            ).astype(BF16)
            total[kind, :, 3 * width :] = typed_sum(
                ids, back, [att[k] for k in range(slots)], kind, slots
            ).astype(BF16)
        bias[...] = jnp.zeros_like(bias)
        row_sums(ids, slots, lambda k: dqkv[k], bias, 3 * width)

    outs = (arr((TYPES, d, 4 * width)), arr((TYPES, d), F32))
    flops = 2 * 2 * slots * dims.length * d * 4 * width
    return run(f"attn_dw{layer}", body, meta, (rows, dqkv, grads, att), outs, flops, 24)


def ffn_forward(dims, layer, meta, rows, own, other, small):
    r, slots, hidden = dims.r, dims.slots, dims.hidden

    def body(meta_ref, ins, outs):
        rows, own, other, small = ins
        parts, act, slope = outs
        ids = Ids(meta_ref, dims)

        def go(in_w, back_w):
            for k in range(slots):
                kind = ids.kind(k)
                pre = dot(rows[k][...], in_w[kind]) + small[pl.ds(IN_B + kind, 1), :hidden]
                gate = 0.5 * (1.0 + lax.erf(pre * HALF_ROOT))
                act[k] = (pre * gate).astype(BF16)
                slope[k] = (gate + pre * (DENSITY * jnp.exp(-0.5 * pre * pre))).astype(BF16)
                parts[k][...] = dot(act[k], back_w[kind]).astype(BF16)

        on_weights(ids, layer, own, other, go)

    outs = ([arr((r, dims.d))] * slots, arr((slots, r, hidden)), arr((slots, r, hidden)))
    flops = 4 * slots * r * dims.d * hidden
    return run(f"ffn_fwd{layer}", body, meta, (rows, own, other, small), outs, flops)


def ffn_backward(dims, layer, meta, grads, slope, own, other):
    r, slots, hidden = dims.r, dims.slots, dims.hidden

    def body(meta_ref, ins, outs):
        grads, slope, own, other = ins
        parts, dpre = outs
        ids = Ids(meta_ref, dims)

        def go(in_w, back_w):
            for k in range(slots):
                kind = ids.kind(k)
                dact = dot_nt(grads[k][...], back_w[kind])
                dpre[k] = (dact * slope[k].astype(F32)).astype(BF16)
                parts[k][...] = dot_nt(dpre[k], in_w[kind]).astype(BF16)

        on_weights(ids, layer, own, other, go)

    outs = ([arr((r, dims.d))] * slots, arr((slots, r, hidden)))
    flops = 4 * slots * r * dims.d * hidden
    return run(f"ffn_bwd{layer}", body, meta, (grads, slope, own, other), outs, flops)


def ffn_weights(dims, layer, meta, rows, dpre, grads, act):
    slots, hidden, d = dims.slots, dims.hidden, dims.d

    def body(meta_ref, ins, outs):
        rows, dpre, grads, act = ins
        total, bias = outs
        ids = Ids(meta_ref, dims)
        for step, (left, right) in enumerate(((rows, dpre), (grads, act))):
            left_rows = [joined(left, k) for k in range(slots)]
            right_rows = [joined(right, k) for k in range(slots)]
            for kind in range(TYPES):
                total[TYPES * step + kind] = typed_sum(ids, left_rows, right_rows, kind, slots).astype(BF16)
        row_sums(ids, slots, lambda k: joined(dpre, k), bias, hidden)

    outs = (arr((2 * TYPES, d, hidden)), arr((TYPES, hidden), F32))
    flops = 2 * 4 * slots * dims.length * d * hidden
    split = lambda a: [[a[h][k] for k in range(slots)] for h in range(SPLIT)]
    return run(f"ffn_dw{layer}", body, meta, (rows, dpre, grads, act), outs, flops, 24)


def normalized(values):
    center = values - jnp.mean(values, axis=-1, keepdims=True)
    inv = lax.rsqrt(jnp.mean(center * center, axis=-1, keepdims=True) + EPS)
    return center * inv, inv


def summed(parts):
    total = parts[0][...].astype(F32)
    for part in parts[1:]:
        total = total + part[...].astype(F32)
    return total


def norm_back(grad, normal, inv, gain):
    scaled = grad * gain
    return inv * (
        scaled
        - jnp.mean(scaled, axis=-1, keepdims=True)
        - normal * jnp.mean(scaled * normal, axis=-1, keepdims=True)
    )


def sum_rows(out, values):
    for row, value in enumerate(values):
        out[row : row + 1, :] = jnp.sum(value, axis=0, keepdims=True)
    out[len(values) :, :] = jnp.zeros((out.shape[0] - len(values), out.shape[1]), F32)


def first_norm(dims, layer, meta, own_rows, parts, small):
    r, d = dims.r, dims.d

    def body(meta_ref, ins, outs):
        own_rows, parts, small = ins
        low, normal, inv = outs
        kind = Ids(meta_ref, dims).kind(0)
        mixed = own_rows[...].astype(F32) + summed(parts) + small[pl.ds(OUT_B + kind, 1), :]
        xhat, scale = normalized(mixed)
        normal[...] = xhat
        inv[...] = jnp.broadcast_to(scale, inv.shape)
        low[...] = (xhat * small[pl.ds(GAIN1 + kind, 1), :] + small[pl.ds(SHIFT1 + kind, 1), :]).astype(BF16)

    outs = (arr((r, d)), arr((r, d), F32), arr((r, 128), F32))
    return run(f"norm1_{layer}", body, meta, (own_rows, parts, small), outs)


def second_values(kind, normal, parts, small):
    normed = normal[...] * small[pl.ds(GAIN1 + kind, 1), :] + small[pl.ds(SHIFT1 + kind, 1), :]
    xhat, scale = normalized(normed + summed(parts) + small[pl.ds(BACK_B + kind, 1), :])
    output = xhat * small[pl.ds(GAIN2 + kind, 1), :] + small[pl.ds(SHIFT2 + kind, 1), :]
    return xhat, scale, output.astype(BF16)


def second_norm(dims, layer, meta, normal, parts, small):
    r, d = dims.r, dims.d

    def body(meta_ref, ins, outs):
        normal, parts, small = ins
        low, xhat_ref, inv = outs
        kind = Ids(meta_ref, dims).kind(0)
        xhat, scale, low[...] = second_values(kind, normal, parts, small)
        xhat_ref[...] = xhat
        inv[...] = jnp.broadcast_to(scale, inv.shape)

    outs = (arr((r, d)), arr((r, d), F32), arr((r, 128), F32))
    return run(f"norm2_{layer}", body, meta, (normal, parts, small), outs)


def second_back(kind, grad, xhat, scale, small, second_grad, low, sums):
    value = norm_back(grad, xhat, scale, small[pl.ds(GAIN2 + kind, 1), :])
    second_grad[...] = value
    low[...] = value.astype(BF16)
    sum_rows(sums, (grad * xhat, grad, value))


def last_norm(dims, layer, meta, normal, parts, small, cotangent):
    r, d = dims.r, dims.d

    def body(meta_ref, ins, outs):
        normal, parts, small, cotangent = ins
        act, second_grad, low, sums = outs
        kind = Ids(meta_ref, dims).kind(0)
        xhat, scale, act[...] = second_values(kind, normal, parts, small)
        second_back(kind, cotangent[...].astype(F32), xhat, scale, small, second_grad, low, sums)

    outs = (arr((r, d)), arr((r, d), F32), arr((r, d)), arr((8, d), F32))
    return run(f"norm2_{layer}", body, meta, (normal, parts, small, cotangent), outs)


def between_layers(dims, layer, meta, parts, first_grad, xhat, inv, small):
    r, d = dims.r, dims.d

    def body(meta_ref, ins, outs):
        parts, first_grad, xhat, inv, small = ins
        input_grad, second_grad, low, sums = outs
        kind = Ids(meta_ref, dims).kind(0)
        value = summed(parts) + first_grad[...]
        input_grad[...] = value
        grad = value.astype(BF16).astype(F32)
        second_back(kind, grad, xhat[...], inv[:, :1], small, second_grad, low, sums)

    outs = (arr((r, d), F32), arr((r, d), F32), arr((r, d)), arr((8, d), F32))
    return run(f"between{layer}", body, meta, (parts, first_grad, xhat, inv, small), outs)


def first_back(dims, layer, meta, parts, second_grad, xhat, inv, small):
    r, d = dims.r, dims.d

    def body(meta_ref, ins, outs):
        parts, second_grad, xhat, inv, small = ins
        first_grad, low, sums = outs
        kind = Ids(meta_ref, dims).kind(0)
        grad = summed(parts) + second_grad[...]
        value = norm_back(grad, xhat[...], inv[:, :1], small[pl.ds(GAIN1 + kind, 1), :])
        first_grad[...] = value
        low[...] = value.astype(BF16)
        sum_rows(sums, (grad * xhat[...], grad, value))

    outs = (arr((r, d), F32), arr((r, d)), arr((8, d), F32))
    return run(f"norm1_back{layer}", body, meta, (parts, second_grad, xhat, inv, small), outs)


def input_gradient(dims, layer, meta, parts, first_grad):
    def body(meta_ref, ins, outs):
        parts, first_grad = ins
        outs[...] = summed(parts) + first_grad[...]

    return run(f"input_grad{layer}", body, meta, (parts, first_grad), arr((dims.r, dims.d), F32))


def swap(value, axis, bit):
    count = lax.axis_size(axis)
    return lax.ppermute(value, axis, [(source, source ^ bit) for source in range(count)])


def gather(value, slots):
    return [value] + [swap(value, "tensor", k) for k in range(1, slots)]


def scatter(parts):
    return [parts[0]] + [swap(part, "tensor", k) for k, part in enumerate(parts) if k]


class GradSum:
    def __init__(self, dims, layer, meta, value, name):
        self.dims, self.layer, self.meta, self.value, self.name = dims, layer, meta, value, name
        self.rows = value.shape[1] // dims.dp
        self.other = lax.ppermute(value, "section", [(1 - layer, layer)])
        if dims.dp == 4:
            self.halved()
        else:
            whole = (self.value.astype(F32) + self.other.astype(F32)).astype(BF16)
            self.direct = lax.psum_scatter(whole, "dp", scatter_dimension=1, tiled=True)

    def permute(self, value, bit):
        base = self.layer * self.dims.dp
        pairs = [(base + z, base + (z ^ bit)) for z in range(self.dims.dp)]
        return lax.ppermute(value, ("section", "dp"), pairs)

    def halved(self):
        dims, rows = self.dims, self.rows
        count, _, cols = self.value.shape

        def part(ref, chunk):
            return ref[:, pl.ds(pl.multiple_of(chunk * rows, 16), rows), :].astype(F32)

        def first(meta_ref, ins, outs):
            value, other = ins
            z = Ids(meta_ref, dims).dp
            for i in range(2):
                chunk = 2 * i + 1 - lax.rem(z, 2)
                outs[i] = (part(value, chunk) + part(other, chunk)).astype(BF16)

        sent = run(f"{self.name}_a", first, self.meta, (self.value, self.other), arr((2, count, rows, cols)))
        near = self.permute(sent, 1)

        def second(meta_ref, ins, outs):
            value, other, near = ins
            chunk = Ids(meta_ref, dims).dp ^ 2
            total = part(value, chunk) + part(other, chunk) + near[lax.div(chunk, 2)].astype(F32)
            outs[...] = total.astype(BF16)

        sent = run(f"{self.name}_b", second, self.meta, (self.value, self.other, near), arr((count, rows, cols)))
        self.pieces = (self.value, self.other, near, self.permute(sent, 2))

    def total(self, ids, pieces, index):
        if self.dims.dp != 4:
            return pieces[index].astype(F32)
        value, other, near, far = pieces
        start = pl.multiple_of(ids.dp * self.rows, 16)
        return (
            value[index, pl.ds(start, self.rows), :].astype(F32)
            + other[index, pl.ds(start, self.rows), :].astype(F32)
            + near[lax.div(ids.dp, 2), index].astype(F32)
            + far[index].astype(F32)
        )

    def operands(self):
        return self.pieces if self.dims.dp == 4 else self.direct


def finish(dims, meta, sums, kinds, name):
    rows = sums[0].rows
    outs = [arr((TYPES, hi - lo, rows) if flip else (TYPES, rows, hi - lo), F32) for _, lo, hi, flip in kinds]

    def body(meta_ref, ins, outs):
        ids = Ids(meta_ref, dims)

        def go(layer):
            for out, (base, lo, hi, flip) in zip(outs, kinds):
                for kind in range(TYPES):
                    total = sums[layer].total(ids, ins[layer], base + kind)[:, lo:hi]
                    out[kind] = total.T if flip else total

        for layer in range(LAYERS):
            pl.when(ids.section == layer)(functools.partial(go, layer))

    return run(name, body, meta, [s.operands() for s in sums], outs, 0, 24)


def small_total(value, axes):
    for axis in axes:
        bit = 1
        while bit < lax.axis_size(axis):
            value = value + swap(value, axis, bit)
            bit *= 2
    return value


def body(
    tokens,
    cotangent,
    lengths,
    chain_type,
    qkv_weight,
    qkv_bias,
    out_weight,
    out_bias,
    ffn_in,
    ffn_in_bias,
    ffn_out,
    ffn_out_bias,
    norm_gain,
    norm_bias,
):
    dims = Dims()
    dims.per_chip, dims.length, dims.d = tokens.shape
    dims.slots = lax.axis_size("tensor")
    dims.dp = lax.axis_size("dp")
    dims.group = lengths.shape[0]
    dims.width = qkv_weight.shape[-1]
    dims.hidden = ffn_in.shape[-1]
    dims.r = dims.length // SPLIT
    sections = lax.axis_size("section")
    assert dims.per_chip == sections == LAYERS and dims.slots & (dims.slots - 1) == 0
    assert dims.dp & (dims.dp - 1) == 0 and 4 * dims.width == dims.d == dims.hidden
    r, d, width = dims.r, dims.d, dims.width
    section = lax.axis_index("section")
    meta = jnp.concatenate(
        [
            jnp.stack([section, lax.axis_index("tensor"), lax.axis_index("dp")]).astype(jnp.int32),
            chain_type,
            lengths,
        ]
    )
    first = section == 0

    def halves(value):
        return [value[h * r : (h + 1) * r] for h in range(SPLIT)]

    own_rows = halves(jnp.where(first, tokens[0], tokens[1]))
    own_cot = halves(jnp.where(first, cotangent[0], cotangent[1]))
    rows = [gather(own_rows[h], dims.slots) for h in range(SPLIT)]

    padded = jnp.concatenate(
        [
            qkv_bias[0, :, 0],
            jnp.zeros_like(qkv_bias[0, :, 0]),
            qkv_bias[0, :, 1],
            jnp.zeros_like(qkv_bias[0, :, 0]),
        ],
        axis=-1,
    )
    packed = jnp.concatenate(
        [
            out_bias[0],
            ffn_out_bias[0],
            norm_gain[0, :, 0],
            norm_gain[0, :, 1],
            norm_bias[0, :, 0],
            norm_bias[0, :, 1],
            ffn_in_bias[0],
            padded,
        ],
        axis=0,
    )
    qkv_own = qkv_weight[0].reshape(TYPES, d, 3 * width)
    weights = [qkv_own, out_weight[0], ffn_in[0], ffn_out[0]]
    swapped = [swap(weight, "section", 1) for weight in weights]
    packed_other = swap(packed, "section", 1)

    def order(meta_ref, ins, outs):
        here = meta_ref[0] == 0
        own, other = ins[0][...], ins[1][...]
        outs[0][...] = jnp.where(here, own, other)
        outs[1][...] = jnp.where(here, other, own)

    small = run("params", order, meta, [packed, packed_other], [arr(packed.shape, F32)] * 2)
    attn_own, attn_other = tuple(weights[:2]), tuple(swapped[:2])
    ffn_own, ffn_other = tuple(weights[2:]), tuple(swapped[2:])
    span = range(SPLIT)

    saved = []
    acts = []
    for layer in range(LAYERS):
        parts, qkv, att = attention_forward(dims, layer, meta, rows, attn_own, attn_other, small[layer])
        parts = [scatter(parts[h]) for h in span]
        firsts = [first_norm(dims, layer, meta, own_rows[h], parts[h], small[layer]) for h in span]
        normed = [gather(firsts[h][0], dims.slots) for h in span]
        ffn = [ffn_forward(dims, layer, meta, normed[h], ffn_own, ffn_other, small[layer]) for h in span]
        parts = [scatter(ffn[h][0]) for h in span]
        if layer < LAYERS - 1:
            seconds = [second_norm(dims, layer, meta, firsts[h][1], parts[h], small[layer]) for h in span]
        else:
            seconds = [
                last_norm(dims, layer, meta, firsts[h][1], parts[h], small[layer], own_cot[h]) for h in span
            ]
        saved.append((rows, qkv, att, firsts, normed, ffn, seconds))
        own_rows = [seconds[h][0] for h in span]
        acts.append(jnp.concatenate(own_rows, axis=0) if SPLIT > 1 else own_rows[0])
        if layer < LAYERS - 1:
            rows = [gather(own_rows[h], dims.slots) for h in span]

    grad_parts = [seconds[h][1:] for h in span]
    input_grads = [None] * LAYERS
    ffn_sums, attn_sums = [None] * LAYERS, [None] * LAYERS
    norm_sums = [None] * LAYERS
    biases = [None] * LAYERS
    for layer in reversed(range(LAYERS)):
        rows, qkv, att, firsts, normed, ffn, seconds = saved[layer]
        second_grad = [grad_parts[h][0] for h in span]
        grads = [gather(grad_parts[h][1], dims.slots) for h in span]
        back = [ffn_backward(dims, layer, meta, grads[h], ffn[h][2], ffn_own, ffn_other) for h in span]
        parts = [scatter(back[h][0]) for h in span]
        ffn_grad, in_bias_grad = ffn_weights(
            dims,
            layer,
            meta,
            normed,
            [[b[1][k] for k in range(dims.slots)] for b in back] if False else [b[1] for b in back],
            grads,
            [f[1] for f in ffn],
        )
        ffn_sums[layer] = GradSum(dims, layer, meta, ffn_grad, f"ffn_sum{layer}")
        ones = [
            first_back(dims, layer, meta, parts[h], second_grad[h], firsts[h][1], firsts[h][2], small[layer])
            for h in span
        ]
        norm_sums[layer] = ([o[2] for o in ones], [grad_parts[h][2] for h in span])
        grads = [gather(ones[h][1], dims.slots) for h in span]
        parts, dqkv = attention_backward(dims, layer, meta, grads, qkv, attn_own, attn_other)
        parts = [scatter(parts[h]) for h in span]
        attn_grad, qkv_bias_grad = attention_weights(dims, layer, meta, rows, dqkv, grads, att)
        attn_sums[layer] = GradSum(dims, layer, meta, attn_grad, f"attn_sum{layer}")
        biases[layer] = (qkv_bias_grad, in_bias_grad)
        if layer > 0:
            seconds = saved[layer - 1][6]
            results = [
                between_layers(
                    dims, layer, meta, parts[h], ones[h][0], seconds[h][1], seconds[h][2], small[layer - 1]
                )
                for h in span
            ]
            input_grads[layer] = [o[0] for o in results]
            grad_parts = [o[1:] for o in results]
        else:
            input_grads[layer] = [input_gradient(dims, layer, meta, parts[h], ones[h][0]) for h in span]

    def collect(meta_ref, ins, outs):
        ids = Ids(meta_ref, dims)
        kind = ids.kind(0)
        for place, layer in ((outs[0], ids.section), (outs[1], 1 - ids.section)):

            def put(which, place=place):
                ones, twos = ins[which]
                one = sum(ref[...] for ref in ones)
                two = sum(ref[...] for ref in twos)
                for t in range(TYPES):
                    here = kind == t
                    place[8 * t : 8 * t + 3, :] = jnp.where(here, one[:3], 0.0)
                    place[8 * t + 3 : 8 * t + 6, :] = jnp.where(here, two[:3], 0.0)
                    place[8 * t + 6 : 8 * t + 8, :] = jnp.zeros((2, d), F32)

            for which in range(LAYERS):
                pl.when(layer == which)(functools.partial(put, which))

    kept, sent = run("norm_sums", collect, meta, norm_sums, [arr((8 * TYPES, d), F32)] * 2)
    norm_total = small_total(kept + swap(sent, "section", 1), ("dp", "tensor"))
    norm_total = norm_total.reshape(TYPES, 8, d)

    def collect_bias(meta_ref, ins, outs):
        here = meta_ref[0] == 0
        for i in range(2):
            zero, one = ins[0][i][...], ins[1][i][...]
            outs[0][2 * i : 2 * i + 2, :] = jnp.where(here, zero, one)
            outs[1][2 * i : 2 * i + 2, :] = jnp.where(here, one, zero)

    kept, sent = run("bias_sums", collect_bias, meta, biases, [arr((2 * TYPES, d), F32)] * 2)
    bias_total = small_total(kept + swap(sent, "section", 1), ("dp",))

    in_total, back_total = finish(
        dims, meta, ffn_sums, [(0, 0, dims.hidden, False), (TYPES, 0, dims.hidden, True)], "ffn_finish"
    )
    qkv_total, out_total = finish(
        dims, meta, attn_sums, [(0, 0, 3 * width, False), (0, 3 * width, 4 * width, True)], "attn_finish"
    )

    def exchange(values):
        received = swap(jnp.where(first, values[1], values[0]), "section", 1)
        return jnp.stack([jnp.where(first, values[0], received), jnp.where(first, received, values[1])])

    acts_out = exchange(acts)
    grads_out = exchange([jnp.concatenate(g, axis=0) for g in input_grads])
    return (
        acts_out[None],
        grads_out[None],
        qkv_total.reshape(1, TYPES, -1, 3, width),
        bias_total[:TYPES, : 3 * width].reshape(TYPES, 3, width)[None, :, ::2],
        out_total[None],
        norm_total[None, :, 2],
        in_total[None],
        bias_total[None, TYPES:],
        back_total[None],
        norm_total[None, :, 5],
        jnp.stack([norm_total[:, 0], norm_total[:, 3]], axis=1)[None],
        jnp.stack([norm_total[:, 1], norm_total[:, 4]], axis=1)[None],
    )


def solution(mesh):
    placed = (
        P(("dp", "tensor"), None, None),
        P(("dp", "tensor"), None, None),
        P("dp"),
        P("dp"),
        P("section", None, None, None, "tensor"),
        P("section", None, None, "tensor"),
        P("section", None, "tensor", None),
        P("section", None, None),
        P("section", None, None, "tensor"),
        P("section", None, "tensor"),
        P("section", None, "tensor", None),
        P("section", None, None),
        P("section", None, None, None),
        P("section", None, None, None),
    )
    return jax.shard_map(
        body,
        mesh=mesh,
        in_specs=placed,
        out_specs=(
            P("section", ("dp", "tensor"), None, None),
            P("section", ("dp", "tensor"), None, None),
            P("section", None, "dp", None, "tensor"),
            P("section", None, None, "tensor"),
            P("section", None, "tensor", "dp"),
            P("section", None, None),
            P("section", None, "dp", "tensor"),
            P("section", None, "tensor"),
            P("section", None, "tensor", "dp"),
            P("section", None, None),
            P("section", None, None, None),
            P("section", None, None, None),
        ),
        check_vma=False,
    )
```

```python
import functools
import math

import jax
import jax.numpy as jnp
from jax import lax
from jax.experimental import pallas as pl
from jax.experimental.pallas import tpu as pltpu
from jax.sharding import PartitionSpec as P

HEAD_DIM = 64
TYPES = 2
LAYERS = 2
EPS = 1e-06
HALF_ROOT = 0.7071067811865476
DENSITY = 0.3989422804014327
SCALE = 1.0 / math.sqrt(HEAD_DIM)
MIB = 1 << 20

F32 = jnp.float32
BF16 = jnp.bfloat16

TAIL = 16
FIRST_SUMS, SECOND_SUMS, QKV_SUMS, IN_SUMS, SMALL = 0, 6, 12, 14, 16

OUT_B, BACK_B, GAIN1, GAIN2, SHIFT1, SHIFT2, IN_B, QKV_B = range(0, 16, 2)


def dot(a, b):
    return jnp.dot(a, b, preferred_element_type=F32)


def dot_nt(a, b):
    return lax.dot_general(a, b, (((1,), (1,)), ((), ())), preferred_element_type=F32)


def dot_tn(a, b):
    return lax.dot_general(a, b, (((0,), (0,)), ((), ())), preferred_element_type=F32)


def nested(structure, flat):
    leaves, tree = jax.tree.flatten(structure)
    return jax.tree.unflatten(tree, flat)


class InHbm:
    def __init__(self, value):
        self.value = value


def run(name, body, meta, ins, outs, limit=6, scratch=(), aliases=None):
    flat_in, flat_out = jax.tree.leaves(ins), jax.tree.leaves(outs)

    def kernel(meta_ref, *refs):
        into = len(flat_in) + len(flat_out)
        body(meta_ref, nested(ins, refs[: len(flat_in)]), nested(outs, refs[len(flat_in) : into]), *refs[into:])

    def spec(leaf):
        return pl.BlockSpec(memory_space=pltpu.HBM if isinstance(leaf, InHbm) else pltpu.VMEM)

    def plain(leaf):
        return leaf.value if isinstance(leaf, InHbm) else leaf

    results = pl.pallas_call(
        kernel,
        name=name,
        in_specs=[pl.BlockSpec(memory_space=pltpu.SMEM)] + [spec(a) for a in flat_in],
        out_specs=[spec(a) for a in flat_out],
        out_shape=[plain(a) for a in flat_out],
        scratch_shapes=list(scratch),
        input_output_aliases={1 + i: o for i, o in (aliases or {}).items()},
        compiler_params=pltpu.CompilerParams(vmem_limit_bytes=limit * MIB),
        cost_estimate=pl.CostEstimate(flops=1, bytes_accessed=1, transcendentals=0),
    )(meta, *[plain(a) for a in flat_in])
    return nested(outs, results)


def arr(shape, dtype=BF16):
    return jax.ShapeDtypeStruct(tuple(shape), dtype)


class Ids:
    def __init__(self, meta, dims):
        self.meta, self.dims = meta, dims
        self.section, self.tensor, self.dp = meta[0], meta[1], meta[2]

    def chain(self, slot):
        return (self.tensor ^ slot) * self.dims.per_chip + self.section

    def kind(self, slot):
        return self.meta[3 + self.chain(slot)]

    def length(self, slot):
        return self.meta[3 + self.dims.group + self.chain(slot)]


def copies(pairs, sems):
    started = [pltpu.make_async_copy(source, target, sems.at[i]) for i, (source, target) in enumerate(pairs)]
    for copy in started:
        copy.start()
    return started


def fetch(dims, layer, meta, own, other, name):
    def body(meta_ref, ins, outs, sems):
        own, other = ins
        ids = Ids(meta_ref, dims)

        def go(source):
            for copy in copies(list(zip(source, outs)), sems):
                copy.wait()

        pl.when(ids.section == layer)(lambda: go(own))
        pl.when(ids.section != layer)(lambda: go(other))

    ins = ([InHbm(w) for w in own], [InHbm(w) for w in other])
    outs = [arr(w.shape, w.dtype) for w in own]
    return run(f"fetch_{name}{layer}", body, meta, ins, outs, scratch=[pltpu.SemaphoreType.DMA((len(own),))])


def pack_weights(dims, meta, qkv_w, out_w):
    rows = qkv_w.shape[1]

    def body(meta_ref, ins, outs, sems):
        pairs = [(ins[0], outs.at[:, :rows]), (ins[1], outs.at[:, rows:])]
        for copy in copies(pairs, sems):
            copy.wait()

    out = InHbm(arr((TYPES, rows + out_w.shape[1], dims.d)))
    ins = (InHbm(qkv_w), InHbm(out_w))
    return run("pack_w", body, meta, ins, out, scratch=[pltpu.SemaphoreType.DMA((2,))])


class Dims:
    pass


def attention_forward(dims, layer, meta, slot, rows, weight, small):
    length, width = dims.length, dims.width

    def body(meta_ref, ins, outs):
        rows, weight, small = ins
        part, qkv, att = outs
        ids = Ids(meta_ref, dims)
        kind = ids.kind(slot)
        bias = small[pl.ds(QKV_B + kind, 1), : 3 * width]
        qkv[...] = (dot_nt(rows[...], weight[kind, : 3 * width, :]) + bias).astype(BF16)
        keep = lax.broadcasted_iota(jnp.int32, (1, length), 1) < ids.length(slot)
        for c in range(0, width, HEAD_DIM):
            query = qkv[:, c : c + HEAD_DIM]
            key = qkv[:, width + c : width + c + HEAD_DIM]
            value = qkv[:, 2 * width + c : 2 * width + c + HEAD_DIM]
            scores = jnp.where(keep, dot_nt(query, key) * SCALE, -1e9)
            expd = jnp.exp(scores - jnp.max(scores, axis=-1, keepdims=True))
            probs = (expd * (1.0 / jnp.sum(expd, axis=-1, keepdims=True))).astype(BF16)
            att[:, c : c + HEAD_DIM] = dot(probs, value).astype(BF16)
        part[...] = dot(att[...], weight[kind, 3 * width :, :]).astype(BF16)

    outs = (arr((length, dims.d)), arr((length, 3 * width)), arr((length, width)))
    return run(f"attn_fwd{layer}_{slot}", body, meta, (rows, weight, small), outs)


def attention_backward(dims, layer, meta, slot, grads, qkv, weight):
    length, width = dims.length, dims.width

    def body(meta_ref, ins, outs):
        grads, qkv, weight = ins
        part, dqkv = outs
        ids = Ids(meta_ref, dims)
        kind = ids.kind(slot)
        keep = lax.broadcasted_iota(jnp.int32, (1, length), 1) < ids.length(slot)
        datt = dot_nt(grads[:length, :], weight[kind, 3 * width :, :]).astype(BF16)
        for c in range(0, width, HEAD_DIM):
            query = qkv[:, c : c + HEAD_DIM]
            key = qkv[:, width + c : width + c + HEAD_DIM]
            value = qkv[:, 2 * width + c : 2 * width + c + HEAD_DIM]
            da = datt[:, c : c + HEAD_DIM]
            scores = jnp.where(keep, dot_nt(query, key) * SCALE, -1e9)
            expd = jnp.exp(scores - jnp.max(scores, axis=-1, keepdims=True))
            probs = expd * (1.0 / jnp.sum(expd, axis=-1, keepdims=True))
            dprobs = dot_nt(da, value)
            dscores = (probs * (dprobs - jnp.sum(probs * dprobs, axis=-1, keepdims=True))).astype(BF16)
            dqkv[:, c : c + HEAD_DIM] = (dot(dscores, key) * SCALE).astype(BF16)
            dqkv[:, width + c : width + c + HEAD_DIM] = (dot_tn(dscores, query) * SCALE).astype(BF16)
            dqkv[:, 2 * width + c : 2 * width + c + HEAD_DIM] = dot_tn(probs.astype(BF16), da).astype(BF16)
        part[...] = dot(dqkv[...], weight[kind, : 3 * width, :]).astype(BF16)

    outs = (arr((length, dims.d)), arr((length, 3 * width)))
    return run(f"attn_bwd{layer}_{slot}", body, meta, (grads, qkv, weight), outs)


def typed_sum(ids, left, right, kind, slots):
    chosen = [
        jnp.where(ids.kind(k) == kind, right[k], jnp.zeros_like(right[k])) for k in range(slots)
    ]
    return dot_tn(jnp.concatenate(left, axis=0), jnp.concatenate(chosen, axis=0))


def halved(value):
    high = value.astype(BF16)
    return high, (value - high.astype(F32)).astype(BF16)


def carried(ids, blocks, slots, r):
    found = []
    for kind in range(TYPES):
        total = jnp.zeros((3, blocks[0].shape[1]), F32)
        for k in range(slots):
            tail = blocks[k][r : r + TAIL, :].astype(F32)
            total = total + jnp.where(ids.kind(k) == kind, tail[0:3] + tail[3:6], 0.0)
        found.append(total)
    return jnp.concatenate(found, axis=0)


def row_sums(ids, slots, rows):
    found = []
    for kind in range(TYPES):
        total = 0.0
        for k in range(slots):
            here = jnp.sum(rows[k].astype(F32), axis=0, keepdims=True)
            total = total + jnp.where(ids.kind(k) == kind, here, 0.0)
        found.append(total)
    return jnp.concatenate(found, axis=0)


def attention_weights(dims, layer, meta, rows, dqkv, grads, att, below):
    length, slots, width, d = dims.length, dims.slots, dims.width, dims.d

    def body(meta_ref, ins, outs):
        rows, dqkv, grads, att, below = ins
        ids = Ids(meta_ref, dims)
        left = [ref[...] for ref in rows]
        back = [ref[:length, :] for ref in grads]
        right = [ref[...] for ref in dqkv]
        heads = [ref[...] for ref in att]
        for kind in range(TYPES):
            span = slice(kind * d, (kind + 1) * d)
            outs[span, : 3 * width] = typed_sum(ids, left, right, kind, slots).astype(BF16)
            outs[span, 3 * width :] = typed_sum(ids, back, heads, kind, slots).astype(BF16)
        qkv_rows = row_sums(ids, slots, right)
        qkv_rows = jnp.concatenate([qkv_rows, jnp.zeros((TYPES, width), F32)], axis=1)
        firsts = carried(ids, grads, slots, length)
        small = jnp.concatenate([firsts, below[:6, :], qkv_rows, below[6:8, :]], axis=0)
        outs[TYPES * d : TYPES * d + SMALL, :], outs[TYPES * d + SMALL :, :] = halved(small)

    out = arr((TYPES * d + 2 * SMALL, d))
    return run(f"attn_dw{layer}", body, meta, (rows, dqkv, grads, att, below), out, 8)


def ffn_weights(dims, layer, meta, rows, dpre, grads, act):
    length, slots, hidden, d = dims.length, dims.slots, dims.hidden, dims.d

    def body(meta_ref, ins, outs):
        rows, dpre, grads, act = ins
        total, small = outs
        ids = Ids(meta_ref, dims)
        for step, (left, right) in enumerate(((rows, dpre), (grads, act))):
            left_rows = [ref[:length, :] for ref in left]
            right_rows = [ref[...] for ref in right]
            for kind in range(TYPES):
                first = (TYPES * step + kind) * d
                total[first : first + d, :] = typed_sum(ids, left_rows, right_rows, kind, slots).astype(BF16)
        small[0:6, :] = carried(ids, grads, slots, length)
        small[6:8, :] = row_sums(ids, slots, [ref[...] for ref in dpre])

    outs = (arr((2 * TYPES * d, hidden)), arr((8, hidden), F32))
    return run(f"ffn_dw{layer}", body, meta, (rows, dpre, grads, act), outs, 8)


def ffn_forward(dims, layer, meta, slot, rows, weight, small):
    length, hidden = dims.length, dims.hidden

    def body(meta_ref, ins, outs):
        rows, (in_w, back_w), small = ins
        part, act, slope = outs
        kind = Ids(meta_ref, dims).kind(slot)
        pre = dot(rows[...], in_w[kind]) + small[pl.ds(IN_B + kind, 1), :hidden]
        gate = 0.5 * (1.0 + lax.erf(pre * HALF_ROOT))
        act[...] = (pre * gate).astype(BF16)
        slope[...] = (gate + pre * (DENSITY * jnp.exp(-0.5 * pre * pre))).astype(BF16)
        part[...] = dot(act[...], back_w[kind]).astype(BF16)

    outs = (arr((length, dims.d)), arr((length, hidden)), arr((length, hidden)))
    return run(f"ffn_fwd{layer}_{slot}", body, meta, (rows, weight, small), outs)


def ffn_backward(dims, layer, meta, slot, grads, slope, weight):
    length, hidden = dims.length, dims.hidden

    def body(meta_ref, ins, outs):
        grads, slope, (in_w, back_w) = ins
        part, dpre = outs
        kind = Ids(meta_ref, dims).kind(slot)
        dact = dot_nt(grads[:length, :], back_w[kind])
        dpre[...] = (dact * slope[...].astype(F32)).astype(BF16)
        part[...] = dot_nt(dpre[...], in_w[kind]).astype(BF16)

    outs = (arr((length, dims.d)), arr((length, hidden)))
    return run(f"ffn_bwd{layer}_{slot}", body, meta, (grads, slope, weight), outs)


def normalized(values):
    center = values - jnp.mean(values, axis=-1, keepdims=True)
    inv = lax.rsqrt(jnp.mean(center * center, axis=-1, keepdims=True) + EPS)
    return center * inv, inv


def summed(parts):
    total = parts[0][...].astype(F32)
    for part in parts[1:]:
        total = total + part[...].astype(F32)
    return total


def norm_back(grad, normal, inv, gain):
    scaled = grad * gain
    return inv * (
        scaled
        - jnp.mean(scaled, axis=-1, keepdims=True)
        - normal * jnp.mean(scaled * normal, axis=-1, keepdims=True)
    )


def with_sums(low, value, sums):
    r = value.shape[0]
    low[:r, :] = value.astype(BF16)
    total = jnp.concatenate([jnp.sum(v, axis=0, keepdims=True) for v in sums], axis=0)
    high, rest = halved(total)
    blank = jnp.zeros((TAIL - 6, value.shape[1]), BF16)
    low[r:, :] = jnp.concatenate([high, rest, blank], axis=0)


def first_norm(dims, layer, meta, own_rows, parts, small):
    r, d = dims.length, dims.d

    def body(meta_ref, ins, outs):
        own_rows, parts, small = ins
        low, normal, inv = outs
        kind = Ids(meta_ref, dims).kind(0)
        mixed = own_rows[...].astype(F32) + summed(parts) + small[pl.ds(OUT_B + kind, 1), :]
        xhat, scale = normalized(mixed)
        normal[...] = xhat
        inv[...] = jnp.broadcast_to(scale, inv.shape)
        low[...] = (xhat * small[pl.ds(GAIN1 + kind, 1), :] + small[pl.ds(SHIFT1 + kind, 1), :]).astype(BF16)

    outs = (arr((r, d)), arr((r, d), F32), arr((r, 128), F32))
    return run(f"norm1_{layer}", body, meta, (own_rows, parts, small), outs)


def second_values(kind, normal, parts, small):
    normed = normal[...] * small[pl.ds(GAIN1 + kind, 1), :] + small[pl.ds(SHIFT1 + kind, 1), :]
    xhat, scale = normalized(normed + summed(parts) + small[pl.ds(BACK_B + kind, 1), :])
    output = xhat * small[pl.ds(GAIN2 + kind, 1), :] + small[pl.ds(SHIFT2 + kind, 1), :]
    return xhat, scale, output.astype(BF16)


def second_norm(dims, layer, meta, normal, parts, small):
    r, d = dims.length, dims.d

    def body(meta_ref, ins, outs):
        normal, parts, small = ins
        low, xhat_ref, inv = outs
        kind = Ids(meta_ref, dims).kind(0)
        xhat, scale, low[...] = second_values(kind, normal, parts, small)
        xhat_ref[...] = xhat
        inv[...] = jnp.broadcast_to(scale, inv.shape)

    outs = (arr((r, d)), arr((r, d), F32), arr((r, 128), F32))
    return run(f"norm2_{layer}", body, meta, (normal, parts, small), outs)


def second_back(kind, grad, xhat, scale, small, second_grad, low):
    value = norm_back(grad, xhat, scale, small[pl.ds(GAIN2 + kind, 1), :])
    second_grad[...] = value
    with_sums(low, value, (grad * xhat, grad, value))


def last_norm(dims, layer, meta, normal, parts, small, cotangent):
    r, d = dims.length, dims.d

    def body(meta_ref, ins, outs):
        normal, parts, small, cotangent = ins
        act, second_grad, low = outs
        ids = Ids(meta_ref, dims)
        kind = ids.kind(0)
        xhat, scale, act[...] = second_values(kind, normal, parts, small)
        grad = cotangent[ids.section].astype(F32)
        second_back(kind, grad, xhat, scale, small, second_grad, low)

    outs = (arr((r, d)), arr((r, d), F32), arr((r + TAIL, d)))
    return run(f"norm2_{layer}", body, meta, (normal, parts, small, cotangent), outs)


def between_layers(dims, layer, meta, parts, first_grad, xhat, inv, small):
    r, d = dims.length, dims.d

    def body(meta_ref, ins, outs):
        parts, first_grad, xhat, inv, small = ins
        input_grad, second_grad, low = outs
        kind = Ids(meta_ref, dims).kind(0)
        value = summed(parts) + first_grad[...]
        input_grad[...] = value
        grad = value.astype(BF16).astype(F32)
        second_back(kind, grad, xhat[...], inv[:, :1], small, second_grad, low)

    outs = (arr((r, d), F32), arr((r, d), F32), arr((r + TAIL, d)))
    return run(f"between{layer}", body, meta, (parts, first_grad, xhat, inv, small), outs)


def first_back(dims, layer, meta, parts, second_grad, xhat, inv, small):
    r, d = dims.length, dims.d

    def body(meta_ref, ins, outs):
        parts, second_grad, xhat, inv, small = ins
        first_grad, low = outs
        kind = Ids(meta_ref, dims).kind(0)
        grad = summed(parts) + second_grad[...]
        value = norm_back(grad, xhat[...], inv[:, :1], small[pl.ds(GAIN1 + kind, 1), :])
        first_grad[...] = value
        with_sums(low, value, (grad * xhat[...], grad, value))

    outs = (arr((r, d), F32), arr((r + TAIL, d)))
    return run(f"norm1_back{layer}", body, meta, (parts, second_grad, xhat, inv, small), outs)


def input_gradient(dims, layer, meta, parts, first_grad):
    def body(meta_ref, ins, outs):
        parts, first_grad = ins
        outs[...] = summed(parts) + first_grad[...]

    return run(f"input_grad{layer}", body, meta, (parts, first_grad), arr((dims.length, dims.d), F32))


def swap(value, axis, bit):
    count = lax.axis_size(axis)
    return lax.ppermute(value, axis, [(source, source ^ bit) for source in range(count)])


def gather(value, slots):
    return [value] + [swap(value, "tensor", k) for k in range(1, slots)]


def scatter(parts):
    return [parts[0]] + [swap(part, "tensor", k) for k, part in enumerate(parts) if k]


def tied(*values):
    return lax.optimization_barrier(values)


class GradSum:
    def __init__(self, dims, layer, meta, name, small):
        self.dims, self.layer, self.meta, self.name = dims, layer, meta, f"{name}{layer}"
        self.small = small

    def start(self, value):
        self.value = value
        self.d, self.cols = self.dims.d, value.shape[1]
        self.count = value.shape[0] // self.d
        self.rows = self.d // self.dims.dp
        self.extra = 2 * SMALL if self.small else 0
        self.other = lax.ppermute(value, "section", [(1 - self.layer, self.layer)])

    def permute(self, value, bit):
        base = self.layer * self.dims.dp
        pairs = [(base + z, base + (z ^ bit)) for z in range(self.dims.dp)]
        return lax.ppermute(value, ("section", "dp"), pairs)

    def whole(self, ref, base):
        return ref[base : base + SMALL, :].astype(F32) + ref[base + SMALL : base + 2 * SMALL, :].astype(F32)

    def near_sum(self):
        dims, rows, count, cols, d = self.dims, self.rows, self.count, self.cols, self.d
        if dims.dp != 4:
            both = self.value.astype(F32) + self.other.astype(F32)
            if self.small:
                low = both[count * d :]
                self.total_small = lax.psum(low[:SMALL] + low[SMALL:], "dp")
            return both[: count * d].reshape(count, d, cols).astype(BF16)
        base = 2 * count * rows

        def body(meta_ref, ins, outs):
            value, other = ins
            sent, kept = outs
            odd = lax.rem(Ids(meta_ref, dims).dp, 2)

            def part(index, chunk):
                start = pl.multiple_of(index * d + chunk * rows, 16)
                return value[pl.ds(start, rows), :].astype(F32) + other[pl.ds(start, rows), :].astype(F32)

            for i in range(2):
                for index in range(count):
                    at = (i * count + index) * rows
                    sent[at : at + rows, :] = part(index, 2 * i + 1 - odd).astype(BF16)
                    kept[at : at + rows, :] = part(index, 2 * i + odd)
            if self.small:
                total = self.whole(value, count * d) + self.whole(other, count * d)
                sent[base : base + SMALL, :], sent[base + SMALL :, :] = halved(total)
                kept[base:, :] = total

        outs = (arr((base + self.extra, cols)), arr((base + self.extra // 2, cols), F32))
        sent, self.kept = run(f"{self.name}_a", body, self.meta, (self.value, self.other), outs)
        return sent

    def near_send(self, sent):
        if self.dims.dp != 4:
            self.pieces = [lax.psum_scatter(sent, "dp", scatter_dimension=1, tiled=True)]
            if self.small:
                self.pieces.append(self.total_small)
        else:
            self.near = self.permute(sent, 1)

    def far_sum(self):
        dims, cols, size = self.dims, self.cols, self.count * self.rows
        if dims.dp != 4:
            return None

        def body(meta_ref, ins, outs):
            kept, near = ins
            sent, final = outs
            mine = lax.div(Ids(meta_ref, dims).dp, 2)

            def half(i):
                span = pl.ds(pl.multiple_of(i * size, 16), size)
                return kept[span, :] + near[span, :].astype(F32)

            sent[:size, :] = half(1 - mine).astype(BF16)
            final[:size, :] = half(mine)
            if self.small:
                total = kept[2 * size :, :] + self.whole(near, 2 * size)
                sent[size : size + SMALL, :], sent[size + SMALL :, :] = halved(total)
                final[size:, :] = total

        outs = (arr((size + self.extra, cols)), arr((size + self.extra // 2, cols), F32))
        sent, self.final = run(f"{self.name}_b", body, self.meta, (self.kept, self.near), outs)
        return sent

    def far_send(self, sent):
        if self.dims.dp == 4:
            self.pieces = [self.final, self.permute(sent, 2)]

    def finish(self, shapes, put, before=None):
        dims, rows, size = self.dims, self.rows, self.count * self.rows
        flat = len(self.pieces)

        def body(meta_ref, ins, outs, *scratch):
            pieces, values, sems = ins[0], scratch[:-1], scratch[-1]

            def total(index):
                if dims.dp != 4:
                    return pieces[0][index].astype(F32)
                span = slice(index * rows, (index + 1) * rows)
                return pieces[0][span, :] + pieces[1][span, :].astype(F32)

            @pl.when(Ids(meta_ref, dims).section == self.layer)
            def _():
                small = None
                if self.small:
                    small = pieces[0][size:, :] + self.whole(pieces[1], size) if dims.dp == 4 else pieces[1][...]
                put(values, [total(index) for index in range(self.count)], small)
                for copy in copies(list(zip(values, outs)), sems):
                    copy.wait()

        outs = [InHbm(arr(shape, F32)) for shape in shapes]
        ins = [self.pieces] + ([] if before is None else [InHbm(a) for a in before])
        aliases = {} if before is None else {flat + i: i for i in range(len(shapes))}
        scratch = [pltpu.VMEM(shape, F32) for shape in shapes] + [pltpu.SemaphoreType.DMA((len(shapes),))]
        return run(f"{self.name}_end", body, self.meta, ins, outs, 8, scratch, aliases)


def pack_params(dims, meta, arrays):
    width = dims.width

    def body(meta_ref, ins, outs, *scratch):
        for copy in copies(list(zip(ins, scratch[:-1])), scratch[-1]):
            copy.wait()
        out_b, back_b, gains, shifts, in_b, qkv_b = scratch[:-1]
        for t in range(TYPES):
            for row, ref in ((OUT_B, out_b), (BACK_B, back_b), (IN_B, in_b)):
                outs[row + t : row + t + 1, :] = ref[0, t : t + 1, :]
            for row, ref in ((GAIN1, gains), (SHIFT1, shifts)):
                for norm in range(2):
                    outs[row + 2 * norm + t : row + 2 * norm + t + 1, :] = ref[0, t, norm : norm + 1, :]
            outs[QKV_B + t : QKV_B + t + 1, :] = jnp.zeros((1, dims.d), F32)
            outs[QKV_B + t : QKV_B + t + 1, :width] = qkv_b[0, t, 0:1, :]
            outs[QKV_B + t : QKV_B + t + 1, 2 * width : 3 * width] = qkv_b[0, t, 1:2, :]

    scratch = [pltpu.VMEM(a.shape, F32) for a in arrays] + [pltpu.SemaphoreType.DMA((len(arrays),))]
    return run("pack", body, meta, [InHbm(a) for a in arrays], arr((16, dims.d), F32), scratch=scratch)


def order_params(dims, meta, own, other):
    def body(meta_ref, ins, outs):
        here = meta_ref[0] == 0
        own, other = ins[0][...], ins[1][...]
        outs[0][...] = jnp.where(here, own, other)
        outs[1][...] = jnp.where(here, other, own)

    return run("params", body, meta, [own, other], [arr(own.shape, F32)] * 2)


def both_chains(dims, meta, own, moved, name):
    def body(meta_ref, ins, outs):
        own, moved = ins
        first = meta_ref[0] == 0

        @pl.when(first)
        def _():
            outs[0, 0] = own[0][...]
            outs[0, 1] = moved[0][...]

        @pl.when(jnp.logical_not(first))
        def _():
            outs[0, 0] = moved[1][...]
            outs[0, 1] = own[1][...]

    return run(name, body, meta, (own, moved), arr((1, 2, dims.length, dims.d), own[0].dtype), 8)


def body(
    tokens,
    cotangent,
    lengths,
    chain_type,
    qkv_weight,
    qkv_bias,
    out_weight,
    out_bias,
    ffn_in,
    ffn_in_bias,
    ffn_out,
    ffn_out_bias,
    norm_gain,
    norm_bias,
):
    dims = Dims()
    dims.per_chip, dims.length, dims.d = tokens.shape
    dims.slots = lax.axis_size("tensor")
    dims.dp = lax.axis_size("dp")
    dims.group = lengths.shape[0]
    dims.width = qkv_weight.shape[-1]
    dims.hidden = ffn_in.shape[-1]
    sections = lax.axis_size("section")
    assert dims.per_chip == sections == LAYERS and dims.slots & (dims.slots - 1) == 0
    assert dims.dp & (dims.dp - 1) == 0 and 4 * dims.width == dims.d == dims.hidden
    d, width, slots = dims.d, dims.width, dims.slots
    each = range(slots)
    section = lax.axis_index("section")
    meta = jnp.concatenate(
        [
            jnp.stack([section, lax.axis_index("tensor"), lax.axis_index("dp")]).astype(jnp.int32),
            chain_type,
            lengths,
        ]
    )

    own_rows = jnp.where(section == 0, tokens[0], tokens[1])
    rows = gather(own_rows, slots)

    qkv_own = qkv_weight[0].transpose(0, 2, 3, 1).reshape(TYPES, 3 * width, d)
    attn_own = pack_weights(dims, meta, qkv_own, out_weight[0])
    attn_other = swap(attn_own, "section", 1)
    packed = pack_params(
        dims, meta, (out_bias, ffn_out_bias, norm_gain, norm_bias, ffn_in_bias, qkv_bias)
    )
    small = order_params(dims, meta, packed, swap(packed, "section", 1))
    ffn_own = [ffn_in[0], ffn_out[0]]

    def moved(value, layer):
        return lax.ppermute(value, "section", [(1 - layer, layer)])

    saved = []
    acts = []
    for layer in range(LAYERS):
        (weight,) = fetch(dims, layer, meta, [attn_own], [attn_other], "attn")
        attn = [attention_forward(dims, layer, meta, k, rows[k], weight, small[layer]) for k in each]
        parts, qkv, att = ([a[i] for a in attn] for i in range(3))
        parts = scatter(parts)
        if layer == 0:
            parts, ffn_sent = tied(parts, ffn_own)
            ffn_other = [swap(w, "section", 1) for w in ffn_sent]
        first = first_norm(dims, layer, meta, own_rows, parts, small[layer])
        normed = gather(first[0], slots)
        weight = fetch(dims, layer, meta, ffn_own, ffn_other, "ffn")
        ffn = [ffn_forward(dims, layer, meta, k, normed[k], weight, small[layer]) for k in each]
        parts, act, slope = ([f[i] for f in ffn] for i in range(3))
        parts = scatter(parts)
        if layer < LAYERS - 1:
            second = second_norm(dims, layer, meta, first[1], parts, small[layer])
        else:
            second = last_norm(dims, layer, meta, first[1], parts, small[layer], cotangent)
        saved.append((rows, qkv, att, first, normed, act, slope, second))
        own_rows = second[0]
        acts.append(own_rows)
        if layer < LAYERS - 1:
            rows = gather(own_rows, slots)

    second_grad, low = second[1:]
    input_grads = [None] * LAYERS
    ffn_sums = [GradSum(dims, layer, meta, "ffn", False) for layer in range(LAYERS)]
    attn_sums = [GradSum(dims, layer, meta, "attn", True) for layer in range(LAYERS)]
    for layer in reversed(range(LAYERS)):
        rows, qkv, att, first, normed, act, slope, second = saved[layer]
        top = layer == LAYERS - 1
        grads = gather(low, slots)
        weight = fetch(dims, layer, meta, ffn_own, ffn_other, "ffn_back")
        if top:
            acts_moved = [moved(acts[i], i) for i in range(LAYERS)]
        else:
            near = attn_sums[layer + 1].near_sum()
            far = ffn_sums[layer + 1].far_sum()
            grads, near, far = tied(grads, near, far)
            attn_sums[layer + 1].near_send(near)
            ffn_sums[layer + 1].far_send(far)
        back = [ffn_backward(dims, layer, meta, k, grads[k], slope[k], weight) for k in each]
        parts, dpre = ([b[i] for b in back] for i in range(2))
        parts = scatter(parts)
        ffn_grad, below = ffn_weights(dims, layer, meta, normed, dpre, grads, act)
        if top:
            acts_out = both_chains(dims, meta, acts, acts_moved, "acts_out")
            parts, ffn_grad, acts_out = tied(parts, ffn_grad, acts_out)
        else:
            parts, ffn_grad = tied(parts, ffn_grad)
        ffn_sums[layer].start(ffn_grad)
        first_grad, low = first_back(
            dims, layer, meta, parts, second_grad, first[1], first[2], small[layer]
        )
        grads = gather(low, slots)
        (weight,) = fetch(dims, layer, meta, [attn_own], [attn_other], "attn_back")
        near = ffn_sums[layer].near_sum()
        if top:
            grads, near = tied(grads, near)
        else:
            far = attn_sums[layer + 1].far_sum()
            grads, near, far = tied(grads, near, far)
            attn_sums[layer + 1].far_send(far)
        ffn_sums[layer].near_send(near)
        back = [attention_backward(dims, layer, meta, k, grads[k], qkv[k], weight) for k in each]
        parts, dqkv = ([b[i] for b in back] for i in range(2))
        parts = scatter(parts)
        attn_grad = attention_weights(dims, layer, meta, rows, dqkv, grads, att, below)
        parts, attn_grad = tied(parts, attn_grad)
        attn_sums[layer].start(attn_grad)
        if layer > 0:
            second = saved[layer - 1][-1]
            input_grads[layer], second_grad, low = between_layers(
                dims, layer, meta, parts, first_grad, second[1], second[2], small[layer - 1]
            )
        else:
            input_grads[layer] = input_gradient(dims, layer, meta, parts, first_grad)

    share = d // dims.dp
    ffn_shapes = [(TYPES, share, dims.hidden)] * 2
    attn_shapes = [
        (TYPES, 3, share, width),
        (TYPES, width, share),
        (1, TYPES, 2, width),
        (1, TYPES, d),
        (1, TYPES, dims.hidden),
        (1, TYPES, d),
        (1, TYPES, 2, d),
        (1, TYPES, 2, d),
    ]

    def put_ffn(outs, totals, small):
        for index, total in enumerate(totals):
            outs[index // TYPES][index % TYPES] = total

    def put_attn(outs, totals, small):
        qkv_out, out_out, qkv_b, out_b, in_b, back_b, gains, shifts = outs
        for kind, total in enumerate(totals):
            for i in range(3):
                qkv_out[kind, i] = total[:, i * width : (i + 1) * width]
            out_out[kind] = total[:, 3 * width :].T
            qkv_b[0, kind, 0:1, :] = small[QKV_SUMS + kind : QKV_SUMS + kind + 1, :width]
            qkv_b[0, kind, 1:2, :] = small[QKV_SUMS + kind : QKV_SUMS + kind + 1, 2 * width : 3 * width]
            in_b[0, kind : kind + 1, :] = small[IN_SUMS + kind : IN_SUMS + kind + 1, :]
            for norm, (base, bias) in enumerate(((FIRST_SUMS, out_b), (SECOND_SUMS, back_b))):
                row = base + 3 * kind
                gains[0, kind, norm : norm + 1, :] = small[row : row + 1, :]
                shifts[0, kind, norm : norm + 1, :] = small[row + 1 : row + 2, :]
                bias[0, kind : kind + 1, :] = small[row + 2 : row + 3, :]

    ffn_out_grads = ffn_sums[1].finish(ffn_shapes, put_ffn)
    attn_out_grads = attn_sums[1].finish(attn_shapes, put_attn)
    near, far = tied(attn_sums[0].near_sum(), ffn_sums[0].far_sum())
    attn_sums[0].near_send(near)
    ffn_sums[0].far_send(far)
    attn_sums[0].far_send(attn_sums[0].far_sum())

    grads_moved = [moved(input_grads[layer], layer) for layer in range(LAYERS)]
    grads_out = both_chains(dims, meta, input_grads, grads_moved, "grads_out")
    in_total, back_total = ffn_sums[0].finish(ffn_shapes, put_ffn, ffn_out_grads)
    qkv_total, out_total, *small_grads = attn_sums[0].finish(attn_shapes, put_attn, attn_out_grads)
    qkv_bias_out, out_bias_out, in_bias_out, back_bias_out, gain_out, shift_out = small_grads
    return (
        acts_out,
        grads_out,
        qkv_total.transpose(0, 2, 1, 3)[None],
        qkv_bias_out,
        out_total[None],
        out_bias_out,
        in_total[None],
        in_bias_out,
        back_total.transpose(0, 2, 1)[None],
        back_bias_out,
        gain_out,
        shift_out,
    )


def solution(mesh):
    placed = (
        P(("dp", "tensor"), None, None),
        P(("dp", "tensor"), None, None),
        P("dp"),
        P("dp"),
        P("section", None, None, None, "tensor"),
        P("section", None, None, "tensor"),
        P("section", None, "tensor", None),
        P("section", None, None),
        P("section", None, None, "tensor"),
        P("section", None, "tensor"),
        P("section", None, "tensor", None),
        P("section", None, None),
        P("section", None, None, None),
        P("section", None, None, None),
    )
    return jax.shard_map(
        body,
        mesh=mesh,
        in_specs=placed,
        out_specs=(
            P("section", ("dp", "tensor"), None, None),
            P("section", ("dp", "tensor"), None, None),
            P("section", None, "dp", None, "tensor"),
            P("section", None, None, "tensor"),
            P("section", None, "tensor", "dp"),
            P("section", None, None),
            P("section", None, "dp", "tensor"),
            P("section", None, "tensor"),
            P("section", None, "tensor", "dp"),
            P("section", None, None),
            P("section", None, None, None),
            P("section", None, None, None),
        ),
        check_vma=False,
    )
```

```python
import functools
import math

import jax
import jax.numpy as jnp
from jax import lax
from jax.experimental import pallas as pl
from jax.experimental.pallas import tpu as pltpu
from jax.sharding import PartitionSpec as P

HEAD_DIM = 64
TYPES = 2
LAYERS = 2
EPS = 1e-06
HALF_ROOT = 0.7071067811865476
DENSITY = 0.3989422804014327
SCALE = 1.0 / math.sqrt(HEAD_DIM)
MIB = 1 << 20

F32 = jnp.float32
BF16 = jnp.bfloat16

TAIL = 16
PAD = 48
FIRST_SUMS, SECOND_SUMS, QKV_SUMS, IN_SUMS, SMALL = 0, 6, 12, 14, 16

OUT_B, BACK_B, GAIN1, GAIN2, SHIFT1, SHIFT2, IN_B, QKV_B = range(0, 16, 2)


def dot(a, b):
    return jnp.dot(a, b, preferred_element_type=F32)


def dot_nt(a, b):
    return lax.dot_general(a, b, (((1,), (1,)), ((), ())), preferred_element_type=F32)


def dot_tn(a, b):
    return lax.dot_general(a, b, (((0,), (0,)), ((), ())), preferred_element_type=F32)


def nested(structure, flat):
    leaves, tree = jax.tree.flatten(structure)
    return jax.tree.unflatten(tree, flat)


class InHbm:
    def __init__(self, value):
        self.value = value


def run(name, body, meta, ins, outs, limit=6, scratch=(), aliases=None):
    flat_in, flat_out = jax.tree.leaves(ins), jax.tree.leaves(outs)

    def kernel(meta_ref, *refs):
        into = len(flat_in) + len(flat_out)
        body(meta_ref, nested(ins, refs[: len(flat_in)]), nested(outs, refs[len(flat_in) : into]), *refs[into:])

    def spec(leaf):
        return pl.BlockSpec(memory_space=pltpu.HBM if isinstance(leaf, InHbm) else pltpu.VMEM)

    def plain(leaf):
        return leaf.value if isinstance(leaf, InHbm) else leaf

    results = pl.pallas_call(
        kernel,
        name=name,
        in_specs=[pl.BlockSpec(memory_space=pltpu.SMEM)] + [spec(a) for a in flat_in],
        out_specs=[spec(a) for a in flat_out],
        out_shape=[plain(a) for a in flat_out],
        scratch_shapes=list(scratch),
        input_output_aliases={1 + i: o for i, o in (aliases or {}).items()},
        compiler_params=pltpu.CompilerParams(vmem_limit_bytes=limit * MIB),
        cost_estimate=pl.CostEstimate(flops=1, bytes_accessed=1, transcendentals=0),
    )(meta, *[plain(a) for a in flat_in])
    return nested(outs, results)


def arr(shape, dtype=BF16):
    return jax.ShapeDtypeStruct(tuple(shape), dtype)


class Ids:
    def __init__(self, meta, dims):
        self.meta, self.dims = meta, dims
        self.section, self.tensor, self.dp = meta[0], meta[1], meta[2]

    def chain(self, slot):
        return (self.tensor ^ slot) * self.dims.per_chip + self.section

    def kind(self, slot):
        return self.meta[3 + self.chain(slot)]

    def length(self, slot):
        return self.meta[3 + self.dims.group + self.chain(slot)]


def copies(pairs, sems):
    started = [pltpu.make_async_copy(source, target, sems.at[i]) for i, (source, target) in enumerate(pairs)]
    for copy in started:
        copy.start()
    return started


def fetch(dims, layer, meta, own, other, name):
    def body(meta_ref, ins, outs, sems):
        own, other = ins
        ids = Ids(meta_ref, dims)

        def go(source):
            for copy in copies(list(zip(source, outs)), sems):
                copy.wait()

        pl.when(ids.section == layer)(lambda: go(own))
        pl.when(ids.section != layer)(lambda: go(other))

    ins = ([InHbm(w) for w in own], [InHbm(w) for w in other])
    outs = [arr(w.shape, w.dtype) for w in own]
    return run(f"fetch_{name}{layer}", body, meta, ins, outs, scratch=[pltpu.SemaphoreType.DMA((len(own),))])


def pack_weights(dims, meta, qkv_w, out_w):
    rows = qkv_w.shape[1]

    def body(meta_ref, ins, outs, sems):
        pairs = [(ins[0], outs.at[:, :rows]), (ins[1], outs.at[:, rows:])]
        for copy in copies(pairs, sems):
            copy.wait()

    out = InHbm(arr((TYPES, rows + out_w.shape[1], dims.d)))
    ins = (InHbm(qkv_w), InHbm(out_w))
    return run("pack_w", body, meta, ins, out, scratch=[pltpu.SemaphoreType.DMA((2,))])


class Dims:
    pass


def attention_forward(dims, layer, meta, slot, rows, weight, small):
    length, width = dims.length, dims.width

    def body(meta_ref, ins, outs):
        rows, weight, small = ins
        part, qkv, att = outs
        ids = Ids(meta_ref, dims)
        kind = ids.kind(slot)
        bias = small[pl.ds(QKV_B + kind, 1), : 3 * width]
        qkv[...] = (dot_nt(rows[...], weight[kind, : 3 * width, :]) + bias).astype(BF16)
        keep = lax.broadcasted_iota(jnp.int32, (1, length), 1) < ids.length(slot)
        for c in range(0, width, HEAD_DIM):
            query = qkv[:, c : c + HEAD_DIM]
            key = qkv[:, width + c : width + c + HEAD_DIM]
            value = qkv[:, 2 * width + c : 2 * width + c + HEAD_DIM]
            scores = jnp.where(keep, dot_nt(query, key) * SCALE, -1e9)
            expd = jnp.exp(scores - jnp.max(scores, axis=-1, keepdims=True))
            probs = (expd * (1.0 / jnp.sum(expd, axis=-1, keepdims=True))).astype(BF16)
            att[:, c : c + HEAD_DIM] = dot(probs, value).astype(BF16)
        part[...] = dot(att[...], weight[kind, 3 * width :, :]).astype(BF16)

    outs = (arr((length, dims.d)), arr((length, 3 * width)), arr((length, width)))
    return run(f"attn_fwd{layer}_{slot}", body, meta, (rows, weight, small), outs)


def attention_backward(dims, layer, meta, slot, grads, qkv, weight):
    length, width = dims.length, dims.width

    def body(meta_ref, ins, outs):
        grads, qkv, weight = ins
        part, dqkv = outs
        ids = Ids(meta_ref, dims)
        kind = ids.kind(slot)
        keep = lax.broadcasted_iota(jnp.int32, (1, length), 1) < ids.length(slot)
        datt = dot_nt(grads[:length, :], weight[kind, 3 * width :, :]).astype(BF16)
        for c in range(0, width, HEAD_DIM):
            query = qkv[:, c : c + HEAD_DIM]
            key = qkv[:, width + c : width + c + HEAD_DIM]
            value = qkv[:, 2 * width + c : 2 * width + c + HEAD_DIM]
            da = datt[:, c : c + HEAD_DIM]
            scores = jnp.where(keep, dot_nt(query, key) * SCALE, -1e9)
            expd = jnp.exp(scores - jnp.max(scores, axis=-1, keepdims=True))
            probs = expd * (1.0 / jnp.sum(expd, axis=-1, keepdims=True))
            dprobs = dot_nt(da, value)
            dscores = (probs * (dprobs - jnp.sum(probs * dprobs, axis=-1, keepdims=True))).astype(BF16)
            dqkv[:, c : c + HEAD_DIM] = (dot(dscores, key) * SCALE).astype(BF16)
            dqkv[:, width + c : width + c + HEAD_DIM] = (dot_tn(dscores, query) * SCALE).astype(BF16)
            dqkv[:, 2 * width + c : 2 * width + c + HEAD_DIM] = dot_tn(probs.astype(BF16), da).astype(BF16)
        part[...] = dot(dqkv[...], weight[kind, : 3 * width, :]).astype(BF16)

    outs = (arr((length, dims.d)), arr((length, 3 * width)))
    return run(f"attn_bwd{layer}_{slot}", body, meta, (grads, qkv, weight), outs)


def typed_sum(ids, left, right, kind, slots):
    chosen = [
        jnp.where(ids.kind(k) == kind, right[k], jnp.zeros_like(right[k])) for k in range(slots)
    ]
    return dot_tn(jnp.concatenate(left, axis=0), jnp.concatenate(chosen, axis=0))


def halved(value):
    high = value.astype(BF16)
    return high, (value - high.astype(F32)).astype(BF16)


def carried(ids, blocks, slots, r):
    found = []
    for kind in range(TYPES):
        total = jnp.zeros((3, blocks[0].shape[1]), F32)
        for k in range(slots):
            tail = blocks[k][r : r + TAIL, :].astype(F32)
            total = total + jnp.where(ids.kind(k) == kind, tail[0:3] + tail[3:6], 0.0)
        found.append(total)
    return jnp.concatenate(found, axis=0)


def row_sums(ids, slots, rows):
    found = []
    for kind in range(TYPES):
        total = 0.0
        for k in range(slots):
            here = jnp.sum(rows[k].astype(F32), axis=0, keepdims=True)
            total = total + jnp.where(ids.kind(k) == kind, here, 0.0)
        found.append(total)
    return jnp.concatenate(found, axis=0)


def attention_weights(dims, layer, meta, rows, dqkv, grads, att, below):
    length, slots, width, d = dims.length, dims.slots, dims.width, dims.d

    def body(meta_ref, ins, outs):
        rows, dqkv, grads, att, below = ins
        ids = Ids(meta_ref, dims)
        left = [ref[...] for ref in rows]
        back = [ref[:length, :] for ref in grads]
        right = [ref[...] for ref in dqkv]
        heads = [ref[...] for ref in att]
        for kind in range(TYPES):
            span = slice(kind * d, (kind + 1) * d)
            outs[span, : 3 * width] = typed_sum(ids, left, right, kind, slots).astype(BF16)
            outs[span, 3 * width :] = typed_sum(ids, back, heads, kind, slots).astype(BF16)
        qkv_rows = row_sums(ids, slots, right)
        qkv_rows = jnp.concatenate([qkv_rows, jnp.zeros((TYPES, width), F32)], axis=1)
        firsts = carried(ids, grads, slots, length)
        small = jnp.concatenate([firsts, below[:6, :], qkv_rows, below[6:8, :]], axis=0)
        outs[TYPES * d : TYPES * d + SMALL, :], outs[TYPES * d + SMALL :, :] = halved(small)

    out = arr((TYPES * d + 2 * SMALL, d))
    return run(f"attn_dw{layer}", body, meta, (rows, dqkv, grads, att, below), out, 8)


def ffn_weights(dims, layer, meta, rows, dpre, grads, act):
    length, slots, hidden, d = dims.length, dims.slots, dims.hidden, dims.d

    def body(meta_ref, ins, outs):
        rows, dpre, grads, act = ins
        total, small = outs
        ids = Ids(meta_ref, dims)
        for step, (left, right) in enumerate(((rows, dpre), (grads, act))):
            left_rows = [ref[:length, :] for ref in left]
            right_rows = [ref[...] for ref in right]
            for kind in range(TYPES):
                first = (TYPES * step + kind) * d
                total[first : first + d, :] = typed_sum(ids, left_rows, right_rows, kind, slots).astype(BF16)
        small[0:6, :] = carried(ids, grads, slots, length)
        small[6:8, :] = row_sums(ids, slots, [ref[...] for ref in dpre])

    outs = (arr((2 * TYPES * d, hidden)), arr((8, hidden), F32))
    return run(f"ffn_dw{layer}", body, meta, (rows, dpre, grads, act), outs, 8)


def ffn_forward(dims, layer, meta, slot, rows, weight, small):
    length, hidden = dims.length, dims.hidden

    def body(meta_ref, ins, outs):
        rows, (in_w, back_w), small = ins
        part, act, slope = outs
        kind = Ids(meta_ref, dims).kind(slot)
        pre = dot(rows[...], in_w[kind]) + small[pl.ds(IN_B + kind, 1), :hidden]
        gate = 0.5 * (1.0 + lax.erf(pre * HALF_ROOT))
        act[...] = (pre * gate).astype(BF16)
        slope[...] = (gate + pre * (DENSITY * jnp.exp(-0.5 * pre * pre))).astype(BF16)
        part[...] = dot(act[...], back_w[kind]).astype(BF16)

    outs = (arr((length, dims.d)), arr((length, hidden)), arr((length, hidden)))
    return run(f"ffn_fwd{layer}_{slot}", body, meta, (rows, weight, small), outs)


def ffn_backward(dims, layer, meta, slot, grads, slope, weight):
    length, hidden = dims.length, dims.hidden

    def body(meta_ref, ins, outs):
        grads, slope, (in_w, back_w) = ins
        part, dpre = outs
        kind = Ids(meta_ref, dims).kind(slot)
        dact = dot_nt(grads[:length, :], back_w[kind])
        dpre[...] = (dact * slope[...].astype(F32)).astype(BF16)
        part[...] = dot_nt(dpre[...], in_w[kind]).astype(BF16)

    outs = (arr((length, dims.d)), arr((length, hidden)))
    return run(f"ffn_bwd{layer}_{slot}", body, meta, (grads, slope, weight), outs)


def normalized(values):
    center = values - jnp.mean(values, axis=-1, keepdims=True)
    inv = lax.rsqrt(jnp.mean(center * center, axis=-1, keepdims=True) + EPS)
    return center * inv, inv


def summed(parts):
    total = parts[0][...].astype(F32)
    for part in parts[1:]:
        total = total + part[...].astype(F32)
    return total


def norm_back(grad, normal, inv, gain):
    scaled = grad * gain
    return inv * (
        scaled
        - jnp.mean(scaled, axis=-1, keepdims=True)
        - normal * jnp.mean(scaled * normal, axis=-1, keepdims=True)
    )


def with_sums(low, value, sums):
    r = value.shape[0]
    low[:r, :] = value.astype(BF16)
    total = jnp.concatenate([jnp.sum(v, axis=0, keepdims=True) for v in sums], axis=0)
    high, rest = halved(total)
    blank = jnp.zeros((TAIL - 6, value.shape[1]), BF16)
    low[r:, :] = jnp.concatenate([high, rest, blank], axis=0)


def first_norm(dims, layer, meta, own_rows, parts, small):
    r, d = dims.length, dims.d

    def body(meta_ref, ins, outs):
        own_rows, parts, small = ins
        low, normal, inv = outs
        kind = Ids(meta_ref, dims).kind(0)
        mixed = own_rows[...].astype(F32) + summed(parts) + small[pl.ds(OUT_B + kind, 1), :]
        xhat, scale = normalized(mixed)
        normal[...] = xhat
        inv[...] = jnp.broadcast_to(scale, inv.shape)
        low[...] = (xhat * small[pl.ds(GAIN1 + kind, 1), :] + small[pl.ds(SHIFT1 + kind, 1), :]).astype(BF16)

    outs = (arr((r, d)), arr((r, d), F32), arr((r, 128), F32))
    return run(f"norm1_{layer}", body, meta, (own_rows, parts, small), outs)


def second_values(kind, normal, parts, small):
    normed = normal[...] * small[pl.ds(GAIN1 + kind, 1), :] + small[pl.ds(SHIFT1 + kind, 1), :]
    xhat, scale = normalized(normed + summed(parts) + small[pl.ds(BACK_B + kind, 1), :])
    output = xhat * small[pl.ds(GAIN2 + kind, 1), :] + small[pl.ds(SHIFT2 + kind, 1), :]
    return xhat, scale, output.astype(BF16)


def second_norm(dims, layer, meta, normal, parts, small):
    r, d = dims.length, dims.d

    def body(meta_ref, ins, outs):
        normal, parts, small = ins
        low, xhat_ref, inv = outs
        kind = Ids(meta_ref, dims).kind(0)
        xhat, scale, low[...] = second_values(kind, normal, parts, small)
        xhat_ref[...] = xhat
        inv[...] = jnp.broadcast_to(scale, inv.shape)

    outs = (arr((r, d)), arr((r, d), F32), arr((r, 128), F32))
    return run(f"norm2_{layer}", body, meta, (normal, parts, small), outs)


def second_back(kind, grad, xhat, scale, small, second_grad, low):
    value = norm_back(grad, xhat, scale, small[pl.ds(GAIN2 + kind, 1), :])
    second_grad[...] = value
    with_sums(low, value, (grad * xhat, grad, value))


def last_norm(dims, layer, meta, normal, parts, small, cotangent):
    r, d = dims.length, dims.d

    def body(meta_ref, ins, outs):
        normal, parts, small, cotangent = ins
        act, second_grad, low = outs
        ids = Ids(meta_ref, dims)
        kind = ids.kind(0)
        xhat, scale, act[...] = second_values(kind, normal, parts, small)
        grad = cotangent[ids.section].astype(F32)
        second_back(kind, grad, xhat, scale, small, second_grad, low)

    outs = (arr((r, d)), arr((r, d), F32), arr((r + TAIL, d)))
    return run(f"norm2_{layer}", body, meta, (normal, parts, small, cotangent), outs)


def between_layers(dims, layer, meta, parts, first_grad, xhat, inv, small):
    r, d = dims.length, dims.d

    def body(meta_ref, ins, outs):
        parts, first_grad, xhat, inv, small = ins
        input_grad, second_grad, low = outs
        kind = Ids(meta_ref, dims).kind(0)
        value = summed(parts) + first_grad[...]
        input_grad[...] = value
        grad = value.astype(BF16).astype(F32)
        second_back(kind, grad, xhat[...], inv[:, :1], small, second_grad, low)

    outs = (arr((r, d), F32), arr((r, d), F32), arr((r + TAIL, d)))
    return run(f"between{layer}", body, meta, (parts, first_grad, xhat, inv, small), outs)


def first_back(dims, layer, meta, parts, second_grad, xhat, inv, small):
    r, d = dims.length, dims.d

    def body(meta_ref, ins, outs):
        parts, second_grad, xhat, inv, small = ins
        first_grad, low = outs
        kind = Ids(meta_ref, dims).kind(0)
        grad = summed(parts) + second_grad[...]
        value = norm_back(grad, xhat[...], inv[:, :1], small[pl.ds(GAIN1 + kind, 1), :])
        first_grad[...] = value
        with_sums(low, value, (grad * xhat[...], grad, value))

    outs = (arr((r, d), F32), arr((r + TAIL, d)))
    return run(f"norm1_back{layer}", body, meta, (parts, second_grad, xhat, inv, small), outs)


def input_gradient(dims, layer, meta, parts, first_grad):
    def body(meta_ref, ins, outs):
        parts, first_grad = ins
        outs[...] = summed(parts) + first_grad[...]

    return run(f"input_grad{layer}", body, meta, (parts, first_grad), arr((dims.length, dims.d), F32))


def swap(value, axis, bit):
    count = lax.axis_size(axis)
    return lax.ppermute(value, axis, [(source, source ^ bit) for source in range(count)])


def gather(value, slots):
    return [value] + [swap(value, "tensor", k) for k in range(1, slots)]


def scatter(parts):
    return [parts[0]] + [swap(part, "tensor", k) for k, part in enumerate(parts) if k]


def tied(*values):
    return lax.optimization_barrier(values)


class GradSum:
    def __init__(self, dims, layer, meta, names, small):
        self.dims, self.layer, self.meta, self.names = dims, layer, meta, [f"{name}{layer}" for name in names]
        self.name, self.small, self.pieces = "_".join(self.names), small, [None] * len(names)

    def start(self, value):
        self.value = value
        self.d, self.cols = self.dims.d, value.shape[1]
        self.count = value.shape[0] // self.d
        self.rows = self.d // self.dims.dp
        self.extra = 2 * SMALL if self.small else 0
        self.pad = 0 if self.small else PAD
        self.other = lax.ppermute(value, "section", [(1 - self.layer, self.layer)])

    def permute(self, value, bit):
        base = self.layer * self.dims.dp
        pairs = [(base + z, base + (z ^ bit)) for z in range(self.dims.dp)]
        return lax.ppermute(value, ("section", "dp"), pairs)

    def whole(self, ref, base):
        return ref[base : base + SMALL, :].astype(F32) + ref[base + SMALL : base + 2 * SMALL, :].astype(F32)

    def near_sum(self):
        dims, rows, count, cols, d = self.dims, self.rows, self.count, self.cols, self.d
        if dims.dp != 4:
            both = self.value.astype(F32) + self.other.astype(F32)
            if self.small:
                low = both[count * d :]
                self.total_small = lax.psum(low[:SMALL] + low[SMALL:], "dp")
            return both[: count * d].reshape(count, d, cols).astype(BF16)
        base = 2 * count * rows

        def body(meta_ref, ins, outs):
            value, other = ins
            sent, kept = outs
            odd = lax.rem(Ids(meta_ref, dims).dp, 2)

            def part(index, chunk):
                start = pl.multiple_of(index * d + chunk * rows, 16)
                return value[pl.ds(start, rows), :].astype(F32) + other[pl.ds(start, rows), :].astype(F32)

            for i in range(2):
                for index in range(count):
                    at = (i * count + index) * rows
                    sent[at : at + rows, :] = part(index, 2 * i + 1 - odd).astype(BF16)
                    kept[at : at + rows, :] = part(index, 2 * i + odd)
            if self.pad:
                sent[base:, :] = jnp.zeros((self.pad, cols), BF16)
            if self.small:
                total = self.whole(value, count * d) + self.whole(other, count * d)
                sent[base : base + SMALL, :], sent[base + SMALL : base + 2 * SMALL, :] = halved(total)
                kept[base:, :] = total

        outs = (arr((base + self.extra + self.pad, cols)), arr((base + self.extra // 2, cols), F32))
        sent, self.kept = run(f"{self.name}_a", body, self.meta, (self.value, self.other), outs)
        return sent

    def near_send(self, sent):
        if self.dims.dp != 4:
            whole = lax.psum_scatter(sent, "dp", scatter_dimension=1, tiled=True)
            each = self.count // len(self.pieces)
            for i in range(len(self.pieces)):
                self.pieces[i] = [whole[each * i : each * (i + 1)]] + ([self.total_small] if self.small else [])
        else:
            self.near = self.permute(sent, 1)

    def far_sum(self):
        dims, cols, size = self.dims, self.cols, self.count // len(self.names) * self.rows
        if dims.dp != 4:
            return [None] * len(self.names)

        def body(meta_ref, ins, outs):
            kept, near = ins
            mine = lax.div(Ids(meta_ref, dims).dp, 2)
            block = self.count * self.rows

            def half(i, piece):
                span = pl.ds(pl.multiple_of(i * block + piece * size, 16), size)
                return kept[span, :] + near[span, :].astype(F32)

            for piece, (sent, final) in enumerate(outs):
                sent[:size, :] = half(1 - mine, piece).astype(BF16)
                final[:size, :] = half(mine, piece)
                if self.small:
                    total = kept[2 * block :, :] + self.whole(near, 2 * block)
                    sent[size : size + SMALL, :], sent[size + SMALL :, :] = halved(total)
                    final[size:, :] = total

        out = (arr((size + self.extra, cols)), arr((size + self.extra // 2, cols), F32))
        outs = run(f"{self.name}_b", body, self.meta, (self.kept, self.near), [out] * len(self.names))
        self.final = [final for _, final in outs]
        return [sent for sent, _ in outs]

    def far_send(self, sent, piece):
        if self.dims.dp == 4:
            self.pieces[piece] = [self.final[piece], self.permute(sent[piece], 2)]

    def finish(self, piece, shapes, put, before=None):
        each = self.count // len(self.names)
        dims, rows, size = self.dims, self.rows, each * self.rows
        pieces = self.pieces[piece]
        flat = len(pieces)

        def body(meta_ref, ins, outs, *scratch):
            pieces, values, sems = ins[0], scratch[:-1], scratch[-1]

            def total(kind):
                if dims.dp != 4:
                    return pieces[0][kind].astype(F32)
                span = slice(kind * rows, (kind + 1) * rows)
                return pieces[0][span, :] + pieces[1][span, :].astype(F32)

            @pl.when(Ids(meta_ref, dims).section == self.layer)
            def _():
                small = None
                if self.small:
                    small = pieces[0][size:, :] + self.whole(pieces[1], size) if dims.dp == 4 else pieces[1][...]
                put(values, [total(index) for index in range(each)], small)
                for copy in copies(list(zip(values, outs)), sems):
                    copy.wait()

        outs = [InHbm(arr(shape, F32)) for shape in shapes]
        ins = [pieces] + ([] if before is None else [InHbm(a) for a in before])
        aliases = {} if before is None else {flat + i: i for i in range(len(shapes))}
        scratch = [pltpu.VMEM(shape, F32) for shape in shapes] + [pltpu.SemaphoreType.DMA((len(shapes),))]
        return run(f"{self.names[piece]}_end", body, self.meta, ins, outs, 8, scratch, aliases)


def pack_params(dims, meta, arrays):
    width = dims.width

    def body(meta_ref, ins, outs, *scratch):
        for copy in copies(list(zip(ins, scratch[:-1])), scratch[-1]):
            copy.wait()
        out_b, back_b, gains, shifts, in_b, qkv_b = scratch[:-1]
        for t in range(TYPES):
            for row, ref in ((OUT_B, out_b), (BACK_B, back_b), (IN_B, in_b)):
                outs[row + t : row + t + 1, :] = ref[0, t : t + 1, :]
            for row, ref in ((GAIN1, gains), (SHIFT1, shifts)):
                for norm in range(2):
                    outs[row + 2 * norm + t : row + 2 * norm + t + 1, :] = ref[0, t, norm : norm + 1, :]
            outs[QKV_B + t : QKV_B + t + 1, :] = jnp.zeros((1, dims.d), F32)
            outs[QKV_B + t : QKV_B + t + 1, :width] = qkv_b[0, t, 0:1, :]
            outs[QKV_B + t : QKV_B + t + 1, 2 * width : 3 * width] = qkv_b[0, t, 1:2, :]

    scratch = [pltpu.VMEM(a.shape, F32) for a in arrays] + [pltpu.SemaphoreType.DMA((len(arrays),))]
    return run("pack", body, meta, [InHbm(a) for a in arrays], arr((16, dims.d), F32), scratch=scratch)


def order_params(dims, meta, own, other):
    def body(meta_ref, ins, outs):
        here = meta_ref[0] == 0
        own, other = ins[0][...], ins[1][...]
        outs[0][...] = jnp.where(here, own, other)
        outs[1][...] = jnp.where(here, other, own)

    return run("params", body, meta, [own, other], [arr(own.shape, F32)] * 2)


def both_chains(dims, meta, own, moved, name):
    def body(meta_ref, ins, outs):
        own, moved = ins
        first = meta_ref[0] == 0

        @pl.when(first)
        def _():
            outs[0, 0] = own[0][...]
            outs[0, 1] = moved[0][...]

        @pl.when(jnp.logical_not(first))
        def _():
            outs[0, 0] = moved[1][...]
            outs[0, 1] = own[1][...]

    return run(name, body, meta, (own, moved), arr((1, 2, dims.length, dims.d), own[0].dtype), 8)


def body(
    tokens,
    cotangent,
    lengths,
    chain_type,
    qkv_weight,
    qkv_bias,
    out_weight,
    out_bias,
    ffn_in,
    ffn_in_bias,
    ffn_out,
    ffn_out_bias,
    norm_gain,
    norm_bias,
):
    dims = Dims()
    dims.per_chip, dims.length, dims.d = tokens.shape
    dims.slots = lax.axis_size("tensor")
    dims.dp = lax.axis_size("dp")
    dims.group = lengths.shape[0]
    dims.width = qkv_weight.shape[-1]
    dims.hidden = ffn_in.shape[-1]
    sections = lax.axis_size("section")
    assert dims.per_chip == sections == LAYERS and dims.slots & (dims.slots - 1) == 0
    assert dims.dp & (dims.dp - 1) == 0 and 4 * dims.width == dims.d == dims.hidden
    d, width, slots = dims.d, dims.width, dims.slots
    each = range(slots)
    section = lax.axis_index("section")
    meta = jnp.concatenate(
        [
            jnp.stack([section, lax.axis_index("tensor"), lax.axis_index("dp")]).astype(jnp.int32),
            chain_type,
            lengths,
        ]
    )

    own_rows = jnp.where(section == 0, tokens[0], tokens[1])
    rows = gather(own_rows, slots)

    qkv_own = qkv_weight[0].transpose(0, 2, 3, 1).reshape(TYPES, 3 * width, d)
    attn_own = pack_weights(dims, meta, qkv_own, out_weight[0])
    attn_other = swap(attn_own, "section", 1)
    packed = pack_params(
        dims, meta, (out_bias, ffn_out_bias, norm_gain, norm_bias, ffn_in_bias, qkv_bias)
    )
    small = order_params(dims, meta, packed, swap(packed, "section", 1))
    ffn_own = [ffn_in[0], ffn_out[0]]

    def moved(value, layer):
        return lax.ppermute(value, "section", [(1 - layer, layer)])

    saved = []
    acts = []
    for layer in range(LAYERS):
        (weight,) = fetch(dims, layer, meta, [attn_own], [attn_other], "attn")
        attn = [attention_forward(dims, layer, meta, k, rows[k], weight, small[layer]) for k in each]
        parts, qkv, att = ([a[i] for a in attn] for i in range(3))
        parts = scatter(parts)
        if layer == 0:
            parts, ffn_sent = tied(parts, ffn_own)
            ffn_other = [swap(w, "section", 1) for w in ffn_sent]
        first = first_norm(dims, layer, meta, own_rows, parts, small[layer])
        normed = gather(first[0], slots)
        weight = fetch(dims, layer, meta, ffn_own, ffn_other, "ffn")
        ffn = [ffn_forward(dims, layer, meta, k, normed[k], weight, small[layer]) for k in each]
        parts, act, slope = ([f[i] for f in ffn] for i in range(3))
        parts = scatter(parts)
        if layer < LAYERS - 1:
            second = second_norm(dims, layer, meta, first[1], parts, small[layer])
        else:
            second = last_norm(dims, layer, meta, first[1], parts, small[layer], cotangent)
        saved.append((rows, qkv, att, first, normed, act, slope, second))
        own_rows = second[0]
        acts.append(own_rows)
        if layer < LAYERS - 1:
            rows = gather(own_rows, slots)

    share = d // dims.dp
    ffn_shapes = [(TYPES, share, dims.hidden)]
    attn_shapes = [
        (TYPES, 3, share, width),
        (TYPES, width, share),
        (1, TYPES, 2, width),
        (1, TYPES, d),
        (1, TYPES, dims.hidden),
        (1, TYPES, d),
        (1, TYPES, 2, d),
        (1, TYPES, 2, d),
    ]

    def put_ffn(outs, totals, small):
        for index, total in enumerate(totals):
            outs[index // TYPES][index % TYPES] = total

    def put_attn(outs, totals, small):
        qkv_out, out_out, qkv_b, out_b, in_b, back_b, gains, shifts = outs
        for kind, total in enumerate(totals):
            for i in range(3):
                qkv_out[kind, i] = total[:, i * width : (i + 1) * width]
            out_out[kind] = total[:, 3 * width :].T
            qkv_b[0, kind, 0:1, :] = small[QKV_SUMS + kind : QKV_SUMS + kind + 1, :width]
            qkv_b[0, kind, 1:2, :] = small[QKV_SUMS + kind : QKV_SUMS + kind + 1, 2 * width : 3 * width]
            in_b[0, kind : kind + 1, :] = small[IN_SUMS + kind : IN_SUMS + kind + 1, :]
            for norm, (base, bias) in enumerate(((FIRST_SUMS, out_b), (SECOND_SUMS, back_b))):
                row = base + 3 * kind
                gains[0, kind, norm : norm + 1, :] = small[row : row + 1, :]
                shifts[0, kind, norm : norm + 1, :] = small[row + 1 : row + 2, :]
                bias[0, kind : kind + 1, :] = small[row + 2 : row + 3, :]

    second_grad, low = second[1:]
    input_grads = [None] * LAYERS
    ffn_sums = [GradSum(dims, layer, meta, ("in", "back") if layer else ("ffn",), False) for layer in range(LAYERS)]
    attn_sums = [GradSum(dims, layer, meta, ("attn",), True) for layer in range(LAYERS)]
    for layer in reversed(range(LAYERS)):
        rows, qkv, att, first, normed, act, slope, second = saved[layer]
        top = layer == LAYERS - 1
        grads = gather(low, slots)
        weight = fetch(dims, layer, meta, ffn_own, ffn_other, "ffn_back")
        if top:
            acts_moved = [moved(acts[i], i) for i in range(LAYERS)]
        else:
            back_done = ffn_sums[layer + 1].finish(1, ffn_shapes, put_ffn)
            grads, near, back_done, ffn_far = tied(
                grads, attn_sums[layer + 1].near_sum(), back_done, ffn_far
            )
            attn_sums[layer + 1].near_send(near)
            ffn_sums[layer + 1].far_send(ffn_far, 0)
        back = [ffn_backward(dims, layer, meta, k, grads[k], slope[k], weight) for k in each]
        parts, dpre = ([b[i] for b in back] for i in range(2))
        parts = scatter(parts)
        ffn_grad, below = ffn_weights(dims, layer, meta, normed, dpre, grads, act)
        if top:
            acts_out = both_chains(dims, meta, acts, acts_moved, "acts_out")
            parts, ffn_grad, acts_out = tied(parts, ffn_grad, acts_out)
        else:
            in_done = ffn_sums[layer + 1].finish(0, ffn_shapes, put_ffn)
            parts, ffn_grad, far, in_done = tied(parts, ffn_grad, attn_sums[layer + 1].far_sum(), in_done)
            attn_sums[layer + 1].far_send(far, 0)
        ffn_sums[layer].start(ffn_grad)
        first_grad, low = first_back(
            dims, layer, meta, parts, second_grad, first[1], first[2], small[layer]
        )
        grads = gather(low, slots)
        (weight,) = fetch(dims, layer, meta, [attn_own], [attn_other], "attn_back")
        near = ffn_sums[layer].near_sum()
        if top:
            grads, _ = tied(grads, near)
        else:
            attn_done = attn_sums[layer + 1].finish(0, attn_shapes, put_attn)
            grads, _, attn_done = tied(grads, near, attn_done)
        ffn_sums[layer].near_send(near)
        back = [attention_backward(dims, layer, meta, k, grads[k], qkv[k], weight) for k in each]
        parts, dqkv = ([b[i] for b in back] for i in range(2))
        parts = scatter(parts)
        attn_grad = attention_weights(dims, layer, meta, rows, dqkv, grads, att, below)
        if top:
            parts, attn_grad, ffn_far = tied(parts, attn_grad, ffn_sums[layer].far_sum())
            ffn_sums[layer].far_send(ffn_far, 1)
        attn_sums[layer].start(attn_grad)
        if layer > 0:
            second = saved[layer - 1][-1]
            input_grads[layer], second_grad, low = between_layers(
                dims, layer, meta, parts, first_grad, second[1], second[2], small[layer - 1]
            )
        else:
            input_grads[layer] = input_gradient(dims, layer, meta, parts, first_grad)

    ffn_far = ffn_sums[0].far_sum()
    attn_sums[0].other, _ = tied(attn_sums[0].other, ffn_far)
    ffn_sums[0].far_send(ffn_far, 0)
    attn_sums[0].near_send(attn_sums[0].near_sum())
    attn_sums[0].far_send(attn_sums[0].far_sum(), 0)
    in_total, back_total = ffn_sums[0].finish(0, ffn_shapes * 2, put_ffn, in_done + back_done)
    grads_moved = [moved(input_grads[layer], layer) for layer in range(LAYERS)]
    grads_out = both_chains(dims, meta, input_grads, grads_moved, "grads_out")
    qkv_total, out_total, *small_grads = attn_sums[0].finish(0, attn_shapes, put_attn, attn_done)
    qkv_bias_out, out_bias_out, in_bias_out, back_bias_out, gain_out, shift_out = small_grads
    return (
        acts_out,
        grads_out,
        qkv_total.transpose(0, 2, 1, 3)[None],
        qkv_bias_out,
        out_total[None],
        out_bias_out,
        in_total[None],
        in_bias_out,
        back_total.transpose(0, 2, 1)[None],
        back_bias_out,
        gain_out,
        shift_out,
    )


def solution(mesh):
    placed = (
        P(("dp", "tensor"), None, None),
        P(("dp", "tensor"), None, None),
        P("dp"),
        P("dp"),
        P("section", None, None, None, "tensor"),
        P("section", None, None, "tensor"),
        P("section", None, "tensor", None),
        P("section", None, None),
        P("section", None, None, "tensor"),
        P("section", None, "tensor"),
        P("section", None, "tensor", None),
        P("section", None, None),
        P("section", None, None, None),
        P("section", None, None, None),
    )
    return jax.shard_map(
        body,
        mesh=mesh,
        in_specs=placed,
        out_specs=(
            P("section", ("dp", "tensor"), None, None),
            P("section", ("dp", "tensor"), None, None),
            P("section", None, "dp", None, "tensor"),
            P("section", None, None, "tensor"),
            P("section", None, "tensor", "dp"),
            P("section", None, None),
            P("section", None, "dp", "tensor"),
            P("section", None, "tensor"),
            P("section", None, "tensor", "dp"),
            P("section", None, None),
            P("section", None, None, None),
            P("section", None, None, None),
        ),
        check_vma=False,
    )
```

```python
import functools
import math

import jax
import jax.numpy as jnp
from jax import lax
from jax.experimental import pallas as pl
from jax.experimental.pallas import tpu as pltpu
from jax.sharding import PartitionSpec as P

HEAD_DIM = 64
TYPES = 2
LAYERS = 2
EPS = 1e-06
HALF_ROOT = 0.7071067811865476
DENSITY = 0.3989422804014327
SCALE = 1.0 / math.sqrt(HEAD_DIM)
MIB = 1 << 20

F32 = jnp.float32
BF16 = jnp.bfloat16

TAIL = 16
PAD = 48
FIRST_SUMS, SECOND_SUMS, QKV_SUMS, IN_SUMS, SMALL = 0, 6, 12, 14, 16

OUT_B, BACK_B, GAIN1, GAIN2, SHIFT1, SHIFT2, IN_B, QKV_B = range(0, 16, 2)


def dot(a, b):
    return jnp.dot(a, b, preferred_element_type=F32)


def dot_nt(a, b):
    return lax.dot_general(a, b, (((1,), (1,)), ((), ())), preferred_element_type=F32)


def dot_tn(a, b):
    return lax.dot_general(a, b, (((0,), (0,)), ((), ())), preferred_element_type=F32)


def nested(structure, flat):
    leaves, tree = jax.tree.flatten(structure)
    return jax.tree.unflatten(tree, flat)


class InHbm:
    def __init__(self, value):
        self.value = value


def run(name, body, meta, ins, outs, limit=6, scratch=(), aliases=None):
    flat_in, flat_out = jax.tree.leaves(ins), jax.tree.leaves(outs)

    def kernel(meta_ref, *refs):
        into = len(flat_in) + len(flat_out)
        body(meta_ref, nested(ins, refs[: len(flat_in)]), nested(outs, refs[len(flat_in) : into]), *refs[into:])

    def spec(leaf):
        return pl.BlockSpec(memory_space=pltpu.HBM if isinstance(leaf, InHbm) else pltpu.VMEM)

    def plain(leaf):
        return leaf.value if isinstance(leaf, InHbm) else leaf

    results = pl.pallas_call(
        kernel,
        name=name,
        in_specs=[pl.BlockSpec(memory_space=pltpu.SMEM)] + [spec(a) for a in flat_in],
        out_specs=[spec(a) for a in flat_out],
        out_shape=[plain(a) for a in flat_out],
        scratch_shapes=list(scratch),
        input_output_aliases={1 + i: o for i, o in (aliases or {}).items()},
        compiler_params=pltpu.CompilerParams(vmem_limit_bytes=limit * MIB),
        cost_estimate=pl.CostEstimate(flops=1, bytes_accessed=1, transcendentals=0),
    )(meta, *[plain(a) for a in flat_in])
    return nested(outs, results)


def arr(shape, dtype=BF16):
    return jax.ShapeDtypeStruct(tuple(shape), dtype)


class Ids:
    def __init__(self, meta, dims):
        self.meta, self.dims = meta, dims
        self.section, self.tensor, self.dp = meta[0], meta[1], meta[2]

    def chain(self, slot):
        return (self.tensor ^ slot) * self.dims.per_chip + self.section

    def kind(self, slot):
        return self.meta[3 + self.chain(slot)]

    def length(self, slot):
        return self.meta[3 + self.dims.group + self.chain(slot)]


def copies(pairs, sems):
    started = [pltpu.make_async_copy(source, target, sems.at[i]) for i, (source, target) in enumerate(pairs)]
    for copy in started:
        copy.start()
    return started


def fetch(dims, layer, meta, own, other, name):
    def body(meta_ref, ins, outs, sems):
        own, other = ins
        ids = Ids(meta_ref, dims)

        def go(source):
            for copy in copies(list(zip(source, outs)), sems):
                copy.wait()

        pl.when(ids.section == layer)(lambda: go(own))
        pl.when(ids.section != layer)(lambda: go(other))

    ins = ([InHbm(w) for w in own], [InHbm(w) for w in other])
    outs = [arr(w.shape, w.dtype) for w in own]
    return run(f"fetch_{name}{layer}", body, meta, ins, outs, scratch=[pltpu.SemaphoreType.DMA((len(own),))])


def pack_weights(dims, meta, qkv_w, out_w):
    rows = qkv_w.shape[1]

    def body(meta_ref, ins, outs, sems):
        pairs = [(ins[0], outs.at[:, :rows]), (ins[1], outs.at[:, rows:])]
        for copy in copies(pairs, sems):
            copy.wait()

    out = InHbm(arr((TYPES, rows + out_w.shape[1], dims.d)))
    ins = (InHbm(qkv_w), InHbm(out_w))
    return run("pack_w", body, meta, ins, out, scratch=[pltpu.SemaphoreType.DMA((2,))])


class Dims:
    pass


def key_major(qkv, width, keep):
    found = []
    for c in range(0, width, HEAD_DIM):
        scores = dot_nt(qkv[:, width + c : width + c + HEAD_DIM], qkv[:, c : c + HEAD_DIM]) * SCALE
        scores = jnp.where(keep, scores, -1e9)
        expd = jnp.exp(scores - jnp.max(scores, axis=0, keepdims=True))
        found.append((expd * (1.0 / jnp.sum(expd, axis=0, keepdims=True)), c))
    return found


def attention_forward(dims, layer, meta, slot, rows, weight, small):
    length, width = dims.length, dims.width

    def body(meta_ref, ins, outs):
        rows, weight, small = ins
        part, qkv, att = outs
        ids = Ids(meta_ref, dims)
        kind = ids.kind(slot)
        bias = small[pl.ds(QKV_B + kind, 1), : 3 * width]
        qkv[...] = (dot_nt(rows[...], weight[kind, : 3 * width, :]) + bias).astype(BF16)
        keep = lax.broadcasted_iota(jnp.int32, (length, 1), 0) < ids.length(slot)
        heads = []
        for probs, c in key_major(qkv, width, keep):
            value = qkv[:, 2 * width + c : 2 * width + c + HEAD_DIM]
            heads.append(dot_tn(probs.astype(BF16), value))
        att[...] = jnp.concatenate(heads, axis=1).astype(BF16)
        part[...] = dot(att[...], weight[kind, 3 * width :, :]).astype(BF16)

    outs = (arr((length, dims.d)), arr((length, 3 * width)), arr((length, width)))
    return run(f"attn_fwd{layer}_{slot}", body, meta, (rows, weight, small), outs)


def attention_backward(dims, layer, meta, slot, grads, qkv, weight):
    length, width = dims.length, dims.width

    def body(meta_ref, ins, outs):
        grads, qkv, weight = ins
        part, dqkv = outs
        ids = Ids(meta_ref, dims)
        kind = ids.kind(slot)
        keep = lax.broadcasted_iota(jnp.int32, (length, 1), 0) < ids.length(slot)
        datt = dot_nt(grads[:length, :], weight[kind, 3 * width :, :]).astype(BF16)
        queries, keys, values = [], [], []
        for probs, c in key_major(qkv, width, keep):
            query = qkv[:, c : c + HEAD_DIM]
            key = qkv[:, width + c : width + c + HEAD_DIM]
            da = datt[:, c : c + HEAD_DIM]
            dprobs = dot_nt(qkv[:, 2 * width + c : 2 * width + c + HEAD_DIM], da)
            dscores = (probs * (dprobs - jnp.sum(probs * dprobs, axis=0, keepdims=True))).astype(BF16)
            queries.append(dot_tn(dscores, key) * SCALE)
            keys.append(dot(dscores, query) * SCALE)
            values.append(dot(probs.astype(BF16), da))
        dqkv[...] = jnp.concatenate(queries + keys + values, axis=1).astype(BF16)
        part[...] = dot(dqkv[...], weight[kind, : 3 * width, :]).astype(BF16)

    outs = (arr((length, dims.d)), arr((length, 3 * width)))
    return run(f"attn_bwd{layer}_{slot}", body, meta, (grads, qkv, weight), outs)


def typed_sum(ids, left, right, kind, slots):
    chosen = [
        jnp.where(ids.kind(k) == kind, right[k], jnp.zeros_like(right[k])) for k in range(slots)
    ]
    return dot_tn(jnp.concatenate(left, axis=0), jnp.concatenate(chosen, axis=0))


def halved(value):
    high = value.astype(BF16)
    return high, (value - high.astype(F32)).astype(BF16)


def carried(ids, blocks, slots, r):
    found = []
    for kind in range(TYPES):
        total = jnp.zeros((3, blocks[0].shape[1]), F32)
        for k in range(slots):
            tail = blocks[k][r : r + TAIL, :].astype(F32)
            total = total + jnp.where(ids.kind(k) == kind, tail[0:3] + tail[3:6], 0.0)
        found.append(total)
    return jnp.concatenate(found, axis=0)


def row_sums(ids, slots, rows):
    found = []
    for kind in range(TYPES):
        total = 0.0
        for k in range(slots):
            here = jnp.sum(rows[k].astype(F32), axis=0, keepdims=True)
            total = total + jnp.where(ids.kind(k) == kind, here, 0.0)
        found.append(total)
    return jnp.concatenate(found, axis=0)


def attention_weights(dims, layer, meta, rows, dqkv, grads, att, below):
    length, slots, width, d = dims.length, dims.slots, dims.width, dims.d

    def body(meta_ref, ins, outs):
        rows, dqkv, grads, att, below = ins
        ids = Ids(meta_ref, dims)
        left = [ref[...] for ref in rows]
        back = [ref[:length, :] for ref in grads]
        right = [ref[...] for ref in dqkv]
        heads = [ref[...] for ref in att]
        for kind in range(TYPES):
            span = slice(kind * d, (kind + 1) * d)
            outs[span, : 3 * width] = typed_sum(ids, left, right, kind, slots).astype(BF16)
            outs[span, 3 * width :] = typed_sum(ids, back, heads, kind, slots).astype(BF16)
        qkv_rows = row_sums(ids, slots, right)
        qkv_rows = jnp.concatenate([qkv_rows, jnp.zeros((TYPES, width), F32)], axis=1)
        firsts = carried(ids, grads, slots, length)
        small = jnp.concatenate([firsts, below[:6, :], qkv_rows, below[6:8, :]], axis=0)
        outs[TYPES * d : TYPES * d + SMALL, :], outs[TYPES * d + SMALL :, :] = halved(small)

    out = arr((TYPES * d + 2 * SMALL, d))
    return run(f"attn_dw{layer}", body, meta, (rows, dqkv, grads, att, below), out, 8)


def ffn_weights(dims, layer, meta, rows, dpre, grads, act):
    length, slots, hidden, d = dims.length, dims.slots, dims.hidden, dims.d

    def body(meta_ref, ins, outs):
        rows, dpre, grads, act = ins
        total, small = outs
        ids = Ids(meta_ref, dims)
        for step, (left, right) in enumerate(((rows, dpre), (grads, act))):
            left_rows = [ref[:length, :] for ref in left]
            right_rows = [ref[...] for ref in right]
            for kind in range(TYPES):
                first = (TYPES * step + kind) * d
                total[first : first + d, :] = typed_sum(ids, left_rows, right_rows, kind, slots).astype(BF16)
        small[0:6, :] = carried(ids, grads, slots, length)
        small[6:8, :] = row_sums(ids, slots, [ref[...] for ref in dpre])

    outs = (arr((2 * TYPES * d, hidden)), arr((8, hidden), F32))
    return run(f"ffn_dw{layer}", body, meta, (rows, dpre, grads, act), outs, 8)


def ffn_forward(dims, layer, meta, slot, rows, weight, small):
    length, hidden = dims.length, dims.hidden

    def body(meta_ref, ins, outs):
        rows, (in_w, back_w), small = ins
        part, act, slope = outs
        kind = Ids(meta_ref, dims).kind(slot)
        pre = dot(rows[...], in_w[kind]) + small[pl.ds(IN_B + kind, 1), :hidden]
        gate = 0.5 * (1.0 + lax.erf(pre * HALF_ROOT))
        act[...] = (pre * gate).astype(BF16)
        slope[...] = (gate + pre * (DENSITY * jnp.exp(-0.5 * pre * pre))).astype(BF16)
        part[...] = dot(act[...], back_w[kind]).astype(BF16)

    outs = (arr((length, dims.d)), arr((length, hidden)), arr((length, hidden)))
    return run(f"ffn_fwd{layer}_{slot}", body, meta, (rows, weight, small), outs)


def ffn_backward(dims, layer, meta, slot, grads, slope, weight):
    length, hidden = dims.length, dims.hidden

    def body(meta_ref, ins, outs):
        grads, slope, (in_w, back_w) = ins
        part, dpre = outs
        kind = Ids(meta_ref, dims).kind(slot)
        dact = dot_nt(grads[:length, :], back_w[kind])
        dpre[...] = (dact * slope[...].astype(F32)).astype(BF16)
        part[...] = dot_nt(dpre[...], in_w[kind]).astype(BF16)

    outs = (arr((length, dims.d)), arr((length, hidden)))
    return run(f"ffn_bwd{layer}_{slot}", body, meta, (grads, slope, weight), outs)


def normalized(values):
    center = values - jnp.mean(values, axis=-1, keepdims=True)
    inv = lax.rsqrt(jnp.mean(center * center, axis=-1, keepdims=True) + EPS)
    return center * inv, inv


def summed(parts):
    total = parts[0][...].astype(F32)
    for part in parts[1:]:
        total = total + part[...].astype(F32)
    return total


def norm_back(grad, normal, inv, gain):
    scaled = grad * gain
    return inv * (
        scaled
        - jnp.mean(scaled, axis=-1, keepdims=True)
        - normal * jnp.mean(scaled * normal, axis=-1, keepdims=True)
    )


def with_sums(low, value, sums):
    r = value.shape[0]
    low[:r, :] = value.astype(BF16)
    total = jnp.concatenate([jnp.sum(v, axis=0, keepdims=True) for v in sums], axis=0)
    high, rest = halved(total)
    blank = jnp.zeros((TAIL - 6, value.shape[1]), BF16)
    low[r:, :] = jnp.concatenate([high, rest, blank], axis=0)


def first_norm(dims, layer, meta, own_rows, parts, small):
    r, d = dims.length, dims.d

    def body(meta_ref, ins, outs):
        own_rows, parts, small = ins
        low, normal, inv = outs
        kind = Ids(meta_ref, dims).kind(0)
        mixed = own_rows[...].astype(F32) + summed(parts) + small[pl.ds(OUT_B + kind, 1), :]
        xhat, scale = normalized(mixed)
        normal[...] = xhat
        inv[...] = jnp.broadcast_to(scale, inv.shape)
        low[...] = (xhat * small[pl.ds(GAIN1 + kind, 1), :] + small[pl.ds(SHIFT1 + kind, 1), :]).astype(BF16)

    outs = (arr((r, d)), arr((r, d), F32), arr((r, 128), F32))
    return run(f"norm1_{layer}", body, meta, (own_rows, parts, small), outs)


def second_values(kind, normal, parts, small):
    normed = normal[...] * small[pl.ds(GAIN1 + kind, 1), :] + small[pl.ds(SHIFT1 + kind, 1), :]
    xhat, scale = normalized(normed + summed(parts) + small[pl.ds(BACK_B + kind, 1), :])
    output = xhat * small[pl.ds(GAIN2 + kind, 1), :] + small[pl.ds(SHIFT2 + kind, 1), :]
    return xhat, scale, output.astype(BF16)


def second_norm(dims, layer, meta, normal, parts, small):
    r, d = dims.length, dims.d

    def body(meta_ref, ins, outs):
        normal, parts, small = ins
        low, xhat_ref, inv = outs
        kind = Ids(meta_ref, dims).kind(0)
        xhat, scale, low[...] = second_values(kind, normal, parts, small)
        xhat_ref[...] = xhat
        inv[...] = jnp.broadcast_to(scale, inv.shape)

    outs = (arr((r, d)), arr((r, d), F32), arr((r, 128), F32))
    return run(f"norm2_{layer}", body, meta, (normal, parts, small), outs)


def second_back(kind, grad, xhat, scale, small, second_grad, low):
    value = norm_back(grad, xhat, scale, small[pl.ds(GAIN2 + kind, 1), :])
    second_grad[...] = value
    with_sums(low, value, (grad * xhat, grad, value))


def last_norm(dims, layer, meta, normal, parts, small, cotangent):
    r, d = dims.length, dims.d

    def body(meta_ref, ins, outs):
        normal, parts, small, cotangent = ins
        act, second_grad, low = outs
        ids = Ids(meta_ref, dims)
        kind = ids.kind(0)
        xhat, scale, act[...] = second_values(kind, normal, parts, small)
        grad = cotangent[ids.section].astype(F32)
        second_back(kind, grad, xhat, scale, small, second_grad, low)

    outs = (arr((r, d)), arr((r, d), F32), arr((r + TAIL, d)))
    return run(f"norm2_{layer}", body, meta, (normal, parts, small, cotangent), outs)


def between_layers(dims, layer, meta, parts, first_grad, xhat, inv, small):
    r, d = dims.length, dims.d

    def body(meta_ref, ins, outs):
        parts, first_grad, xhat, inv, small = ins
        input_grad, second_grad, low = outs
        kind = Ids(meta_ref, dims).kind(0)
        value = summed(parts) + first_grad[...]
        input_grad[...] = value
        grad = value.astype(BF16).astype(F32)
        second_back(kind, grad, xhat[...], inv[:, :1], small, second_grad, low)

    outs = (arr((r, d), F32), arr((r, d), F32), arr((r + TAIL, d)))
    return run(f"between{layer}", body, meta, (parts, first_grad, xhat, inv, small), outs)


def first_back(dims, layer, meta, parts, second_grad, xhat, inv, small):
    r, d = dims.length, dims.d

    def body(meta_ref, ins, outs):
        parts, second_grad, xhat, inv, small = ins
        first_grad, low = outs
        kind = Ids(meta_ref, dims).kind(0)
        grad = summed(parts) + second_grad[...]
        value = norm_back(grad, xhat[...], inv[:, :1], small[pl.ds(GAIN1 + kind, 1), :])
        first_grad[...] = value
        with_sums(low, value, (grad * xhat[...], grad, value))

    outs = (arr((r, d), F32), arr((r + TAIL, d)))
    return run(f"norm1_back{layer}", body, meta, (parts, second_grad, xhat, inv, small), outs)


def input_gradient(dims, layer, meta, parts, first_grad):
    def body(meta_ref, ins, outs):
        parts, first_grad = ins
        outs[...] = summed(parts) + first_grad[...]

    return run(f"input_grad{layer}", body, meta, (parts, first_grad), arr((dims.length, dims.d), F32))


def swap(value, axis, bit):
    count = lax.axis_size(axis)
    return lax.ppermute(value, axis, [(source, source ^ bit) for source in range(count)])


def gather(value, slots):
    return [value] + [swap(value, "tensor", k) for k in range(1, slots)]


def scatter(parts):
    return [parts[0]] + [swap(part, "tensor", k) for k, part in enumerate(parts) if k]


def tied(*values):
    return lax.optimization_barrier(values)


class GradSum:
    def __init__(self, dims, layer, meta, names, small):
        self.dims, self.layer, self.meta, self.names = dims, layer, meta, [f"{name}{layer}" for name in names]
        self.name, self.small, self.pieces = "_".join(self.names), small, [None] * len(names)

    def start(self, value):
        self.value = value
        self.d, self.cols = self.dims.d, value.shape[1]
        self.count = value.shape[0] // self.d
        self.rows = self.d // self.dims.dp
        self.extra = 2 * SMALL if self.small else 0
        self.pad = 0 if self.small else PAD
        self.other = lax.ppermute(value, "section", [(1 - self.layer, self.layer)])

    def permute(self, value, bit):
        base = self.layer * self.dims.dp
        pairs = [(base + z, base + (z ^ bit)) for z in range(self.dims.dp)]
        return lax.ppermute(value, ("section", "dp"), pairs)

    def whole(self, ref, base):
        return ref[base : base + SMALL, :].astype(F32) + ref[base + SMALL : base + 2 * SMALL, :].astype(F32)

    def near_sum(self):
        dims, rows, count, cols, d = self.dims, self.rows, self.count, self.cols, self.d
        if dims.dp != 4:
            both = self.value.astype(F32) + self.other.astype(F32)
            if self.small:
                low = both[count * d :]
                self.total_small = lax.psum(low[:SMALL] + low[SMALL:], "dp")
            return both[: count * d].reshape(count, d, cols).astype(BF16)
        base = 2 * count * rows

        def body(meta_ref, ins, outs):
            value, other = ins
            sent, kept = outs
            odd = lax.rem(Ids(meta_ref, dims).dp, 2)

            def part(index, chunk):
                start = pl.multiple_of(index * d + chunk * rows, 16)
                return value[pl.ds(start, rows), :].astype(F32) + other[pl.ds(start, rows), :].astype(F32)

            for i in range(2):
                for index in range(count):
                    at = (i * count + index) * rows
                    sent[at : at + rows, :] = part(index, 2 * i + 1 - odd).astype(BF16)
                    kept[at : at + rows, :] = part(index, 2 * i + odd)
            if self.pad:
                sent[base:, :] = jnp.zeros((self.pad, cols), BF16)
            if self.small:
                total = self.whole(value, count * d) + self.whole(other, count * d)
                sent[base : base + SMALL, :], sent[base + SMALL : base + 2 * SMALL, :] = halved(total)
                kept[base:, :] = total

        outs = (arr((base + self.extra + self.pad, cols)), arr((base + self.extra // 2, cols), F32))
        sent, self.kept = run(f"{self.name}_a", body, self.meta, (self.value, self.other), outs)
        return sent

    def near_send(self, sent):
        if self.dims.dp != 4:
            whole = lax.psum_scatter(sent, "dp", scatter_dimension=1, tiled=True)
            each = self.count // len(self.pieces)
            for i in range(len(self.pieces)):
                self.pieces[i] = [whole[each * i : each * (i + 1)]] + ([self.total_small] if self.small else [])
        else:
            self.near = self.permute(sent, 1)

    def far_sum(self):
        dims, cols, size = self.dims, self.cols, self.count // len(self.names) * self.rows
        if dims.dp != 4:
            return [None] * len(self.names)

        def body(meta_ref, ins, outs):
            kept, near = ins
            mine = lax.div(Ids(meta_ref, dims).dp, 2)
            block = self.count * self.rows

            def half(i, piece):
                span = pl.ds(pl.multiple_of(i * block + piece * size, 16), size)
                return kept[span, :] + near[span, :].astype(F32)

            for piece, (sent, final) in enumerate(outs):
                sent[:size, :] = half(1 - mine, piece).astype(BF16)
                final[:size, :] = half(mine, piece)
                if self.small:
                    total = kept[2 * block :, :] + self.whole(near, 2 * block)
                    sent[size : size + SMALL, :], sent[size + SMALL :, :] = halved(total)
                    final[size:, :] = total

        out = (arr((size + self.extra, cols)), arr((size + self.extra // 2, cols), F32))
        outs = run(f"{self.name}_b", body, self.meta, (self.kept, self.near), [out] * len(self.names))
        self.final = [final for _, final in outs]
        return [sent for sent, _ in outs]

    def far_send(self, sent, piece):
        if self.dims.dp == 4:
            self.pieces[piece] = [self.final[piece], self.permute(sent[piece], 2)]

    def finish(self, piece, shapes, put, before=None):
        each = self.count // len(self.names)
        dims, rows, size = self.dims, self.rows, each * self.rows
        pieces = self.pieces[piece]
        flat = len(pieces)

        def body(meta_ref, ins, outs, *scratch):
            pieces, values, sems = ins[0], scratch[:-1], scratch[-1]

            def total(kind):
                if dims.dp != 4:
                    return pieces[0][kind].astype(F32)
                span = slice(kind * rows, (kind + 1) * rows)
                return pieces[0][span, :] + pieces[1][span, :].astype(F32)

            @pl.when(Ids(meta_ref, dims).section == self.layer)
            def _():
                small = None
                if self.small:
                    small = pieces[0][size:, :] + self.whole(pieces[1], size) if dims.dp == 4 else pieces[1][...]
                put(values, [total(index) for index in range(each)], small)
                for copy in copies(list(zip(values, outs)), sems):
                    copy.wait()

        outs = [InHbm(arr(shape, F32)) for shape in shapes]
        ins = [pieces] + ([] if before is None else [InHbm(a) for a in before])
        aliases = {} if before is None else {flat + i: i for i in range(len(shapes))}
        scratch = [pltpu.VMEM(shape, F32) for shape in shapes] + [pltpu.SemaphoreType.DMA((len(shapes),))]
        return run(f"{self.names[piece]}_end", body, self.meta, ins, outs, 8, scratch, aliases)


def pack_params(dims, meta, arrays):
    width = dims.width

    def body(meta_ref, ins, outs, *scratch):
        for copy in copies(list(zip(ins, scratch[:-1])), scratch[-1]):
            copy.wait()
        out_b, back_b, gains, shifts, in_b, qkv_b = scratch[:-1]
        for t in range(TYPES):
            for row, ref in ((OUT_B, out_b), (BACK_B, back_b), (IN_B, in_b)):
                outs[row + t : row + t + 1, :] = ref[0, t : t + 1, :]
            for row, ref in ((GAIN1, gains), (SHIFT1, shifts)):
                for norm in range(2):
                    outs[row + 2 * norm + t : row + 2 * norm + t + 1, :] = ref[0, t, norm : norm + 1, :]
            outs[QKV_B + t : QKV_B + t + 1, :] = jnp.zeros((1, dims.d), F32)
            outs[QKV_B + t : QKV_B + t + 1, :width] = qkv_b[0, t, 0:1, :]
            outs[QKV_B + t : QKV_B + t + 1, 2 * width : 3 * width] = qkv_b[0, t, 1:2, :]

    scratch = [pltpu.VMEM(a.shape, F32) for a in arrays] + [pltpu.SemaphoreType.DMA((len(arrays),))]
    return run("pack", body, meta, [InHbm(a) for a in arrays], arr((16, dims.d), F32), scratch=scratch)


def order_params(dims, meta, own, other):
    def body(meta_ref, ins, outs):
        here = meta_ref[0] == 0
        own, other = ins[0][...], ins[1][...]
        outs[0][...] = jnp.where(here, own, other)
        outs[1][...] = jnp.where(here, other, own)

    return run("params", body, meta, [own, other], [arr(own.shape, F32)] * 2)


def both_chains(dims, meta, own, moved, name):
    def body(meta_ref, ins, outs):
        own, moved = ins
        first = meta_ref[0] == 0

        @pl.when(first)
        def _():
            outs[0, 0] = own[0][...]
            outs[0, 1] = moved[0][...]

        @pl.when(jnp.logical_not(first))
        def _():
            outs[0, 0] = moved[1][...]
            outs[0, 1] = own[1][...]

    return run(name, body, meta, (own, moved), arr((1, 2, dims.length, dims.d), own[0].dtype), 8)


def body(
    tokens,
    cotangent,
    lengths,
    chain_type,
    qkv_weight,
    qkv_bias,
    out_weight,
    out_bias,
    ffn_in,
    ffn_in_bias,
    ffn_out,
    ffn_out_bias,
    norm_gain,
    norm_bias,
):
    dims = Dims()
    dims.per_chip, dims.length, dims.d = tokens.shape
    dims.slots = lax.axis_size("tensor")
    dims.dp = lax.axis_size("dp")
    dims.group = lengths.shape[0]
    dims.width = qkv_weight.shape[-1]
    dims.hidden = ffn_in.shape[-1]
    sections = lax.axis_size("section")
    assert dims.per_chip == sections == LAYERS and dims.slots & (dims.slots - 1) == 0
    assert dims.dp & (dims.dp - 1) == 0 and 4 * dims.width == dims.d == dims.hidden
    d, width, slots = dims.d, dims.width, dims.slots
    each = range(slots)
    section = lax.axis_index("section")
    meta = jnp.concatenate(
        [
            jnp.stack([section, lax.axis_index("tensor"), lax.axis_index("dp")]).astype(jnp.int32),
            chain_type,
            lengths,
        ]
    )

    own_rows = jnp.where(section == 0, tokens[0], tokens[1])
    rows = gather(own_rows, slots)

    qkv_own = qkv_weight[0].transpose(0, 2, 3, 1).reshape(TYPES, 3 * width, d)
    attn_own = pack_weights(dims, meta, qkv_own, out_weight[0])
    attn_other = swap(attn_own, "section", 1)
    packed = pack_params(
        dims, meta, (out_bias, ffn_out_bias, norm_gain, norm_bias, ffn_in_bias, qkv_bias)
    )
    small = order_params(dims, meta, packed, swap(packed, "section", 1))
    ffn_own = [ffn_in[0], ffn_out[0]]

    def moved(value, layer):
        return lax.ppermute(value, "section", [(1 - layer, layer)])

    saved = []
    acts = []
    for layer in range(LAYERS):
        (weight,) = fetch(dims, layer, meta, [attn_own], [attn_other], "attn")
        attn = [attention_forward(dims, layer, meta, k, rows[k], weight, small[layer]) for k in each]
        parts, qkv, att = ([a[i] for a in attn] for i in range(3))
        parts = scatter(parts)
        if layer == 0:
            parts, ffn_sent = tied(parts, ffn_own)
            ffn_other = [swap(w, "section", 1) for w in ffn_sent]
        first = first_norm(dims, layer, meta, own_rows, parts, small[layer])
        normed = gather(first[0], slots)
        weight = fetch(dims, layer, meta, ffn_own, ffn_other, "ffn")
        ffn = [ffn_forward(dims, layer, meta, k, normed[k], weight, small[layer]) for k in each]
        parts, act, slope = ([f[i] for f in ffn] for i in range(3))
        parts = scatter(parts)
        if layer < LAYERS - 1:
            second = second_norm(dims, layer, meta, first[1], parts, small[layer])
        else:
            second = last_norm(dims, layer, meta, first[1], parts, small[layer], cotangent)
        saved.append((rows, qkv, att, first, normed, act, slope, second))
        own_rows = second[0]
        acts.append(own_rows)
        if layer < LAYERS - 1:
            rows = gather(own_rows, slots)

    share = d // dims.dp
    ffn_shapes = [(TYPES, share, dims.hidden)]
    attn_shapes = [
        (TYPES, 3, share, width),
        (TYPES, width, share),
        (1, TYPES, 2, width),
        (1, TYPES, d),
        (1, TYPES, dims.hidden),
        (1, TYPES, d),
        (1, TYPES, 2, d),
        (1, TYPES, 2, d),
    ]

    def put_ffn(outs, totals, small):
        for index, total in enumerate(totals):
            outs[index // TYPES][index % TYPES] = total

    def put_attn(outs, totals, small):
        qkv_out, out_out, qkv_b, out_b, in_b, back_b, gains, shifts = outs
        for kind, total in enumerate(totals):
            for i in range(3):
                qkv_out[kind, i] = total[:, i * width : (i + 1) * width]
            out_out[kind] = total[:, 3 * width :].T
            qkv_b[0, kind, 0:1, :] = small[QKV_SUMS + kind : QKV_SUMS + kind + 1, :width]
            qkv_b[0, kind, 1:2, :] = small[QKV_SUMS + kind : QKV_SUMS + kind + 1, 2 * width : 3 * width]
            in_b[0, kind : kind + 1, :] = small[IN_SUMS + kind : IN_SUMS + kind + 1, :]
            for norm, (base, bias) in enumerate(((FIRST_SUMS, out_b), (SECOND_SUMS, back_b))):
                row = base + 3 * kind
                gains[0, kind, norm : norm + 1, :] = small[row : row + 1, :]
                shifts[0, kind, norm : norm + 1, :] = small[row + 1 : row + 2, :]
                bias[0, kind : kind + 1, :] = small[row + 2 : row + 3, :]

    second_grad, low = second[1:]
    input_grads = [None] * LAYERS
    ffn_sums = [GradSum(dims, layer, meta, ("in", "back") if layer else ("ffn",), False) for layer in range(LAYERS)]
    attn_sums = [GradSum(dims, layer, meta, ("attn",), True) for layer in range(LAYERS)]
    for layer in reversed(range(LAYERS)):
        rows, qkv, att, first, normed, act, slope, second = saved[layer]
        top = layer == LAYERS - 1
        grads = gather(low, slots)
        weight = fetch(dims, layer, meta, ffn_own, ffn_other, "ffn_back")
        if top:
            acts_moved = [moved(acts[i], i) for i in range(LAYERS)]
        else:
            ffn_up, attn_up = ffn_sums[layer + 1], attn_sums[layer + 1]
            grads, near, ffn_up.pieces[1], ffn_far = tied(
                grads, attn_up.near_sum(), ffn_up.pieces[1], ffn_far
            )
            attn_sums[layer + 1].near_send(near)
            ffn_sums[layer + 1].far_send(ffn_far, 0)
        back = [ffn_backward(dims, layer, meta, k, grads[k], slope[k], weight) for k in each]
        parts, dpre = ([b[i] for b in back] for i in range(2))
        parts = scatter(parts)
        ffn_grad, below = ffn_weights(dims, layer, meta, normed, dpre, grads, act)
        if top:
            acts_out = both_chains(dims, meta, acts, acts_moved, "acts_out")
            parts, ffn_grad, acts_out = tied(parts, ffn_grad, acts_out)
        else:
            far = attn_up.far_sum()
            parts, ffn_grad, far, ffn_up.pieces[0] = tied(parts, ffn_grad, far, ffn_up.pieces[0])
            attn_sums[layer + 1].far_send(far, 0)
        ffn_sums[layer].start(ffn_grad)
        first_grad, low = first_back(
            dims, layer, meta, parts, second_grad, first[1], first[2], small[layer]
        )
        grads = gather(low, slots)
        (weight,) = fetch(dims, layer, meta, [attn_own], [attn_other], "attn_back")
        near = ffn_sums[layer].near_sum()
        grads, _ = tied(grads, near)
        ffn_sums[layer].near_send(near)
        back = [attention_backward(dims, layer, meta, k, grads[k], qkv[k], weight) for k in each]
        parts, dqkv = ([b[i] for b in back] for i in range(2))
        parts = scatter(parts)
        if not top:
            dqkv, attn_up.pieces[0] = tied(dqkv, attn_up.pieces[0])
        attn_grad = attention_weights(dims, layer, meta, rows, dqkv, grads, att, below)
        if top:
            parts, attn_grad, ffn_far = tied(parts, attn_grad, ffn_sums[layer].far_sum())
            ffn_sums[layer].far_send(ffn_far, 1)
        attn_sums[layer].start(attn_grad)
        if layer > 0:
            second = saved[layer - 1][-1]
            input_grads[layer], second_grad, low = between_layers(
                dims, layer, meta, parts, first_grad, second[1], second[2], small[layer - 1]
            )
        else:
            input_grads[layer] = input_gradient(dims, layer, meta, parts, first_grad)

    back_done = ffn_up.finish(1, ffn_shapes, put_ffn)
    in_done = ffn_up.finish(0, ffn_shapes, put_ffn)
    attn_done = attn_up.finish(0, attn_shapes, put_attn)
    ffn_far = ffn_sums[0].far_sum()
    attn_sums[0].other, _ = tied(attn_sums[0].other, ffn_far)
    ffn_sums[0].far_send(ffn_far, 0)
    attn_sums[0].near_send(attn_sums[0].near_sum())
    attn_sums[0].far_send(attn_sums[0].far_sum(), 0)
    in_total, back_total = ffn_sums[0].finish(0, ffn_shapes * 2, put_ffn, in_done + back_done)
    grads_moved = [moved(input_grads[layer], layer) for layer in range(LAYERS)]
    grads_out = both_chains(dims, meta, input_grads, grads_moved, "grads_out")
    qkv_total, out_total, *small_grads = attn_sums[0].finish(0, attn_shapes, put_attn, attn_done)
    qkv_bias_out, out_bias_out, in_bias_out, back_bias_out, gain_out, shift_out = small_grads
    return (
        acts_out,
        grads_out,
        qkv_total.transpose(0, 2, 1, 3)[None],
        qkv_bias_out,
        out_total[None],
        out_bias_out,
        in_total[None],
        in_bias_out,
        back_total.transpose(0, 2, 1)[None],
        back_bias_out,
        gain_out,
        shift_out,
    )


def solution(mesh):
    placed = (
        P(("dp", "tensor"), None, None),
        P(("dp", "tensor"), None, None),
        P("dp"),
        P("dp"),
        P("section", None, None, None, "tensor"),
        P("section", None, None, "tensor"),
        P("section", None, "tensor", None),
        P("section", None, None),
        P("section", None, None, "tensor"),
        P("section", None, "tensor"),
        P("section", None, "tensor", None),
        P("section", None, None),
        P("section", None, None, None),
        P("section", None, None, None),
    )
    return jax.shard_map(
        body,
        mesh=mesh,
        in_specs=placed,
        out_specs=(
            P("section", ("dp", "tensor"), None, None),
            P("section", ("dp", "tensor"), None, None),
            P("section", None, "dp", None, "tensor"),
            P("section", None, None, "tensor"),
            P("section", None, "tensor", "dp"),
            P("section", None, None),
            P("section", None, "dp", "tensor"),
            P("section", None, "tensor"),
            P("section", None, "tensor", "dp"),
            P("section", None, None),
            P("section", None, None, None),
            P("section", None, None, None),
        ),
        check_vma=False,
    )
```

```python
import functools
import math

import jax
import jax.numpy as jnp
from jax import lax
from jax.experimental import pallas as pl
from jax.experimental.pallas import tpu as pltpu
from jax.sharding import PartitionSpec as P

HEAD_DIM = 64
TYPES = 2
LAYERS = 2
EPS = 1e-06
HALF_ROOT = 0.7071067811865476
DENSITY = 0.3989422804014327
SCALE = 1.0 / math.sqrt(HEAD_DIM)
MIB = 1 << 20

F32 = jnp.float32
BF16 = jnp.bfloat16

TAIL = 16
PAD = 64
FIRST_SUMS, SECOND_SUMS, QKV_SUMS, IN_SUMS, SMALL = 0, 6, 12, 14, 16

OUT_B, BACK_B, GAIN1, GAIN2, SHIFT1, SHIFT2, IN_B, QKV_B = range(0, 16, 2)


def dot(a, b):
    return jnp.dot(a, b, preferred_element_type=F32)


def dot_nt(a, b):
    return lax.dot_general(a, b, (((1,), (1,)), ((), ())), preferred_element_type=F32)


def dot_tn(a, b):
    return lax.dot_general(a, b, (((0,), (0,)), ((), ())), preferred_element_type=F32)


def nested(structure, flat):
    leaves, tree = jax.tree.flatten(structure)
    return jax.tree.unflatten(tree, flat)


class InHbm:
    def __init__(self, value):
        self.value = value


def run(name, body, meta, ins, outs, limit=6, scratch=(), aliases=None):
    flat_in, flat_out = jax.tree.leaves(ins), jax.tree.leaves(outs)

    def kernel(meta_ref, *refs):
        into = len(flat_in) + len(flat_out)
        body(meta_ref, nested(ins, refs[: len(flat_in)]), nested(outs, refs[len(flat_in) : into]), *refs[into:])

    def spec(leaf):
        return pl.BlockSpec(memory_space=pltpu.HBM if isinstance(leaf, InHbm) else pltpu.VMEM)

    def plain(leaf):
        return leaf.value if isinstance(leaf, InHbm) else leaf

    results = pl.pallas_call(
        kernel,
        name=name,
        in_specs=[pl.BlockSpec(memory_space=pltpu.SMEM)] + [spec(a) for a in flat_in],
        out_specs=[spec(a) for a in flat_out],
        out_shape=[plain(a) for a in flat_out],
        scratch_shapes=list(scratch),
        input_output_aliases={1 + i: o for i, o in (aliases or {}).items()},
        compiler_params=pltpu.CompilerParams(vmem_limit_bytes=limit * MIB),
        cost_estimate=pl.CostEstimate(flops=1, bytes_accessed=1, transcendentals=0),
    )(meta, *[plain(a) for a in flat_in])
    return nested(outs, results)


def arr(shape, dtype=BF16):
    return jax.ShapeDtypeStruct(tuple(shape), dtype)


class Ids:
    def __init__(self, meta, dims):
        self.meta, self.dims = meta, dims
        self.section, self.tensor, self.dp = meta[0], meta[1], meta[2]

    def chain(self, slot):
        return (self.tensor ^ slot) * self.dims.per_chip + self.section

    def kind(self, slot):
        return self.meta[3 + self.chain(slot)]

    def length(self, slot):
        return self.meta[3 + self.dims.group + self.chain(slot)]


def copies(pairs, sems):
    started = [pltpu.make_async_copy(source, target, sems.at[i]) for i, (source, target) in enumerate(pairs)]
    for copy in started:
        copy.start()
    return started


def fetch(dims, layer, meta, own, other, name):
    def body(meta_ref, ins, outs, sems):
        own, other = ins
        ids = Ids(meta_ref, dims)

        def go(source):
            for copy in copies(list(zip(source, outs)), sems):
                copy.wait()

        pl.when(ids.section == layer)(lambda: go(own))
        pl.when(ids.section != layer)(lambda: go(other))

    ins = ([InHbm(w) for w in own], [InHbm(w) for w in other])
    outs = [arr(w.shape, w.dtype) for w in own]
    return run(f"fetch_{name}{layer}", body, meta, ins, outs, scratch=[pltpu.SemaphoreType.DMA((len(own),))])


class Dims:
    pass


def key_major(qkv, width, keep):
    found = []
    for c in range(0, width, HEAD_DIM):
        scores = dot_nt(qkv[:, width + c : width + c + HEAD_DIM], qkv[:, c : c + HEAD_DIM]) * SCALE
        scores = jnp.where(keep, scores, -1e9)
        expd = jnp.exp(scores - jnp.max(scores, axis=0, keepdims=True))
        found.append((expd * (1.0 / jnp.sum(expd, axis=0, keepdims=True)), c))
    return found


def attention_forward(dims, layer, meta, slot, rows, weight, biases):
    length, width = dims.length, dims.width

    def body(meta_ref, ins, outs):
        rows, (qkv_w, out_w), biases = ins
        part, qkv, att = outs
        ids = Ids(meta_ref, dims)
        kind = ids.kind(slot)
        here = ids.section == layer
        parts = [jnp.where(here, biases[0][0, kind, i : i + 1, :], biases[1][0, kind, i : i + 1, :]) for i in range(2)]
        bias = jnp.concatenate([parts[0], jnp.zeros_like(parts[0]), parts[1]], axis=1)
        qkv[...] = (dot_nt(rows[...], qkv_w[kind]) + bias).astype(BF16)
        keep = lax.broadcasted_iota(jnp.int32, (length, 1), 0) < ids.length(slot)
        heads = []
        for probs, c in key_major(qkv, width, keep):
            value = qkv[:, 2 * width + c : 2 * width + c + HEAD_DIM]
            heads.append(dot_tn(probs.astype(BF16), value))
        att[...] = jnp.concatenate(heads, axis=1).astype(BF16)
        part[...] = dot(att[...], out_w[kind]).astype(BF16)

    outs = (arr((length, dims.d)), arr((length, 3 * width)), arr((length, width)))
    return run(f"attn_fwd{layer}_{slot}", body, meta, (rows, weight, biases), outs)


def attention_backward(dims, layer, meta, slot, grads, qkv, weight):
    length, width = dims.length, dims.width

    def body(meta_ref, ins, outs):
        grads, qkv, (qkv_w, out_w) = ins
        part, dqkv = outs
        ids = Ids(meta_ref, dims)
        kind = ids.kind(slot)
        keep = lax.broadcasted_iota(jnp.int32, (length, 1), 0) < ids.length(slot)
        datt = dot_nt(grads[:length, :], out_w[kind]).astype(BF16)
        queries, keys, values = [], [], []
        for probs, c in key_major(qkv, width, keep):
            query = qkv[:, c : c + HEAD_DIM]
            key = qkv[:, width + c : width + c + HEAD_DIM]
            da = datt[:, c : c + HEAD_DIM]
            dprobs = dot_nt(qkv[:, 2 * width + c : 2 * width + c + HEAD_DIM], da)
            dscores = (probs * (dprobs - jnp.sum(probs * dprobs, axis=0, keepdims=True))).astype(BF16)
            queries.append(dot_tn(dscores, key) * SCALE)
            keys.append(dot(dscores, query) * SCALE)
            values.append(dot(probs.astype(BF16), da))
        dqkv[...] = jnp.concatenate(queries + keys + values, axis=1).astype(BF16)
        part[...] = dot(dqkv[...], qkv_w[kind]).astype(BF16)

    outs = (arr((length, dims.d)), arr((length, 3 * width)))
    return run(f"attn_bwd{layer}_{slot}", body, meta, (grads, qkv, weight), outs)


def typed_sum(ids, left, right, kind, slots):
    chosen = [
        jnp.where(ids.kind(k) == kind, right[k], jnp.zeros_like(right[k])) for k in range(slots)
    ]
    return dot_tn(jnp.concatenate(left, axis=0), jnp.concatenate(chosen, axis=0))


def halved(value):
    high = value.astype(BF16)
    return high, (value - high.astype(F32)).astype(BF16)


def carried(ids, blocks, slots, r):
    found = []
    for kind in range(TYPES):
        total = jnp.zeros((3, blocks[0].shape[1]), F32)
        for k in range(slots):
            tail = blocks[k][r : r + TAIL, :].astype(F32)
            total = total + jnp.where(ids.kind(k) == kind, tail[0:3] + tail[3:6], 0.0)
        found.append(total)
    return jnp.concatenate(found, axis=0)


def row_sums(ids, slots, rows):
    found = []
    for kind in range(TYPES):
        total = 0.0
        for k in range(slots):
            here = jnp.sum(rows[k].astype(F32), axis=0, keepdims=True)
            total = total + jnp.where(ids.kind(k) == kind, here, 0.0)
        found.append(total)
    return jnp.concatenate(found, axis=0)


def attention_weights(dims, layer, meta, rows, dqkv, grads, att, below):
    length, slots, width, d = dims.length, dims.slots, dims.width, dims.d

    def body(meta_ref, ins, outs):
        rows, dqkv, grads, att, below = ins
        ids = Ids(meta_ref, dims)
        left = [ref[...] for ref in rows]
        back = [ref[:length, :] for ref in grads]
        right = [ref[...] for ref in dqkv]
        heads = [ref[...] for ref in att]
        for kind in range(TYPES):
            span = slice(kind * d, (kind + 1) * d)
            outs[span, : 3 * width] = typed_sum(ids, left, right, kind, slots).astype(BF16)
            outs[span, 3 * width :] = typed_sum(ids, back, heads, kind, slots).astype(BF16)
        qkv_rows = row_sums(ids, slots, right)
        qkv_rows = jnp.concatenate([qkv_rows, jnp.zeros((TYPES, width), F32)], axis=1)
        firsts = carried(ids, grads, slots, length)
        small = jnp.concatenate([firsts, below[:6, :], qkv_rows, below[6:8, :]], axis=0)
        outs[TYPES * d : TYPES * d + SMALL, :], outs[TYPES * d + SMALL :, :] = halved(small)

    out = arr((TYPES * d + 2 * SMALL, d))
    return run(f"attn_dw{layer}", body, meta, (rows, dqkv, grads, att, below), out, 8)


def ffn_weights(dims, layer, meta, rows, dpre, grads, act):
    length, slots, hidden, d = dims.length, dims.slots, dims.hidden, dims.d

    def body(meta_ref, ins, outs):
        rows, dpre, grads, act = ins
        total, small = outs
        ids = Ids(meta_ref, dims)
        for step, (left, right) in enumerate(((rows, dpre), (grads, act))):
            left_rows = [ref[:length, :] for ref in left]
            right_rows = [ref[...] for ref in right]
            for kind in range(TYPES):
                first = (TYPES * step + kind) * d
                total[first : first + d, :] = typed_sum(ids, left_rows, right_rows, kind, slots).astype(BF16)
        small[0:6, :] = carried(ids, grads, slots, length)
        small[6:8, :] = row_sums(ids, slots, [ref[...] for ref in dpre])

    outs = (arr((2 * TYPES * d, hidden)), arr((8, hidden), F32))
    return run(f"ffn_dw{layer}", body, meta, (rows, dpre, grads, act), outs, 8)


def ffn_forward(dims, layer, meta, slot, rows, weight, small):
    length, hidden = dims.length, dims.hidden

    def body(meta_ref, ins, outs):
        rows, (in_w, back_w), small = ins
        part, act, slope = outs
        kind = Ids(meta_ref, dims).kind(slot)
        pre = dot(rows[...], in_w[kind]) + small[pl.ds(IN_B + kind, 1), :hidden]
        gate = 0.5 * (1.0 + lax.erf(pre * HALF_ROOT))
        act[...] = (pre * gate).astype(BF16)
        slope[...] = (gate + pre * (DENSITY * jnp.exp(-0.5 * pre * pre))).astype(BF16)
        part[...] = dot(act[...], back_w[kind]).astype(BF16)

    outs = (arr((length, dims.d)), arr((length, hidden)), arr((length, hidden)))
    return run(f"ffn_fwd{layer}_{slot}", body, meta, (rows, weight, small), outs)


def ffn_backward(dims, layer, meta, slot, grads, slope, weight):
    length, hidden = dims.length, dims.hidden

    def body(meta_ref, ins, outs):
        grads, slope, (in_w, back_w) = ins
        part, dpre = outs
        kind = Ids(meta_ref, dims).kind(slot)
        dact = dot_nt(grads[:length, :], back_w[kind])
        dpre[...] = (dact * slope[...].astype(F32)).astype(BF16)
        part[...] = dot_nt(dpre[...], in_w[kind]).astype(BF16)

    outs = (arr((length, dims.d)), arr((length, hidden)))
    return run(f"ffn_bwd{layer}_{slot}", body, meta, (grads, slope, weight), outs)


def normalized(values):
    center = values - jnp.mean(values, axis=-1, keepdims=True)
    inv = lax.rsqrt(jnp.mean(center * center, axis=-1, keepdims=True) + EPS)
    return center * inv, inv


def summed(parts):
    total = parts[0][...].astype(F32)
    for part in parts[1:]:
        total = total + part[...].astype(F32)
    return total


def norm_back(grad, normal, inv, gain):
    scaled = grad * gain
    return inv * (
        scaled
        - jnp.mean(scaled, axis=-1, keepdims=True)
        - normal * jnp.mean(scaled * normal, axis=-1, keepdims=True)
    )


def with_sums(low, value, sums):
    r = value.shape[0]
    low[:r, :] = value.astype(BF16)
    total = jnp.concatenate([jnp.sum(v, axis=0, keepdims=True) for v in sums], axis=0)
    high, rest = halved(total)
    blank = jnp.zeros((TAIL - 6, value.shape[1]), BF16)
    low[r:, :] = jnp.concatenate([high, rest, blank], axis=0)


def first_norm(dims, layer, meta, own_rows, parts, small):
    r, d = dims.length, dims.d

    def body(meta_ref, ins, outs):
        own_rows, parts, small = ins
        low, normal, inv = outs
        kind = Ids(meta_ref, dims).kind(0)
        mixed = own_rows[...].astype(F32) + summed(parts) + small[pl.ds(OUT_B + kind, 1), :]
        xhat, scale = normalized(mixed)
        normal[...] = xhat
        inv[...] = jnp.broadcast_to(scale, inv.shape)
        low[...] = (xhat * small[pl.ds(GAIN1 + kind, 1), :] + small[pl.ds(SHIFT1 + kind, 1), :]).astype(BF16)

    outs = (arr((r, d)), arr((r, d), F32), arr((r, 128), F32))
    return run(f"norm1_{layer}", body, meta, (own_rows, parts, small), outs)


def second_values(kind, normal, parts, small):
    normed = normal[...] * small[pl.ds(GAIN1 + kind, 1), :] + small[pl.ds(SHIFT1 + kind, 1), :]
    xhat, scale = normalized(normed + summed(parts) + small[pl.ds(BACK_B + kind, 1), :])
    output = xhat * small[pl.ds(GAIN2 + kind, 1), :] + small[pl.ds(SHIFT2 + kind, 1), :]
    return xhat, scale, output.astype(BF16)


def second_norm(dims, layer, meta, normal, parts, small):
    r, d = dims.length, dims.d

    def body(meta_ref, ins, outs):
        normal, parts, small = ins
        low, xhat_ref, inv = outs
        kind = Ids(meta_ref, dims).kind(0)
        xhat, scale, low[...] = second_values(kind, normal, parts, small)
        xhat_ref[...] = xhat
        inv[...] = jnp.broadcast_to(scale, inv.shape)

    outs = (arr((r, d)), arr((r, d), F32), arr((r, 128), F32))
    return run(f"norm2_{layer}", body, meta, (normal, parts, small), outs)


def second_back(kind, grad, xhat, scale, small, second_grad, low):
    value = norm_back(grad, xhat, scale, small[pl.ds(GAIN2 + kind, 1), :])
    second_grad[...] = value
    with_sums(low, value, (grad * xhat, grad, value))


def last_norm(dims, layer, meta, normal, parts, small, cotangent):
    r, d = dims.length, dims.d

    def body(meta_ref, ins, outs):
        normal, parts, small, cotangent = ins
        act, second_grad, low = outs
        ids = Ids(meta_ref, dims)
        kind = ids.kind(0)
        xhat, scale, act[...] = second_values(kind, normal, parts, small)
        grad = cotangent[ids.section].astype(F32)
        second_back(kind, grad, xhat, scale, small, second_grad, low)

    outs = (arr((r, d)), arr((r, d), F32), arr((r + TAIL, d)))
    return run(f"norm2_{layer}", body, meta, (normal, parts, small, cotangent), outs)


def between_layers(dims, layer, meta, parts, first_grad, xhat, inv, small):
    r, d = dims.length, dims.d

    def body(meta_ref, ins, outs):
        parts, first_grad, xhat, inv, small = ins
        input_grad, second_grad, low = outs
        kind = Ids(meta_ref, dims).kind(0)
        value = summed(parts) + first_grad[...]
        input_grad[...] = value
        grad = value.astype(BF16).astype(F32)
        second_back(kind, grad, xhat[...], inv[:, :1], small, second_grad, low)

    outs = (arr((r, d), F32), arr((r, d), F32), arr((r + TAIL, d)))
    return run(f"between{layer}", body, meta, (parts, first_grad, xhat, inv, small), outs)


def first_back(dims, layer, meta, parts, second_grad, xhat, inv, small):
    r, d = dims.length, dims.d

    def body(meta_ref, ins, outs):
        parts, second_grad, xhat, inv, small = ins
        first_grad, low = outs
        kind = Ids(meta_ref, dims).kind(0)
        grad = summed(parts) + second_grad[...]
        value = norm_back(grad, xhat[...], inv[:, :1], small[pl.ds(GAIN1 + kind, 1), :])
        first_grad[...] = value
        with_sums(low, value, (grad * xhat[...], grad, value))

    outs = (arr((r, d), F32), arr((r + TAIL, d)))
    return run(f"norm1_back{layer}", body, meta, (parts, second_grad, xhat, inv, small), outs)


def input_gradient(dims, layer, meta, parts, first_grad):
    def body(meta_ref, ins, outs):
        parts, first_grad = ins
        outs[...] = summed(parts) + first_grad[...]

    return run(f"input_grad{layer}", body, meta, (parts, first_grad), arr((dims.length, dims.d), F32))


def swap(value, axis, bit):
    count = lax.axis_size(axis)
    return lax.ppermute(value, axis, [(source, source ^ bit) for source in range(count)])


def gather(value, slots):
    return [value] + [swap(value, "tensor", k) for k in range(1, slots)]


def scatter(parts):
    return [parts[0]] + [swap(part, "tensor", k) for k, part in enumerate(parts) if k]


def tied(*values):
    return lax.optimization_barrier(values)


class GradSum:
    def __init__(self, dims, layer, meta, names, small):
        self.dims, self.layer, self.meta, self.names = dims, layer, meta, [f"{name}{layer}" for name in names]
        self.name, self.small, self.pieces = "_".join(self.names), small, [None] * len(names)

    def start(self, value):
        self.value = value
        self.d, self.cols = self.dims.d, value.shape[1]
        self.count = value.shape[0] // self.d
        self.rows = self.d // self.dims.dp
        self.extra = 2 * SMALL if self.small else 0
        self.pad = 0 if self.small else PAD
        self.other = lax.ppermute(value, "section", [(1 - self.layer, self.layer)])

    def permute(self, value, bit):
        base = self.layer * self.dims.dp
        pairs = [(base + z, base + (z ^ bit)) for z in range(self.dims.dp)]
        return lax.ppermute(value, ("section", "dp"), pairs)

    def whole(self, ref, base):
        return ref[base : base + SMALL, :].astype(F32) + ref[base + SMALL : base + 2 * SMALL, :].astype(F32)

    def near_sum(self):
        dims, rows, count, cols, d = self.dims, self.rows, self.count, self.cols, self.d
        if dims.dp != 4:
            both = self.value.astype(F32) + self.other.astype(F32)
            if self.small:
                low = both[count * d :]
                self.total_small = lax.psum(low[:SMALL] + low[SMALL:], "dp")
            return both[: count * d].reshape(count, d, cols).astype(BF16)
        base = 2 * count * rows

        def body(meta_ref, ins, outs):
            value, other = ins
            sent, kept = outs
            odd = lax.rem(Ids(meta_ref, dims).dp, 2)

            def part(index, chunk):
                start = pl.multiple_of(index * d + chunk * rows, 16)
                return value[pl.ds(start, rows), :].astype(F32) + other[pl.ds(start, rows), :].astype(F32)

            for i in range(2):
                for index in range(count):
                    at = (i * count + index) * rows
                    sent[at : at + rows, :] = part(index, 2 * i + 1 - odd).astype(BF16)
                    kept[at : at + rows, :] = part(index, 2 * i + odd)
            if self.pad:
                sent[base:, :] = jnp.zeros((self.pad, cols), BF16)
            if self.small:
                total = self.whole(value, count * d) + self.whole(other, count * d)
                sent[base : base + SMALL, :], sent[base + SMALL : base + 2 * SMALL, :] = halved(total)
                kept[base:, :] = total

        outs = (arr((base + self.extra + self.pad, cols)), arr((base + self.extra // 2, cols), F32))
        sent, self.kept = run(f"{self.name}_a", body, self.meta, (self.value, self.other), outs)
        return sent

    def near_send(self, sent):
        if self.dims.dp != 4:
            whole = lax.psum_scatter(sent, "dp", scatter_dimension=1, tiled=True)
            each = self.count // len(self.pieces)
            for i in range(len(self.pieces)):
                self.pieces[i] = [whole[each * i : each * (i + 1)]] + ([self.total_small] if self.small else [])
        else:
            self.near = self.permute(sent, 1)

    def far_sum(self):
        dims, cols, size = self.dims, self.cols, self.count // len(self.names) * self.rows
        if dims.dp != 4:
            return [None] * len(self.names)

        def body(meta_ref, ins, outs):
            kept, near = ins
            mine = lax.div(Ids(meta_ref, dims).dp, 2)
            block = self.count * self.rows

            def half(i, piece):
                span = pl.ds(pl.multiple_of(i * block + piece * size, 16), size)
                return kept[span, :] + near[span, :].astype(F32)

            for piece, (sent, final) in enumerate(outs):
                sent[:size, :] = half(1 - mine, piece).astype(BF16)
                final[:size, :] = half(mine, piece)
                if self.small:
                    total = kept[2 * block :, :] + self.whole(near, 2 * block)
                    sent[size : size + SMALL, :], sent[size + SMALL :, :] = halved(total)
                    final[size:, :] = total

        out = (arr((size + self.extra, cols)), arr((size + self.extra // 2, cols), F32))
        outs = run(f"{self.name}_b", body, self.meta, (self.kept, self.near), [out] * len(self.names))
        self.final = [final for _, final in outs]
        return [sent for sent, _ in outs]

    def far_send(self, sent, piece):
        if self.dims.dp == 4:
            self.pieces[piece] = [self.final[piece], self.permute(sent[piece], 2)]

    def finish(self, piece, shapes, put, before=None):
        each = self.count // len(self.names)
        dims, rows, size = self.dims, self.rows, each * self.rows
        pieces = self.pieces[piece]
        flat = len(pieces)

        def body(meta_ref, ins, outs, *scratch):
            pieces, values, sems = ins[0], scratch[:-1], scratch[-1]

            def total(kind):
                if dims.dp != 4:
                    return pieces[0][kind].astype(F32)
                span = slice(kind * rows, (kind + 1) * rows)
                return pieces[0][span, :] + pieces[1][span, :].astype(F32)

            @pl.when(Ids(meta_ref, dims).section == self.layer)
            def _():
                small = None
                if self.small:
                    small = pieces[0][size:, :] + self.whole(pieces[1], size) if dims.dp == 4 else pieces[1][...]
                put(values, [total(index) for index in range(each)], small)
                for copy in copies(list(zip(values, outs)), sems):
                    copy.wait()

        outs = [InHbm(arr(shape, F32)) for shape in shapes]
        ins = [pieces] + ([] if before is None else [InHbm(a) for a in before])
        aliases = {} if before is None else {flat + i: i for i in range(len(shapes))}
        scratch = [pltpu.VMEM(shape, F32) for shape in shapes] + [pltpu.SemaphoreType.DMA((len(shapes),))]
        return run(f"{self.names[piece]}_end", body, self.meta, ins, outs, 8, scratch, aliases)


def pack_params(dims, meta, arrays):
    width = dims.width

    def body(meta_ref, ins, outs, *scratch):
        for copy in copies(list(zip(ins, scratch[:-1])), scratch[-1]):
            copy.wait()
        out_b, back_b, gains, shifts, in_b, qkv_b = scratch[:-1]
        for t in range(TYPES):
            for row, ref in ((OUT_B, out_b), (BACK_B, back_b), (IN_B, in_b)):
                outs[row + t : row + t + 1, :] = ref[0, t : t + 1, :]
            for row, ref in ((GAIN1, gains), (SHIFT1, shifts)):
                for norm in range(2):
                    outs[row + 2 * norm + t : row + 2 * norm + t + 1, :] = ref[0, t, norm : norm + 1, :]
            outs[QKV_B + t : QKV_B + t + 1, :] = jnp.zeros((1, dims.d), F32)
            outs[QKV_B + t : QKV_B + t + 1, :width] = qkv_b[0, t, 0:1, :]
            outs[QKV_B + t : QKV_B + t + 1, 2 * width : 3 * width] = qkv_b[0, t, 1:2, :]

    scratch = [pltpu.VMEM(a.shape, F32) for a in arrays] + [pltpu.SemaphoreType.DMA((len(arrays),))]
    return run("pack", body, meta, [InHbm(a) for a in arrays], arr((16, dims.d), F32), scratch=scratch)


def order_params(dims, meta, own, other):
    def body(meta_ref, ins, outs):
        here = meta_ref[0] == 0
        own, other = ins[0][...], ins[1][...]
        outs[0][...] = jnp.where(here, own, other)
        outs[1][...] = jnp.where(here, other, own)

    return run("params", body, meta, [own, other], [arr(own.shape, F32)] * 2)


def both_chains(dims, meta, own, moved, name):
    def body(meta_ref, ins, outs):
        own, moved = ins
        first = meta_ref[0] == 0

        @pl.when(first)
        def _():
            outs[0, 0] = own[0][...]
            outs[0, 1] = moved[0][...]

        @pl.when(jnp.logical_not(first))
        def _():
            outs[0, 0] = moved[1][...]
            outs[0, 1] = own[1][...]

    return run(name, body, meta, (own, moved), arr((1, 2, dims.length, dims.d), own[0].dtype), 8)


def body(
    tokens,
    cotangent,
    lengths,
    chain_type,
    qkv_weight,
    qkv_bias,
    out_weight,
    out_bias,
    ffn_in,
    ffn_in_bias,
    ffn_out,
    ffn_out_bias,
    norm_gain,
    norm_bias,
):
    dims = Dims()
    dims.per_chip, dims.length, dims.d = tokens.shape
    dims.slots = lax.axis_size("tensor")
    dims.dp = lax.axis_size("dp")
    dims.group = lengths.shape[0]
    dims.width = qkv_weight.shape[-1]
    dims.hidden = ffn_in.shape[-1]
    sections = lax.axis_size("section")
    assert dims.per_chip == sections == LAYERS and dims.slots & (dims.slots - 1) == 0
    assert dims.dp & (dims.dp - 1) == 0 and 4 * dims.width == dims.d == dims.hidden
    d, width, slots = dims.d, dims.width, dims.slots
    each = range(slots)
    section = lax.axis_index("section")
    meta = jnp.concatenate(
        [
            jnp.stack([section, lax.axis_index("tensor"), lax.axis_index("dp")]).astype(jnp.int32),
            chain_type,
            lengths,
        ]
    )

    own_rows = jnp.where(section == 0, tokens[0], tokens[1])
    rows = gather(own_rows, slots)

    qkv_own = qkv_weight[0].transpose(0, 2, 3, 1).reshape(TYPES, 3 * width, d)
    attn_own = [qkv_own, out_weight[0]]
    attn_other = [swap(w, "section", 1) for w in attn_own]
    biases = [qkv_bias, swap(qkv_bias, "section", 1)]
    packed = pack_params(
        dims, meta, (out_bias, ffn_out_bias, norm_gain, norm_bias, ffn_in_bias, qkv_bias)
    )
    small = order_params(dims, meta, packed, swap(packed, "section", 1))
    ffn_own = [ffn_in[0], ffn_out[0]]
    rows[0], small = tied(rows[0], small)

    def moved(value, layer):
        return lax.ppermute(value, "section", [(1 - layer, layer)])

    saved = []
    acts = []
    for layer in range(LAYERS):
        weight = fetch(dims, layer, meta, attn_own, attn_other, "attn")
        attn = [attention_forward(dims, layer, meta, k, rows[k], weight, biases) for k in each]
        parts, qkv, att = ([a[i] for a in attn] for i in range(3))
        parts = scatter(parts)
        if layer == 0:
            parts, ffn_sent = tied(parts, ffn_own)
            ffn_other = [swap(w, "section", 1) for w in ffn_sent]
        first = first_norm(dims, layer, meta, own_rows, parts, small[layer])
        normed = gather(first[0], slots)
        weight = fetch(dims, layer, meta, ffn_own, ffn_other, "ffn")
        ffn = [ffn_forward(dims, layer, meta, k, normed[k], weight, small[layer]) for k in each]
        parts, act, slope = ([f[i] for f in ffn] for i in range(3))
        parts = scatter(parts)
        if layer < LAYERS - 1:
            second = second_norm(dims, layer, meta, first[1], parts, small[layer])
        else:
            second = last_norm(dims, layer, meta, first[1], parts, small[layer], cotangent)
        saved.append((rows, qkv, att, first, normed, act, slope, second))
        own_rows = second[0]
        acts.append(own_rows)
        if layer < LAYERS - 1:
            rows = gather(own_rows, slots)

    share = d // dims.dp
    ffn_shapes = [(TYPES, share, dims.hidden)]
    attn_shapes = [
        (TYPES, 3, share, width),
        (TYPES, width, share),
        (1, TYPES, 2, width),
        (1, TYPES, d),
        (1, TYPES, dims.hidden),
        (1, TYPES, d),
        (1, TYPES, 2, d),
        (1, TYPES, 2, d),
    ]

    def put_ffn(outs, totals, small):
        for index, total in enumerate(totals):
            outs[index // TYPES][index % TYPES] = total

    def put_attn(outs, totals, small):
        qkv_out, out_out, qkv_b, out_b, in_b, back_b, gains, shifts = outs
        for kind, total in enumerate(totals):
            for i in range(3):
                qkv_out[kind, i] = total[:, i * width : (i + 1) * width]
            out_out[kind] = total[:, 3 * width :].T
            qkv_b[0, kind, 0:1, :] = small[QKV_SUMS + kind : QKV_SUMS + kind + 1, :width]
            qkv_b[0, kind, 1:2, :] = small[QKV_SUMS + kind : QKV_SUMS + kind + 1, 2 * width : 3 * width]
            in_b[0, kind : kind + 1, :] = small[IN_SUMS + kind : IN_SUMS + kind + 1, :]
            for norm, (base, bias) in enumerate(((FIRST_SUMS, out_b), (SECOND_SUMS, back_b))):
                row = base + 3 * kind
                gains[0, kind, norm : norm + 1, :] = small[row : row + 1, :]
                shifts[0, kind, norm : norm + 1, :] = small[row + 1 : row + 2, :]
                bias[0, kind : kind + 1, :] = small[row + 2 : row + 3, :]

    second_grad, low = second[1:]
    input_grads = [None] * LAYERS
    ffn_sums = [GradSum(dims, layer, meta, ("in", "back") if layer else ("ffn",), False) for layer in range(LAYERS)]
    attn_sums = [GradSum(dims, layer, meta, ("attn",), True) for layer in range(LAYERS)]
    for layer in reversed(range(LAYERS)):
        rows, qkv, att, first, normed, act, slope, second = saved[layer]
        top = layer == LAYERS - 1
        grads = gather(low, slots)
        weight = fetch(dims, layer, meta, ffn_own, ffn_other, "ffn_back")
        if top:
            acts_moved = [moved(acts[i], i) for i in range(LAYERS)]
        else:
            ffn_up, attn_up = ffn_sums[layer + 1], attn_sums[layer + 1]
            grads, near, ffn_up.pieces[1], ffn_far = tied(
                grads, attn_up.near_sum(), ffn_up.pieces[1], ffn_far
            )
            attn_sums[layer + 1].near_send(near)
            ffn_sums[layer + 1].far_send(ffn_far, 0)
        back = [ffn_backward(dims, layer, meta, k, grads[k], slope[k], weight) for k in each]
        parts, dpre = ([b[i] for b in back] for i in range(2))
        parts = scatter(parts)
        ffn_grad, below = ffn_weights(dims, layer, meta, normed, dpre, grads, act)
        if top:
            acts_out = both_chains(dims, meta, acts, acts_moved, "acts_out")
            parts, ffn_grad, acts_out = tied(parts, ffn_grad, acts_out)
        else:
            far = attn_up.far_sum()
            parts, ffn_grad, far, ffn_up.pieces[0] = tied(parts, ffn_grad, far, ffn_up.pieces[0])
            attn_sums[layer + 1].far_send(far, 0)
        ffn_sums[layer].start(ffn_grad)
        first_grad, low = first_back(
            dims, layer, meta, parts, second_grad, first[1], first[2], small[layer]
        )
        grads = gather(low, slots)
        weight = fetch(dims, layer, meta, attn_own, attn_other, "attn_back")
        near = ffn_sums[layer].near_sum()
        grads, _ = tied(grads, near)
        ffn_sums[layer].near_send(near)
        back = [attention_backward(dims, layer, meta, k, grads[k], qkv[k], weight) for k in each]
        parts, dqkv = ([b[i] for b in back] for i in range(2))
        parts = scatter(parts)
        if not top:
            dqkv, attn_up.pieces[0] = tied(dqkv, attn_up.pieces[0])
        attn_grad = attention_weights(dims, layer, meta, rows, dqkv, grads, att, below)
        if top:
            parts, attn_grad, ffn_far = tied(parts, attn_grad, ffn_sums[layer].far_sum())
            ffn_sums[layer].far_send(ffn_far, 1)
        attn_sums[layer].start(attn_grad)
        if layer > 0:
            second = saved[layer - 1][-1]
            input_grads[layer], second_grad, low = between_layers(
                dims, layer, meta, parts, first_grad, second[1], second[2], small[layer - 1]
            )
        else:
            input_grads[layer] = input_gradient(dims, layer, meta, parts, first_grad)

    back_done = ffn_up.finish(1, ffn_shapes, put_ffn)
    in_done = ffn_up.finish(0, ffn_shapes, put_ffn)
    attn_done = attn_up.finish(0, attn_shapes, put_attn)
    ffn_far = ffn_sums[0].far_sum()
    attn_sums[0].other, _ = tied(attn_sums[0].other, ffn_far)
    ffn_sums[0].far_send(ffn_far, 0)
    attn_sums[0].near_send(attn_sums[0].near_sum())
    attn_sums[0].far_send(attn_sums[0].far_sum(), 0)
    in_total, back_total = ffn_sums[0].finish(0, ffn_shapes * 2, put_ffn, in_done + back_done)
    grads_moved = [moved(input_grads[layer], layer) for layer in range(LAYERS)]
    grads_out = both_chains(dims, meta, input_grads, grads_moved, "grads_out")
    qkv_total, out_total, *small_grads = attn_sums[0].finish(0, attn_shapes, put_attn, attn_done)
    qkv_bias_out, out_bias_out, in_bias_out, back_bias_out, gain_out, shift_out = small_grads
    return (
        acts_out,
        grads_out,
        qkv_total.transpose(0, 2, 1, 3)[None],
        qkv_bias_out,
        out_total[None],
        out_bias_out,
        in_total[None],
        in_bias_out,
        back_total.transpose(0, 2, 1)[None],
        back_bias_out,
        gain_out,
        shift_out,
    )


def solution(mesh):
    placed = (
        P(("dp", "tensor"), None, None),
        P(("dp", "tensor"), None, None),
        P("dp"),
        P("dp"),
        P("section", None, None, None, "tensor"),
        P("section", None, None, "tensor"),
        P("section", None, "tensor", None),
        P("section", None, None),
        P("section", None, None, "tensor"),
        P("section", None, "tensor"),
        P("section", None, "tensor", None),
        P("section", None, None),
        P("section", None, None, None),
        P("section", None, None, None),
    )
    return jax.shard_map(
        body,
        mesh=mesh,
        in_specs=placed,
        out_specs=(
            P("section", ("dp", "tensor"), None, None),
            P("section", ("dp", "tensor"), None, None),
            P("section", None, "dp", None, "tensor"),
            P("section", None, None, "tensor"),
            P("section", None, "tensor", "dp"),
            P("section", None, None),
            P("section", None, "dp", "tensor"),
            P("section", None, "tensor"),
            P("section", None, "tensor", "dp"),
            P("section", None, None),
            P("section", None, None, None),
            P("section", None, None, None),
        ),
        check_vma=False,
    )
```

```python
import functools
import math

import jax
import jax.numpy as jnp
from jax import lax
from jax.experimental import pallas as pl
from jax.experimental.pallas import tpu as pltpu
from jax.sharding import PartitionSpec as P

HEAD_DIM = 64
TYPES = 2
LAYERS = 2
EPS = 1e-06
HALF_ROOT = 0.7071067811865476
DENSITY = 0.3989422804014327
SCALE = 1.0 / math.sqrt(HEAD_DIM)
MIB = 1 << 20

F32 = jnp.float32
BF16 = jnp.bfloat16

TAIL = 16
PAD = 64
FIRST_SUMS, SECOND_SUMS, QKV_SUMS, IN_SUMS, SMALL = 0, 6, 12, 14, 16

OUT_B, BACK_B, GAIN1, GAIN2, SHIFT1, SHIFT2, IN_B, QKV_B = range(0, 16, 2)


def dot(a, b):
    return jnp.dot(a, b, preferred_element_type=F32)


def dot_nt(a, b):
    return lax.dot_general(a, b, (((1,), (1,)), ((), ())), preferred_element_type=F32)


def dot_tn(a, b):
    return lax.dot_general(a, b, (((0,), (0,)), ((), ())), preferred_element_type=F32)


def nested(structure, flat):
    leaves, tree = jax.tree.flatten(structure)
    return jax.tree.unflatten(tree, flat)


class InHbm:
    def __init__(self, value):
        self.value = value


def run(name, body, meta, ins, outs, limit=6, scratch=(), aliases=None):
    flat_in, flat_out = jax.tree.leaves(ins), jax.tree.leaves(outs)

    def kernel(meta_ref, *refs):
        into = len(flat_in) + len(flat_out)
        body(meta_ref, nested(ins, refs[: len(flat_in)]), nested(outs, refs[len(flat_in) : into]), *refs[into:])

    def spec(leaf):
        return pl.BlockSpec(memory_space=pltpu.HBM if isinstance(leaf, InHbm) else pltpu.VMEM)

    def plain(leaf):
        return leaf.value if isinstance(leaf, InHbm) else leaf

    results = pl.pallas_call(
        kernel,
        name=name,
        in_specs=[pl.BlockSpec(memory_space=pltpu.SMEM)] + [spec(a) for a in flat_in],
        out_specs=[spec(a) for a in flat_out],
        out_shape=[plain(a) for a in flat_out],
        scratch_shapes=list(scratch),
        input_output_aliases={1 + i: o for i, o in (aliases or {}).items()},
        compiler_params=pltpu.CompilerParams(vmem_limit_bytes=limit * MIB),
        cost_estimate=pl.CostEstimate(flops=1, bytes_accessed=1, transcendentals=0),
    )(meta, *[plain(a) for a in flat_in])
    return nested(outs, results)


def arr(shape, dtype=BF16):
    return jax.ShapeDtypeStruct(tuple(shape), dtype)


class Ids:
    def __init__(self, meta, dims):
        self.meta, self.dims = meta, dims
        self.section, self.tensor, self.dp = meta[0], meta[1], meta[2]

    def chain(self, slot):
        return (self.tensor ^ slot) * self.dims.per_chip + self.section

    def kind(self, slot):
        return self.meta[3 + self.chain(slot)]

    def length(self, slot):
        return self.meta[3 + self.dims.group + self.chain(slot)]


def copies(pairs, sems):
    started = [pltpu.make_async_copy(source, target, sems.at[i]) for i, (source, target) in enumerate(pairs)]
    for copy in started:
        copy.start()
    return started


def fetch(dims, layer, meta, own, other, name):
    def body(meta_ref, ins, outs, sems):
        own, other = ins
        ids = Ids(meta_ref, dims)

        def go(source):
            for copy in copies(list(zip(source, outs)), sems):
                copy.wait()

        pl.when(ids.section == layer)(lambda: go(own))
        pl.when(ids.section != layer)(lambda: go(other))

    ins = ([InHbm(w) for w in own], [InHbm(w) for w in other])
    outs = [arr(w.shape, w.dtype) for w in own]
    return run(f"fetch_{name}{layer}", body, meta, ins, outs, scratch=[pltpu.SemaphoreType.DMA((len(own),))])


class Dims:
    pass


def key_major(qkv, width, keep):
    found = []
    for c in range(0, width, HEAD_DIM):
        scores = dot_nt(qkv[:, width + c : width + c + HEAD_DIM], qkv[:, c : c + HEAD_DIM]) * SCALE
        scores = jnp.where(keep, scores, -1e9)
        expd = jnp.exp(scores - jnp.max(scores, axis=0, keepdims=True))
        found.append((expd * (1.0 / jnp.sum(expd, axis=0, keepdims=True)), c))
    return found


def attention_forward(dims, layer, meta, slot, rows, weight, biases):
    length, width = dims.length, dims.width

    def body(meta_ref, ins, outs):
        rows, (qkv_w, out_w), biases = ins
        part, qkv, att = outs
        ids = Ids(meta_ref, dims)
        kind = ids.kind(slot)
        here = ids.section == layer
        parts = [jnp.where(here, biases[0][0, kind, i : i + 1, :], biases[1][0, kind, i : i + 1, :]) for i in range(2)]
        bias = jnp.concatenate([parts[0], jnp.zeros_like(parts[0]), parts[1]], axis=1)
        qkv[...] = (dot_nt(rows[...], qkv_w[kind]) + bias).astype(BF16)
        keep = lax.broadcasted_iota(jnp.int32, (length, 1), 0) < ids.length(slot)
        heads = []
        for probs, c in key_major(qkv, width, keep):
            value = qkv[:, 2 * width + c : 2 * width + c + HEAD_DIM]
            heads.append(dot_tn(probs.astype(BF16), value))
        att[...] = jnp.concatenate(heads, axis=1).astype(BF16)
        part[...] = dot(att[...], out_w[kind]).astype(BF16)

    outs = (arr((length, dims.d)), arr((length, 3 * width)), arr((length, width)))
    return run(f"attn_fwd{layer}_{slot}", body, meta, (rows, weight, biases), outs)


def attention_backward(dims, layer, meta, slot, grads, qkv, weight):
    length, width = dims.length, dims.width

    def body(meta_ref, ins, outs):
        grads, qkv, (qkv_w, out_w) = ins
        part, dqkv = outs
        ids = Ids(meta_ref, dims)
        kind = ids.kind(slot)
        keep = lax.broadcasted_iota(jnp.int32, (length, 1), 0) < ids.length(slot)
        datt = dot_nt(grads[:length, :], out_w[kind]).astype(BF16)
        queries, keys, values = [], [], []
        for probs, c in key_major(qkv, width, keep):
            query = qkv[:, c : c + HEAD_DIM]
            key = qkv[:, width + c : width + c + HEAD_DIM]
            da = datt[:, c : c + HEAD_DIM]
            dprobs = dot_nt(qkv[:, 2 * width + c : 2 * width + c + HEAD_DIM], da)
            dscores = (probs * (dprobs - jnp.sum(probs * dprobs, axis=0, keepdims=True))).astype(BF16)
            queries.append(dot_tn(dscores, key) * SCALE)
            keys.append(dot(dscores, query) * SCALE)
            values.append(dot(probs.astype(BF16), da))
        dqkv[...] = jnp.concatenate(queries + keys + values, axis=1).astype(BF16)
        part[...] = dot(dqkv[...], qkv_w[kind]).astype(BF16)

    outs = (arr((length, dims.d)), arr((length, 3 * width)))
    return run(f"attn_bwd{layer}_{slot}", body, meta, (grads, qkv, weight), outs)


def typed_sum(ids, left, right, kind, slots):
    chosen = [
        jnp.where(ids.kind(k) == kind, right[k], jnp.zeros_like(right[k])) for k in range(slots)
    ]
    return dot_tn(jnp.concatenate(left, axis=0), jnp.concatenate(chosen, axis=0))


def halved(value):
    high = value.astype(BF16)
    return high, (value - high.astype(F32)).astype(BF16)


def carried(ids, blocks, slots, r):
    found = []
    for kind in range(TYPES):
        total = jnp.zeros((3, blocks[0].shape[1]), F32)
        for k in range(slots):
            tail = blocks[k][r : r + TAIL, :].astype(F32)
            total = total + jnp.where(ids.kind(k) == kind, tail[0:3] + tail[3:6], 0.0)
        found.append(total)
    return jnp.concatenate(found, axis=0)


def row_sums(ids, slots, rows):
    found = []
    for kind in range(TYPES):
        total = 0.0
        for k in range(slots):
            here = jnp.sum(rows[k].astype(F32), axis=0, keepdims=True)
            total = total + jnp.where(ids.kind(k) == kind, here, 0.0)
        found.append(total)
    return jnp.concatenate(found, axis=0)


def attention_weights(dims, layer, meta, rows, dqkv, grads, att, below):
    length, slots, width, d = dims.length, dims.slots, dims.width, dims.d

    def body(meta_ref, ins, outs):
        rows, dqkv, grads, att, below = ins
        ids = Ids(meta_ref, dims)
        left = [ref[...] for ref in rows]
        back = [ref[:length, :] for ref in grads]
        right = [ref[...] for ref in dqkv]
        heads = [ref[...] for ref in att]

        @pl.loop(0, TYPES)
        def _(kind):
            span = pl.ds(pl.multiple_of(kind * d, 16), d)
            outs[span, : 3 * width] = typed_sum(ids, left, right, kind, slots).astype(BF16)
            outs[span, 3 * width :] = typed_sum(ids, back, heads, kind, slots).astype(BF16)

        qkv_rows = row_sums(ids, slots, right)
        qkv_rows = jnp.concatenate([qkv_rows, jnp.zeros((TYPES, width), F32)], axis=1)
        firsts = carried(ids, grads, slots, length)
        small = jnp.concatenate([firsts, below[:6, :], qkv_rows, below[6:8, :]], axis=0)
        outs[TYPES * d : TYPES * d + SMALL, :], outs[TYPES * d + SMALL :, :] = halved(small)

    out = arr((TYPES * d + 2 * SMALL, d))
    return run(f"attn_dw{layer}", body, meta, (rows, dqkv, grads, att, below), out, 8)


def ffn_weights(dims, layer, meta, rows, dpre, grads, act):
    length, slots, hidden, d = dims.length, dims.slots, dims.hidden, dims.d

    def body(meta_ref, ins, outs):
        rows, dpre, grads, act = ins
        total, small = outs
        ids = Ids(meta_ref, dims)
        for step, (left, right) in enumerate(((rows, dpre), (grads, act))):
            left_rows = [ref[:length, :] for ref in left]
            right_rows = [ref[...] for ref in right]

            @pl.loop(0, TYPES)
            def _(kind, step=step, left_rows=left_rows, right_rows=right_rows):
                span = pl.ds(pl.multiple_of((TYPES * step + kind) * d, 16), d)
                total[span, :] = typed_sum(ids, left_rows, right_rows, kind, slots).astype(BF16)

        small[0:6, :] = carried(ids, grads, slots, length)
        small[6:8, :] = row_sums(ids, slots, [ref[...] for ref in dpre])

    outs = (arr((2 * TYPES * d, hidden)), arr((8, hidden), F32))
    return run(f"ffn_dw{layer}", body, meta, (rows, dpre, grads, act), outs, 8)


def ffn_forward(dims, layer, meta, slot, rows, weight, small):
    length, hidden = dims.length, dims.hidden

    def body(meta_ref, ins, outs):
        rows, (in_w, back_w), small = ins
        part, act, slope = outs
        kind = Ids(meta_ref, dims).kind(slot)
        pre = dot(rows[...], in_w[kind]) + small[pl.ds(IN_B + kind, 1), :hidden]
        gate = 0.5 * (1.0 + lax.erf(pre * HALF_ROOT))
        act[...] = (pre * gate).astype(BF16)
        slope[...] = (gate + pre * (DENSITY * jnp.exp(-0.5 * pre * pre))).astype(BF16)
        part[...] = dot(act[...], back_w[kind]).astype(BF16)

    outs = (arr((length, dims.d)), arr((length, hidden)), arr((length, hidden)))
    return run(f"ffn_fwd{layer}_{slot}", body, meta, (rows, weight, small), outs)


def ffn_backward(dims, layer, meta, slot, grads, slope, weight):
    length, hidden = dims.length, dims.hidden

    def body(meta_ref, ins, outs):
        grads, slope, (in_w, back_w) = ins
        part, dpre = outs
        kind = Ids(meta_ref, dims).kind(slot)
        dact = dot_nt(grads[:length, :], back_w[kind])
        dpre[...] = (dact * slope[...].astype(F32)).astype(BF16)
        part[...] = dot_nt(dpre[...], in_w[kind]).astype(BF16)

    outs = (arr((length, dims.d)), arr((length, hidden)))
    return run(f"ffn_bwd{layer}_{slot}", body, meta, (grads, slope, weight), outs)


def normalized(values):
    center = values - jnp.mean(values, axis=-1, keepdims=True)
    inv = lax.rsqrt(jnp.mean(center * center, axis=-1, keepdims=True) + EPS)
    return center * inv, inv


def summed(parts):
    total = parts[0][...].astype(F32)
    for part in parts[1:]:
        total = total + part[...].astype(F32)
    return total


def norm_back(grad, normal, inv, gain):
    scaled = grad * gain
    return inv * (
        scaled
        - jnp.mean(scaled, axis=-1, keepdims=True)
        - normal * jnp.mean(scaled * normal, axis=-1, keepdims=True)
    )


def with_sums(low, value, sums):
    r = value.shape[0]
    low[:r, :] = value.astype(BF16)
    total = jnp.concatenate([jnp.sum(v, axis=0, keepdims=True) for v in sums], axis=0)
    high, rest = halved(total)
    blank = jnp.zeros((TAIL - 6, value.shape[1]), BF16)
    low[r:, :] = jnp.concatenate([high, rest, blank], axis=0)


def first_norm(dims, layer, meta, own_rows, parts, small):
    r, d = dims.length, dims.d

    def body(meta_ref, ins, outs):
        own_rows, parts, small = ins
        low, normal, inv = outs
        kind = Ids(meta_ref, dims).kind(0)
        mixed = own_rows[...].astype(F32) + summed(parts) + small[pl.ds(OUT_B + kind, 1), :]
        xhat, scale = normalized(mixed)
        normal[...] = xhat
        inv[...] = jnp.broadcast_to(scale, inv.shape)
        low[...] = (xhat * small[pl.ds(GAIN1 + kind, 1), :] + small[pl.ds(SHIFT1 + kind, 1), :]).astype(BF16)

    outs = (arr((r, d)), arr((r, d), F32), arr((r, 128), F32))
    return run(f"norm1_{layer}", body, meta, (own_rows, parts, small), outs)


def second_values(kind, normal, parts, small):
    normed = normal[...] * small[pl.ds(GAIN1 + kind, 1), :] + small[pl.ds(SHIFT1 + kind, 1), :]
    xhat, scale = normalized(normed + summed(parts) + small[pl.ds(BACK_B + kind, 1), :])
    output = xhat * small[pl.ds(GAIN2 + kind, 1), :] + small[pl.ds(SHIFT2 + kind, 1), :]
    return xhat, scale, output.astype(BF16)


def second_norm(dims, layer, meta, normal, parts, small):
    r, d = dims.length, dims.d

    def body(meta_ref, ins, outs):
        normal, parts, small = ins
        low, xhat_ref, inv = outs
        kind = Ids(meta_ref, dims).kind(0)
        xhat, scale, low[...] = second_values(kind, normal, parts, small)
        xhat_ref[...] = xhat
        inv[...] = jnp.broadcast_to(scale, inv.shape)

    outs = (arr((r, d)), arr((r, d), F32), arr((r, 128), F32))
    return run(f"norm2_{layer}", body, meta, (normal, parts, small), outs)


def second_back(kind, grad, xhat, scale, small, second_grad, low):
    value = norm_back(grad, xhat, scale, small[pl.ds(GAIN2 + kind, 1), :])
    second_grad[...] = value
    with_sums(low, value, (grad * xhat, grad, value))


def last_norm(dims, layer, meta, normal, parts, small, cotangent):
    r, d = dims.length, dims.d

    def body(meta_ref, ins, outs):
        normal, parts, small, cotangent = ins
        act, second_grad, low = outs
        ids = Ids(meta_ref, dims)
        kind = ids.kind(0)
        xhat, scale, act[...] = second_values(kind, normal, parts, small)
        grad = cotangent[ids.section].astype(F32)
        second_back(kind, grad, xhat, scale, small, second_grad, low)

    outs = (arr((r, d)), arr((r, d), F32), arr((r + TAIL, d)))
    return run(f"norm2_{layer}", body, meta, (normal, parts, small, cotangent), outs)


def between_layers(dims, layer, meta, parts, first_grad, xhat, inv, small):
    r, d = dims.length, dims.d

    def body(meta_ref, ins, outs):
        parts, first_grad, xhat, inv, small = ins
        input_grad, second_grad, low = outs
        kind = Ids(meta_ref, dims).kind(0)
        value = summed(parts) + first_grad[...]
        input_grad[...] = value
        grad = value.astype(BF16).astype(F32)
        second_back(kind, grad, xhat[...], inv[:, :1], small, second_grad, low)

    outs = (arr((r, d), F32), arr((r, d), F32), arr((r + TAIL, d)))
    return run(f"between{layer}", body, meta, (parts, first_grad, xhat, inv, small), outs)


def first_back(dims, layer, meta, parts, second_grad, xhat, inv, small):
    r, d = dims.length, dims.d

    def body(meta_ref, ins, outs):
        parts, second_grad, xhat, inv, small = ins
        first_grad, low = outs
        kind = Ids(meta_ref, dims).kind(0)
        grad = summed(parts) + second_grad[...]
        value = norm_back(grad, xhat[...], inv[:, :1], small[pl.ds(GAIN1 + kind, 1), :])
        first_grad[...] = value
        with_sums(low, value, (grad * xhat[...], grad, value))

    outs = (arr((r, d), F32), arr((r + TAIL, d)))
    return run(f"norm1_back{layer}", body, meta, (parts, second_grad, xhat, inv, small), outs)


def input_gradient(dims, layer, meta, parts, first_grad):
    def body(meta_ref, ins, outs):
        parts, first_grad = ins
        outs[...] = summed(parts) + first_grad[...]

    return run(f"input_grad{layer}", body, meta, (parts, first_grad), arr((dims.length, dims.d), F32))


def swap(value, axis, bit):
    count = lax.axis_size(axis)
    return lax.ppermute(value, axis, [(source, source ^ bit) for source in range(count)])


def gather(value, slots):
    return [value] + [swap(value, "tensor", k) for k in range(1, slots)]


def scatter(parts):
    return [parts[0]] + [swap(part, "tensor", k) for k, part in enumerate(parts) if k]


def tied(*values):
    return lax.optimization_barrier(values)


class GradSum:
    def __init__(self, dims, layer, meta, names, small):
        self.dims, self.layer, self.meta, self.names = dims, layer, meta, [f"{name}{layer}" for name in names]
        self.name, self.small, self.pieces = "_".join(self.names), small, [None] * len(names)

    def start(self, value):
        self.value = value
        self.d, self.cols = self.dims.d, value.shape[1]
        self.count = value.shape[0] // self.d
        self.rows = self.d // self.dims.dp
        self.extra = 2 * SMALL if self.small else 0
        self.pad = 0 if self.small else PAD
        self.other = lax.ppermute(value, "section", [(1 - self.layer, self.layer)])

    def permute(self, value, bit):
        base = self.layer * self.dims.dp
        pairs = [(base + z, base + (z ^ bit)) for z in range(self.dims.dp)]
        return lax.ppermute(value, ("section", "dp"), pairs)

    def whole(self, ref, base):
        return ref[base : base + SMALL, :].astype(F32) + ref[base + SMALL : base + 2 * SMALL, :].astype(F32)

    def near_sum(self):
        dims, rows, count, cols, d = self.dims, self.rows, self.count, self.cols, self.d
        if dims.dp != 4:
            both = self.value.astype(F32) + self.other.astype(F32)
            if self.small:
                low = both[count * d :]
                self.total_small = lax.psum(low[:SMALL] + low[SMALL:], "dp")
            return both[: count * d].reshape(count, d, cols).astype(BF16)
        base = 2 * count * rows

        def body(meta_ref, ins, outs):
            value, other = ins
            sent, kept = outs
            odd = lax.rem(Ids(meta_ref, dims).dp, 2)

            def part(index, chunk):
                start = pl.multiple_of(index * d + chunk * rows, 16)
                return value[pl.ds(start, rows), :].astype(F32) + other[pl.ds(start, rows), :].astype(F32)

            for i in range(2):
                for index in range(count):
                    at = (i * count + index) * rows
                    sent[at : at + rows, :] = part(index, 2 * i + 1 - odd).astype(BF16)
                    kept[at : at + rows, :] = part(index, 2 * i + odd)
            if self.pad:
                sent[base:, :] = jnp.zeros((self.pad, cols), BF16)
            if self.small:
                total = self.whole(value, count * d) + self.whole(other, count * d)
                sent[base : base + SMALL, :], sent[base + SMALL : base + 2 * SMALL, :] = halved(total)
                kept[base:, :] = total

        outs = (arr((base + self.extra + self.pad, cols)), arr((base + self.extra // 2, cols), F32))
        sent, self.kept = run(f"{self.name}_a", body, self.meta, (self.value, self.other), outs)
        return sent

    def near_send(self, sent):
        if self.dims.dp != 4:
            whole = lax.psum_scatter(sent, "dp", scatter_dimension=1, tiled=True)
            each = self.count // len(self.pieces)
            for i in range(len(self.pieces)):
                self.pieces[i] = [whole[each * i : each * (i + 1)]] + ([self.total_small] if self.small else [])
        else:
            self.near = self.permute(sent, 1)

    def far_sum(self):
        dims, cols, size = self.dims, self.cols, self.count // len(self.names) * self.rows
        if dims.dp != 4:
            return [None] * len(self.names)

        def body(meta_ref, ins, outs):
            kept, near = ins
            mine = lax.div(Ids(meta_ref, dims).dp, 2)
            block = self.count * self.rows

            def half(i, piece):
                span = pl.ds(pl.multiple_of(i * block + piece * size, 16), size)
                return kept[span, :] + near[span, :].astype(F32)

            for piece, (sent, final) in enumerate(outs):
                sent[:size, :] = half(1 - mine, piece).astype(BF16)
                final[:size, :] = half(mine, piece)
                if self.small:
                    total = kept[2 * block :, :] + self.whole(near, 2 * block)
                    sent[size : size + SMALL, :], sent[size + SMALL :, :] = halved(total)
                    final[size:, :] = total

        out = (arr((size + self.extra, cols)), arr((size + self.extra // 2, cols), F32))
        outs = run(f"{self.name}_b", body, self.meta, (self.kept, self.near), [out] * len(self.names))
        self.final = [final for _, final in outs]
        return [sent for sent, _ in outs]

    def far_send(self, sent, piece):
        if self.dims.dp == 4:
            self.pieces[piece] = [self.final[piece], self.permute(sent[piece], 2)]

    def finish(self, piece, shapes, put, before=None):
        each = self.count // len(self.names)
        dims, rows, size = self.dims, self.rows, each * self.rows
        pieces = self.pieces[piece]
        flat = len(pieces)

        def body(meta_ref, ins, outs, *scratch):
            pieces, values, sems = ins[0], scratch[:-1], scratch[-1]

            def total(kind):
                if dims.dp != 4:
                    return pieces[0][kind].astype(F32)
                span = slice(kind * rows, (kind + 1) * rows)
                return pieces[0][span, :] + pieces[1][span, :].astype(F32)

            @pl.when(Ids(meta_ref, dims).section == self.layer)
            def _():
                small = None
                if self.small:
                    small = pieces[0][size:, :] + self.whole(pieces[1], size) if dims.dp == 4 else pieces[1][...]
                put(values, [total(index) for index in range(each)], small)
                for copy in copies(list(zip(values, outs)), sems):
                    copy.wait()

        outs = [InHbm(arr(shape, F32)) for shape in shapes]
        ins = [pieces] + ([] if before is None else [InHbm(a) for a in before])
        aliases = {} if before is None else {flat + i: i for i in range(len(shapes))}
        scratch = [pltpu.VMEM(shape, F32) for shape in shapes] + [pltpu.SemaphoreType.DMA((len(shapes),))]
        return run(f"{self.names[piece]}_end", body, self.meta, ins, outs, 8, scratch, aliases)


def pack_params(dims, meta, arrays):
    width = dims.width

    def body(meta_ref, ins, outs, *scratch):
        for copy in copies(list(zip(ins, scratch[:-1])), scratch[-1]):
            copy.wait()
        out_b, back_b, gains, shifts, in_b, qkv_b = scratch[:-1]
        for t in range(TYPES):
            for row, ref in ((OUT_B, out_b), (BACK_B, back_b), (IN_B, in_b)):
                outs[row + t : row + t + 1, :] = ref[0, t : t + 1, :]
            for row, ref in ((GAIN1, gains), (SHIFT1, shifts)):
                for norm in range(2):
                    outs[row + 2 * norm + t : row + 2 * norm + t + 1, :] = ref[0, t, norm : norm + 1, :]
            outs[QKV_B + t : QKV_B + t + 1, :] = jnp.zeros((1, dims.d), F32)
            outs[QKV_B + t : QKV_B + t + 1, :width] = qkv_b[0, t, 0:1, :]
            outs[QKV_B + t : QKV_B + t + 1, 2 * width : 3 * width] = qkv_b[0, t, 1:2, :]

    scratch = [pltpu.VMEM(a.shape, F32) for a in arrays] + [pltpu.SemaphoreType.DMA((len(arrays),))]
    return run("pack", body, meta, [InHbm(a) for a in arrays], arr((16, dims.d), F32), scratch=scratch)


def order_params(dims, meta, own, other):
    def body(meta_ref, ins, outs):
        here = meta_ref[0] == 0
        own, other = ins[0][...], ins[1][...]
        outs[0][...] = jnp.where(here, own, other)
        outs[1][...] = jnp.where(here, other, own)

    return run("params", body, meta, [own, other], [arr(own.shape, F32)] * 2)


def both_chains(dims, meta, own, moved, name):
    def body(meta_ref, ins, outs):
        own, moved = ins
        first = meta_ref[0] == 0

        @pl.when(first)
        def _():
            outs[0, 0] = own[0][...]
            outs[0, 1] = moved[0][...]

        @pl.when(jnp.logical_not(first))
        def _():
            outs[0, 0] = moved[1][...]
            outs[0, 1] = own[1][...]

    return run(name, body, meta, (own, moved), arr((1, 2, dims.length, dims.d), own[0].dtype), 8)


def body(
    tokens,
    cotangent,
    lengths,
    chain_type,
    qkv_weight,
    qkv_bias,
    out_weight,
    out_bias,
    ffn_in,
    ffn_in_bias,
    ffn_out,
    ffn_out_bias,
    norm_gain,
    norm_bias,
):
    dims = Dims()
    dims.per_chip, dims.length, dims.d = tokens.shape
    dims.slots = lax.axis_size("tensor")
    dims.dp = lax.axis_size("dp")
    dims.group = lengths.shape[0]
    dims.width = qkv_weight.shape[-1]
    dims.hidden = ffn_in.shape[-1]
    sections = lax.axis_size("section")
    assert dims.per_chip == sections == LAYERS and dims.slots & (dims.slots - 1) == 0
    assert dims.dp & (dims.dp - 1) == 0 and 4 * dims.width == dims.d == dims.hidden
    d, width, slots = dims.d, dims.width, dims.slots
    each = range(slots)
    section = lax.axis_index("section")
    meta = jnp.concatenate(
        [
            jnp.stack([section, lax.axis_index("tensor"), lax.axis_index("dp")]).astype(jnp.int32),
            chain_type,
            lengths,
        ]
    )

    own_rows = jnp.where(section == 0, tokens[0], tokens[1])
    rows = gather(own_rows, slots)

    qkv_own = qkv_weight[0].transpose(0, 2, 3, 1).reshape(TYPES, 3 * width, d)
    attn_own = [qkv_own, out_weight[0]]
    attn_other = [swap(w, "section", 1) for w in attn_own]
    biases = [qkv_bias, swap(qkv_bias, "section", 1)]
    packed = pack_params(
        dims, meta, (out_bias, ffn_out_bias, norm_gain, norm_bias, ffn_in_bias, qkv_bias)
    )
    small = order_params(dims, meta, packed, swap(packed, "section", 1))
    ffn_own = [ffn_in[0], ffn_out[0]]
    rows[0], small = tied(rows[0], small)

    def moved(value, layer):
        return lax.ppermute(value, "section", [(1 - layer, layer)])

    saved = []
    acts = []
    for layer in range(LAYERS):
        weight = fetch(dims, layer, meta, attn_own, attn_other, "attn")
        attn = [attention_forward(dims, layer, meta, k, rows[k], weight, biases) for k in each]
        parts, qkv, att = ([a[i] for a in attn] for i in range(3))
        parts = scatter(parts)
        if layer == 0:
            parts, ffn_sent = tied(parts, ffn_own)
            ffn_other = [swap(w, "section", 1) for w in ffn_sent]
        first = first_norm(dims, layer, meta, own_rows, parts, small[layer])
        normed = gather(first[0], slots)
        weight = fetch(dims, layer, meta, ffn_own, ffn_other, "ffn")
        ffn = [ffn_forward(dims, layer, meta, k, normed[k], weight, small[layer]) for k in each]
        parts, act, slope = ([f[i] for f in ffn] for i in range(3))
        parts = scatter(parts)
        if layer < LAYERS - 1:
            second = second_norm(dims, layer, meta, first[1], parts, small[layer])
        else:
            second = last_norm(dims, layer, meta, first[1], parts, small[layer], cotangent)
        saved.append((rows, qkv, att, first, normed, act, slope, second))
        own_rows = second[0]
        acts.append(own_rows)
        if layer < LAYERS - 1:
            rows = gather(own_rows, slots)

    share = d // dims.dp
    ffn_shapes = [(TYPES, share, dims.hidden)]
    attn_shapes = [
        (TYPES, 3, share, width),
        (TYPES, width, share),
        (1, TYPES, 2, width),
        (1, TYPES, d),
        (1, TYPES, dims.hidden),
        (1, TYPES, d),
        (1, TYPES, 2, d),
        (1, TYPES, 2, d),
    ]

    def put_ffn(outs, totals, small):
        for index, total in enumerate(totals):
            outs[index // TYPES][index % TYPES] = total

    def put_attn(outs, totals, small):
        qkv_out, out_out, qkv_b, out_b, in_b, back_b, gains, shifts = outs
        for kind, total in enumerate(totals):
            for i in range(3):
                qkv_out[kind, i] = total[:, i * width : (i + 1) * width]
            out_out[kind] = total[:, 3 * width :].T
            qkv_b[0, kind, 0:1, :] = small[QKV_SUMS + kind : QKV_SUMS + kind + 1, :width]
            qkv_b[0, kind, 1:2, :] = small[QKV_SUMS + kind : QKV_SUMS + kind + 1, 2 * width : 3 * width]
            in_b[0, kind : kind + 1, :] = small[IN_SUMS + kind : IN_SUMS + kind + 1, :]
            for norm, (base, bias) in enumerate(((FIRST_SUMS, out_b), (SECOND_SUMS, back_b))):
                row = base + 3 * kind
                gains[0, kind, norm : norm + 1, :] = small[row : row + 1, :]
                shifts[0, kind, norm : norm + 1, :] = small[row + 1 : row + 2, :]
                bias[0, kind : kind + 1, :] = small[row + 2 : row + 3, :]

    second_grad, low = second[1:]
    input_grads = [None] * LAYERS
    ffn_sums = [GradSum(dims, layer, meta, ("in", "back") if layer else ("ffn",), False) for layer in range(LAYERS)]
    attn_sums = [GradSum(dims, layer, meta, ("attn",), True) for layer in range(LAYERS)]
    for layer in reversed(range(LAYERS)):
        rows, qkv, att, first, normed, act, slope, second = saved[layer]
        top = layer == LAYERS - 1
        grads = gather(low, slots)
        weight = fetch(dims, layer, meta, ffn_own, ffn_other, "ffn_back")
        if top:
            acts_moved = [moved(acts[i], i) for i in range(LAYERS)]
        else:
            ffn_up, attn_up = ffn_sums[layer + 1], attn_sums[layer + 1]
            grads, near, ffn_up.pieces[1], ffn_far = tied(
                grads, attn_up.near_sum(), ffn_up.pieces[1], ffn_far
            )
            attn_sums[layer + 1].near_send(near)
            ffn_sums[layer + 1].far_send(ffn_far, 0)
        back = [ffn_backward(dims, layer, meta, k, grads[k], slope[k], weight) for k in each]
        parts, dpre = ([b[i] for b in back] for i in range(2))
        parts = scatter(parts)
        ffn_grad, below = ffn_weights(dims, layer, meta, normed, dpre, grads, act)
        if top:
            acts_out = both_chains(dims, meta, acts, acts_moved, "acts_out")
            parts, ffn_grad, acts_out = tied(parts, ffn_grad, acts_out)
        else:
            far = attn_up.far_sum()
            parts, ffn_grad, far, ffn_up.pieces[0] = tied(parts, ffn_grad, far, ffn_up.pieces[0])
            attn_sums[layer + 1].far_send(far, 0)
        ffn_sums[layer].start(ffn_grad)
        first_grad, low = first_back(
            dims, layer, meta, parts, second_grad, first[1], first[2], small[layer]
        )
        grads = gather(low, slots)
        weight = fetch(dims, layer, meta, attn_own, attn_other, "attn_back")
        near = ffn_sums[layer].near_sum()
        grads, _ = tied(grads, near)
        ffn_sums[layer].near_send(near)
        back = [attention_backward(dims, layer, meta, k, grads[k], qkv[k], weight) for k in each]
        parts, dqkv = ([b[i] for b in back] for i in range(2))
        parts = scatter(parts)
        if not top:
            dqkv, attn_up.pieces[0] = tied(dqkv, attn_up.pieces[0])
        attn_grad = attention_weights(dims, layer, meta, rows, dqkv, grads, att, below)
        if top:
            parts, attn_grad, ffn_far = tied(parts, attn_grad, ffn_sums[layer].far_sum())
            ffn_sums[layer].far_send(ffn_far, 1)
        attn_sums[layer].start(attn_grad)
        if layer > 0:
            second = saved[layer - 1][-1]
            input_grads[layer], second_grad, low = between_layers(
                dims, layer, meta, parts, first_grad, second[1], second[2], small[layer - 1]
            )
        else:
            input_grads[layer] = input_gradient(dims, layer, meta, parts, first_grad)

    back_done = ffn_up.finish(1, ffn_shapes, put_ffn)
    in_done = ffn_up.finish(0, ffn_shapes, put_ffn)
    attn_done = attn_up.finish(0, attn_shapes, put_attn)
    ffn_far = ffn_sums[0].far_sum()
    attn_sums[0].other, _ = tied(attn_sums[0].other, ffn_far)
    ffn_sums[0].far_send(ffn_far, 0)
    attn_sums[0].near_send(attn_sums[0].near_sum())
    attn_sums[0].far_send(attn_sums[0].far_sum(), 0)
    in_total, back_total = ffn_sums[0].finish(0, ffn_shapes * 2, put_ffn, in_done + back_done)
    grads_moved = [moved(input_grads[layer], layer) for layer in range(LAYERS)]
    grads_out = both_chains(dims, meta, input_grads, grads_moved, "grads_out")
    qkv_total, out_total, *small_grads = attn_sums[0].finish(0, attn_shapes, put_attn, attn_done)
    qkv_bias_out, out_bias_out, in_bias_out, back_bias_out, gain_out, shift_out = small_grads
    return (
        acts_out,
        grads_out,
        qkv_total.transpose(0, 2, 1, 3)[None],
        qkv_bias_out,
        out_total[None],
        out_bias_out,
        in_total[None],
        in_bias_out,
        back_total.transpose(0, 2, 1)[None],
        back_bias_out,
        gain_out,
        shift_out,
    )


def solution(mesh):
    placed = (
        P(("dp", "tensor"), None, None),
        P(("dp", "tensor"), None, None),
        P("dp"),
        P("dp"),
        P("section", None, None, None, "tensor"),
        P("section", None, None, "tensor"),
        P("section", None, "tensor", None),
        P("section", None, None),
        P("section", None, None, "tensor"),
        P("section", None, "tensor"),
        P("section", None, "tensor", None),
        P("section", None, None),
        P("section", None, None, None),
        P("section", None, None, None),
    )
    return jax.shard_map(
        body,
        mesh=mesh,
        in_specs=placed,
        out_specs=(
            P("section", ("dp", "tensor"), None, None),
            P("section", ("dp", "tensor"), None, None),
            P("section", None, "dp", None, "tensor"),
            P("section", None, None, "tensor"),
            P("section", None, "tensor", "dp"),
            P("section", None, None),
            P("section", None, "dp", "tensor"),
            P("section", None, "tensor"),
            P("section", None, "tensor", "dp"),
            P("section", None, None),
            P("section", None, None, None),
            P("section", None, None, None),
        ),
        check_vma=False,
    )
```

```python
import functools
import math

import jax
import jax.numpy as jnp
from jax import lax
from jax.experimental import pallas as pl
from jax.experimental.pallas import tpu as pltpu
from jax.sharding import PartitionSpec as P

HEAD_DIM = 64
TYPES = 2
LAYERS = 2
EPS = 1e-06
HALF_ROOT = 0.7071067811865476
DENSITY = 0.3989422804014327
SCALE = 1.0 / math.sqrt(HEAD_DIM)
MIB = 1 << 20

F32 = jnp.float32
BF16 = jnp.bfloat16

TAIL = 16
PAD = 64
FIRST_SUMS, SECOND_SUMS, QKV_SUMS, IN_SUMS, SMALL = 0, 6, 12, 14, 16

OUT_B, BACK_B, GAIN1, GAIN2, SHIFT1, SHIFT2, IN_B, QKV_B = range(0, 16, 2)


def dot(a, b):
    return jnp.dot(a, b, preferred_element_type=F32)


def dot_nt(a, b):
    return lax.dot_general(a, b, (((1,), (1,)), ((), ())), preferred_element_type=F32)


def dot_tn(a, b):
    return lax.dot_general(a, b, (((0,), (0,)), ((), ())), preferred_element_type=F32)


def nested(structure, flat):
    leaves, tree = jax.tree.flatten(structure)
    return jax.tree.unflatten(tree, flat)


class InHbm:
    def __init__(self, value):
        self.value = value


def run(name, body, meta, ins, outs, limit=6, scratch=(), aliases=None):
    flat_in, flat_out = jax.tree.leaves(ins), jax.tree.leaves(outs)

    def kernel(meta_ref, *refs):
        into = len(flat_in) + len(flat_out)
        body(meta_ref, nested(ins, refs[: len(flat_in)]), nested(outs, refs[len(flat_in) : into]), *refs[into:])

    def spec(leaf):
        return pl.BlockSpec(memory_space=pltpu.HBM if isinstance(leaf, InHbm) else pltpu.VMEM)

    def plain(leaf):
        return leaf.value if isinstance(leaf, InHbm) else leaf

    results = pl.pallas_call(
        kernel,
        name=name,
        in_specs=[pl.BlockSpec(memory_space=pltpu.SMEM)] + [spec(a) for a in flat_in],
        out_specs=[spec(a) for a in flat_out],
        out_shape=[plain(a) for a in flat_out],
        scratch_shapes=list(scratch),
        input_output_aliases={1 + i: o for i, o in (aliases or {}).items()},
        compiler_params=pltpu.CompilerParams(vmem_limit_bytes=limit * MIB),
        cost_estimate=pl.CostEstimate(flops=1, bytes_accessed=1, transcendentals=0),
    )(meta, *[plain(a) for a in flat_in])
    return nested(outs, results)


def arr(shape, dtype=BF16):
    return jax.ShapeDtypeStruct(tuple(shape), dtype)


class Ids:
    def __init__(self, meta, dims):
        self.meta, self.dims = meta, dims
        self.section, self.tensor, self.dp = meta[0], meta[1], meta[2]

    def chain(self, slot):
        return (self.tensor ^ slot) * self.dims.per_chip + self.section

    def kind(self, slot):
        return self.meta[3 + self.chain(slot)]

    def length(self, slot):
        return self.meta[3 + self.dims.group + self.chain(slot)]


def copies(pairs, sems):
    started = [pltpu.make_async_copy(source, target, sems.at[i]) for i, (source, target) in enumerate(pairs)]
    for copy in started:
        copy.start()
    return started


def fetch(dims, layer, meta, own, other, name):
    def body(meta_ref, ins, outs, sems):
        own, other = ins
        ids = Ids(meta_ref, dims)

        def go(source):
            for copy in copies(list(zip(source, outs)), sems):
                copy.wait()

        pl.when(ids.section == layer)(lambda: go(own))
        pl.when(ids.section != layer)(lambda: go(other))

    ins = ([InHbm(w) for w in own], [InHbm(w) for w in other])
    outs = [arr(w.shape, w.dtype) for w in own]
    return run(f"fetch_{name}{layer}", body, meta, ins, outs, scratch=[pltpu.SemaphoreType.DMA((len(own),))])


class Dims:
    pass


def key_major(qkv, width, keep):
    found = []
    for c in range(0, width, HEAD_DIM):
        scores = dot_nt(qkv[:, width + c : width + c + HEAD_DIM], qkv[:, c : c + HEAD_DIM]) * SCALE
        scores = jnp.where(keep, scores, -1e9)
        expd = jnp.exp(scores - jnp.max(scores, axis=0, keepdims=True))
        found.append((expd * (1.0 / jnp.sum(expd, axis=0, keepdims=True)), c))
    return found


def attention_forward(dims, layer, meta, slot, rows, weight, biases):
    length, width = dims.length, dims.width

    def body(meta_ref, ins, outs):
        rows, (qkv_w, out_w), biases = ins
        part, qkv, att = outs
        ids = Ids(meta_ref, dims)
        kind = ids.kind(slot)
        here = ids.section == layer
        parts = [jnp.where(here, biases[0][0, kind, i : i + 1, :], biases[1][0, kind, i : i + 1, :]) for i in range(2)]
        bias = jnp.concatenate([parts[0], jnp.zeros_like(parts[0]), parts[1]], axis=1)
        qkv[...] = (dot_nt(rows[...], qkv_w[kind]) + bias).astype(BF16)
        keep = lax.broadcasted_iota(jnp.int32, (length, 1), 0) < ids.length(slot)
        heads = []
        for probs, c in key_major(qkv, width, keep):
            value = qkv[:, 2 * width + c : 2 * width + c + HEAD_DIM]
            heads.append(dot_tn(probs.astype(BF16), value))
        att[...] = jnp.concatenate(heads, axis=1).astype(BF16)
        part[...] = dot(att[...], out_w[kind]).astype(BF16)

    outs = (arr((length, dims.d)), arr((length, 3 * width)), arr((length, width)))
    return run(f"attn_fwd{layer}_{slot}", body, meta, (rows, weight, biases), outs)


def attention_backward(dims, layer, meta, slot, grads, qkv, weight):
    length, width = dims.length, dims.width

    def body(meta_ref, ins, outs):
        grads, qkv, (qkv_w, out_w) = ins
        part, dqkv = outs
        ids = Ids(meta_ref, dims)
        kind = ids.kind(slot)
        keep = lax.broadcasted_iota(jnp.int32, (length, 1), 0) < ids.length(slot)
        datt = dot_nt(grads[:length, :], out_w[kind]).astype(BF16)
        queries, keys, values = [], [], []
        for probs, c in key_major(qkv, width, keep):
            query = qkv[:, c : c + HEAD_DIM]
            key = qkv[:, width + c : width + c + HEAD_DIM]
            da = datt[:, c : c + HEAD_DIM]
            dprobs = dot_nt(qkv[:, 2 * width + c : 2 * width + c + HEAD_DIM], da)
            dscores = (probs * (dprobs - jnp.sum(probs * dprobs, axis=0, keepdims=True))).astype(BF16)
            queries.append(dot_tn(dscores, key) * SCALE)
            keys.append(dot(dscores, query) * SCALE)
            values.append(dot(probs.astype(BF16), da))
        dqkv[...] = jnp.concatenate(queries + keys + values, axis=1).astype(BF16)
        part[...] = dot(dqkv[...], qkv_w[kind]).astype(BF16)

    outs = (arr((length, dims.d)), arr((length, 3 * width)))
    return run(f"attn_bwd{layer}_{slot}", body, meta, (grads, qkv, weight), outs)


def typed_sum(ids, left, right, kind, slots):
    chosen = [
        jnp.where(ids.kind(k) == kind, right[k], jnp.zeros_like(right[k])) for k in range(slots)
    ]
    return dot_tn(jnp.concatenate(left, axis=0), jnp.concatenate(chosen, axis=0))


def halved(value):
    high = value.astype(BF16)
    return high, (value - high.astype(F32)).astype(BF16)


def carried(ids, blocks, slots, r):
    found = []
    for kind in range(TYPES):
        total = jnp.zeros((3, blocks[0].shape[1]), F32)
        for k in range(slots):
            tail = blocks[k][r : r + TAIL, :].astype(F32)
            total = total + jnp.where(ids.kind(k) == kind, tail[0:3] + tail[3:6], 0.0)
        found.append(total)
    return jnp.concatenate(found, axis=0)


def row_sums(ids, slots, rows):
    found = []
    for kind in range(TYPES):
        total = 0.0
        for k in range(slots):
            here = jnp.sum(rows[k].astype(F32), axis=0, keepdims=True)
            total = total + jnp.where(ids.kind(k) == kind, here, 0.0)
        found.append(total)
    return jnp.concatenate(found, axis=0)


def attention_weights(dims, layer, meta, rows, dqkv, grads, att, below):
    length, slots, width, d = dims.length, dims.slots, dims.width, dims.d

    def body(meta_ref, ins, outs):
        rows, dqkv, grads, att, below = ins
        ids = Ids(meta_ref, dims)
        left = [ref[...] for ref in rows]
        back = [ref[:length, :] for ref in grads]
        right = [ref[...] for ref in dqkv]
        heads = [ref[...] for ref in att]

        @pl.loop(0, TYPES)
        def _(kind):
            span = pl.ds(pl.multiple_of(kind * d, 16), d)
            outs[span, : 3 * width] = typed_sum(ids, left, right, kind, slots).astype(BF16)
            outs[span, 3 * width :] = typed_sum(ids, back, heads, kind, slots).astype(BF16)

        qkv_rows = row_sums(ids, slots, right)
        qkv_rows = jnp.concatenate([qkv_rows, jnp.zeros((TYPES, width), F32)], axis=1)
        firsts = carried(ids, grads, slots, length)
        small = jnp.concatenate([firsts, below[:6, :], qkv_rows, below[6:8, :]], axis=0)
        outs[TYPES * d : TYPES * d + SMALL, :], outs[TYPES * d + SMALL :, :] = halved(small)

    out = arr((TYPES * d + 2 * SMALL, d))
    return run(f"attn_dw{layer}", body, meta, (rows, dqkv, grads, att, below), out, 8)


def ffn_weights(dims, layer, meta, rows, dpre, grads, act):
    length, slots, hidden, d = dims.length, dims.slots, dims.hidden, dims.d

    def body(meta_ref, ins, outs):
        rows, dpre, grads, act = ins
        total, small = outs
        ids = Ids(meta_ref, dims)
        for step, (left, right) in enumerate(((rows, dpre), (grads, act))):
            left_rows = [ref[:length, :] for ref in left]
            right_rows = [ref[...] for ref in right]

            @pl.loop(0, TYPES)
            def _(kind, step=step, left_rows=left_rows, right_rows=right_rows):
                span = pl.ds(pl.multiple_of((TYPES * step + kind) * d, 16), d)
                total[span, :] = typed_sum(ids, left_rows, right_rows, kind, slots).astype(BF16)

        small[0:6, :] = carried(ids, grads, slots, length)
        small[6:8, :] = row_sums(ids, slots, [ref[...] for ref in dpre])

    outs = (arr((2 * TYPES * d, hidden)), arr((8, hidden), F32))
    return run(f"ffn_dw{layer}", body, meta, (rows, dpre, grads, act), outs, 8)


def ffn_forward(dims, layer, meta, slot, rows, weight, small):
    length, hidden = dims.length, dims.hidden

    def body(meta_ref, ins, outs):
        rows, (in_w, back_w), small = ins
        part, act, slope = outs
        kind = Ids(meta_ref, dims).kind(slot)
        pre = dot(rows[...], in_w[kind]) + small[pl.ds(IN_B + kind, 1), :hidden]
        gate = 0.5 * (1.0 + lax.erf(pre * HALF_ROOT))
        act[...] = (pre * gate).astype(BF16)
        slope[...] = (gate + pre * (DENSITY * jnp.exp(-0.5 * pre * pre))).astype(BF16)
        part[...] = dot(act[...], back_w[kind]).astype(BF16)

    outs = (arr((length, dims.d)), arr((length, hidden)), arr((length, hidden)))
    return run(f"ffn_fwd{layer}_{slot}", body, meta, (rows, weight, small), outs)


def ffn_backward(dims, layer, meta, slot, grads, slope, weight):
    length, hidden = dims.length, dims.hidden

    def body(meta_ref, ins, outs):
        grads, slope, (in_w, back_w) = ins
        part, dpre = outs
        kind = Ids(meta_ref, dims).kind(slot)
        dact = dot_nt(grads[:length, :], back_w[kind])
        dpre[...] = (dact * slope[...].astype(F32)).astype(BF16)
        part[...] = dot_nt(dpre[...], in_w[kind]).astype(BF16)

    outs = (arr((length, dims.d)), arr((length, hidden)))
    return run(f"ffn_bwd{layer}_{slot}", body, meta, (grads, slope, weight), outs)


def normalized(values):
    center = values - jnp.mean(values, axis=-1, keepdims=True)
    inv = lax.rsqrt(jnp.mean(center * center, axis=-1, keepdims=True) + EPS)
    return center * inv, inv


def summed(parts):
    total = parts[0][...].astype(F32)
    for part in parts[1:]:
        total = total + part[...].astype(F32)
    return total


def norm_back(grad, normal, inv, gain):
    scaled = grad * gain
    return inv * (
        scaled
        - jnp.mean(scaled, axis=-1, keepdims=True)
        - normal * jnp.mean(scaled * normal, axis=-1, keepdims=True)
    )


def with_sums(low, value, sums):
    r = value.shape[0]
    low[:r, :] = value.astype(BF16)
    total = jnp.concatenate([jnp.sum(v, axis=0, keepdims=True) for v in sums], axis=0)
    high, rest = halved(total)
    blank = jnp.zeros((TAIL - 6, value.shape[1]), BF16)
    low[r:, :] = jnp.concatenate([high, rest, blank], axis=0)


def first_norm(dims, layer, meta, own_rows, parts, small):
    r, d = dims.length, dims.d

    def body(meta_ref, ins, outs):
        own_rows, parts, small = ins
        low, normal, inv = outs
        kind = Ids(meta_ref, dims).kind(0)
        mixed = own_rows[...].astype(F32) + summed(parts) + small[pl.ds(OUT_B + kind, 1), :]
        xhat, scale = normalized(mixed)
        normal[...] = xhat
        inv[...] = jnp.broadcast_to(scale, inv.shape)
        low[...] = (xhat * small[pl.ds(GAIN1 + kind, 1), :] + small[pl.ds(SHIFT1 + kind, 1), :]).astype(BF16)

    outs = (arr((r, d)), arr((r, d), F32), arr((r, 128), F32))
    return run(f"norm1_{layer}", body, meta, (own_rows, parts, small), outs)


def second_values(kind, normal, parts, small):
    normed = normal[...] * small[pl.ds(GAIN1 + kind, 1), :] + small[pl.ds(SHIFT1 + kind, 1), :]
    xhat, scale = normalized(normed + summed(parts) + small[pl.ds(BACK_B + kind, 1), :])
    output = xhat * small[pl.ds(GAIN2 + kind, 1), :] + small[pl.ds(SHIFT2 + kind, 1), :]
    return xhat, scale, output.astype(BF16)


def second_norm(dims, layer, meta, normal, parts, small):
    r, d = dims.length, dims.d

    def body(meta_ref, ins, outs):
        normal, parts, small = ins
        low, xhat_ref, inv = outs
        kind = Ids(meta_ref, dims).kind(0)
        xhat, scale, low[...] = second_values(kind, normal, parts, small)
        xhat_ref[...] = xhat
        inv[...] = jnp.broadcast_to(scale, inv.shape)

    outs = (arr((r, d)), arr((r, d), F32), arr((r, 128), F32))
    return run(f"norm2_{layer}", body, meta, (normal, parts, small), outs)


def second_back(kind, grad, xhat, scale, small, second_grad, low):
    value = norm_back(grad, xhat, scale, small[pl.ds(GAIN2 + kind, 1), :])
    second_grad[...] = value
    with_sums(low, value, (grad * xhat, grad, value))


def last_norm(dims, layer, meta, normal, parts, small, cotangent):
    r, d = dims.length, dims.d

    def body(meta_ref, ins, outs):
        normal, parts, small, cotangent = ins
        act, second_grad, low = outs
        ids = Ids(meta_ref, dims)
        kind = ids.kind(0)
        xhat, scale, act[...] = second_values(kind, normal, parts, small)
        grad = cotangent[ids.section].astype(F32)
        second_back(kind, grad, xhat, scale, small, second_grad, low)

    outs = (arr((r, d)), arr((r, d), F32), arr((r + TAIL, d)))
    return run(f"norm2_{layer}", body, meta, (normal, parts, small, cotangent), outs)


def between_layers(dims, layer, meta, parts, first_grad, xhat, inv, small):
    r, d = dims.length, dims.d

    def body(meta_ref, ins, outs):
        parts, first_grad, xhat, inv, small = ins
        input_grad, second_grad, low = outs
        kind = Ids(meta_ref, dims).kind(0)
        value = summed(parts) + first_grad[...]
        input_grad[...] = value
        grad = value.astype(BF16).astype(F32)
        second_back(kind, grad, xhat[...], inv[:, :1], small, second_grad, low)

    outs = (arr((r, d), F32), arr((r, d), F32), arr((r + TAIL, d)))
    return run(f"between{layer}", body, meta, (parts, first_grad, xhat, inv, small), outs)


def first_back(dims, layer, meta, parts, second_grad, xhat, inv, small):
    r, d = dims.length, dims.d

    def body(meta_ref, ins, outs):
        parts, second_grad, xhat, inv, small = ins
        first_grad, low = outs
        kind = Ids(meta_ref, dims).kind(0)
        grad = summed(parts) + second_grad[...]
        value = norm_back(grad, xhat[...], inv[:, :1], small[pl.ds(GAIN1 + kind, 1), :])
        first_grad[...] = value
        with_sums(low, value, (grad * xhat[...], grad, value))

    outs = (arr((r, d), F32), arr((r + TAIL, d)))
    return run(f"norm1_back{layer}", body, meta, (parts, second_grad, xhat, inv, small), outs)


def input_gradient(dims, layer, meta, parts, first_grad):
    def body(meta_ref, ins, outs):
        parts, first_grad = ins
        outs[...] = summed(parts) + first_grad[...]

    return run(f"input_grad{layer}", body, meta, (parts, first_grad), arr((dims.length, dims.d), F32))


def swap(value, axis, bit):
    count = lax.axis_size(axis)
    return lax.ppermute(value, axis, [(source, source ^ bit) for source in range(count)])


def gather(value, slots):
    return [value] + [swap(value, "tensor", k) for k in range(1, slots)]


def scatter(parts):
    return [parts[0]] + [swap(part, "tensor", k) for k, part in enumerate(parts) if k]


def tied(*values):
    return lax.optimization_barrier(values)


class GradSum:
    def __init__(self, dims, layer, meta, names, small):
        self.dims, self.layer, self.meta, self.names = dims, layer, meta, [f"{name}{layer}" for name in names]
        self.name, self.small, self.pieces = "_".join(self.names), small, [None] * len(names)

    def start(self, value):
        self.value = value
        self.d, self.cols = self.dims.d, value.shape[1]
        self.count = value.shape[0] // self.d
        self.rows = self.d // self.dims.dp
        self.extra = 2 * SMALL if self.small else 0
        self.pad = 0 if self.small else PAD
        self.other = lax.ppermute(value, "section", [(1 - self.layer, self.layer)])

    def permute(self, value, bit):
        base = self.layer * self.dims.dp
        pairs = [(base + z, base + (z ^ bit)) for z in range(self.dims.dp)]
        return lax.ppermute(value, ("section", "dp"), pairs)

    def whole(self, ref, base):
        return ref[base : base + SMALL, :].astype(F32) + ref[base + SMALL : base + 2 * SMALL, :].astype(F32)

    def near_sum(self):
        dims, rows, count, cols, d = self.dims, self.rows, self.count, self.cols, self.d
        if dims.dp != 4:
            both = self.value.astype(F32) + self.other.astype(F32)
            if self.small:
                low = both[count * d :]
                self.total_small = lax.psum(low[:SMALL] + low[SMALL:], "dp")
            return both[: count * d].reshape(count, d, cols).astype(BF16)
        base = 2 * count * rows

        def body(meta_ref, ins, outs):
            value, other = ins
            sent, kept = outs
            odd = lax.rem(Ids(meta_ref, dims).dp, 2)

            def part(index, chunk):
                start = pl.multiple_of(index * d + chunk * rows, 16)
                return value[pl.ds(start, rows), :].astype(F32) + other[pl.ds(start, rows), :].astype(F32)

            for i in range(2):
                for index in range(count):
                    at = (i * count + index) * rows
                    sent[at : at + rows, :] = part(index, 2 * i + 1 - odd).astype(BF16)
                    kept[at : at + rows, :] = part(index, 2 * i + odd)
            if self.pad:
                sent[base:, :] = jnp.zeros((self.pad, cols), BF16)
            if self.small:
                total = self.whole(value, count * d) + self.whole(other, count * d)
                sent[base : base + SMALL, :], sent[base + SMALL : base + 2 * SMALL, :] = halved(total)
                kept[base:, :] = total

        outs = (arr((base + self.extra + self.pad, cols)), arr((base + self.extra // 2, cols), F32))
        sent, self.kept = run(f"{self.name}_a", body, self.meta, (self.value, self.other), outs)
        return sent

    def near_send(self, sent):
        if self.dims.dp != 4:
            whole = lax.psum_scatter(sent, "dp", scatter_dimension=1, tiled=True)
            each = self.count // len(self.pieces)
            for i in range(len(self.pieces)):
                self.pieces[i] = [whole[each * i : each * (i + 1)]] + ([self.total_small] if self.small else [])
        else:
            self.near = self.permute(sent, 1)

    def far_sum(self):
        dims, cols, size = self.dims, self.cols, self.count // len(self.names) * self.rows
        if dims.dp != 4:
            return [None] * len(self.names)

        def body(meta_ref, ins, outs):
            kept, near = ins
            mine = lax.div(Ids(meta_ref, dims).dp, 2)
            block = self.count * self.rows

            def half(i, piece):
                span = pl.ds(pl.multiple_of(i * block + piece * size, 16), size)
                return kept[span, :] + near[span, :].astype(F32)

            for piece, (sent, final) in enumerate(outs):
                sent[:size, :] = half(1 - mine, piece).astype(BF16)
                final[:size, :] = half(mine, piece)
                if self.small:
                    total = kept[2 * block :, :] + self.whole(near, 2 * block)
                    sent[size : size + SMALL, :], sent[size + SMALL :, :] = halved(total)
                    final[size:, :] = total

        out = (arr((size + self.extra, cols)), arr((size + self.extra // 2, cols), F32))
        outs = run(f"{self.name}_b", body, self.meta, (self.kept, self.near), [out] * len(self.names))
        self.final = [final for _, final in outs]
        return [sent for sent, _ in outs]

    def far_send(self, sent, piece):
        if self.dims.dp == 4:
            self.pieces[piece] = [self.final[piece], self.permute(sent[piece], 2)]

    def finish(self, piece, shapes, put, before=None):
        each = self.count // len(self.names)
        dims, rows, size = self.dims, self.rows, each * self.rows
        pieces = self.pieces[piece]
        flat = len(pieces)

        def body(meta_ref, ins, outs, *scratch):
            pieces, values, sems = ins[0], scratch[:-1], scratch[-1]

            def total(kind):
                if dims.dp != 4:
                    return pieces[0][kind].astype(F32)
                span = slice(kind * rows, (kind + 1) * rows)
                return pieces[0][span, :] + pieces[1][span, :].astype(F32)

            @pl.when(Ids(meta_ref, dims).section == self.layer)
            def _():
                small = None
                if self.small:
                    small = pieces[0][size:, :] + self.whole(pieces[1], size) if dims.dp == 4 else pieces[1][...]
                put(values, [total(index) for index in range(each)], small)
                for copy in copies(list(zip(values, outs)), sems):
                    copy.wait()

        outs = [InHbm(arr(shape, F32)) for shape in shapes]
        ins = [pieces] + ([] if before is None else [InHbm(a) for a in before])
        aliases = {} if before is None else {flat + i: i for i in range(len(shapes))}
        scratch = [pltpu.VMEM(shape, F32) for shape in shapes] + [pltpu.SemaphoreType.DMA((len(shapes),))]
        return run(f"{self.names[piece]}_end", body, self.meta, ins, outs, 8, scratch, aliases)


def pack_params(dims, meta, arrays):
    width = dims.width

    def body(meta_ref, ins, outs, *scratch):
        for copy in copies(list(zip(ins, scratch[:-1])), scratch[-1]):
            copy.wait()
        out_b, back_b, gains, shifts, in_b, qkv_b = scratch[:-1]
        for t in range(TYPES):
            for row, ref in ((OUT_B, out_b), (BACK_B, back_b), (IN_B, in_b)):
                outs[row + t : row + t + 1, :] = ref[0, t : t + 1, :]
            for row, ref in ((GAIN1, gains), (SHIFT1, shifts)):
                for norm in range(2):
                    outs[row + 2 * norm + t : row + 2 * norm + t + 1, :] = ref[0, t, norm : norm + 1, :]
            outs[QKV_B + t : QKV_B + t + 1, :] = jnp.zeros((1, dims.d), F32)
            outs[QKV_B + t : QKV_B + t + 1, :width] = qkv_b[0, t, 0:1, :]
            outs[QKV_B + t : QKV_B + t + 1, 2 * width : 3 * width] = qkv_b[0, t, 1:2, :]

    scratch = [pltpu.VMEM(a.shape, F32) for a in arrays] + [pltpu.SemaphoreType.DMA((len(arrays),))]
    return run("pack", body, meta, [InHbm(a) for a in arrays], arr((16, dims.d), F32), scratch=scratch)


def order_params(dims, meta, own, other):
    def body(meta_ref, ins, outs):
        here = meta_ref[0] == 0
        own, other = ins[0][...], ins[1][...]
        outs[0][...] = jnp.where(here, own, other)
        outs[1][...] = jnp.where(here, other, own)

    return run("params", body, meta, [own, other], [arr(own.shape, F32)] * 2)


def both_chains(dims, meta, own, moved, name):
    def body(meta_ref, ins, outs):
        own, moved = ins
        first = meta_ref[0] == 0

        @pl.when(first)
        def _():
            outs[0, 0] = own[0][...]
            outs[0, 1] = moved[0][...]

        @pl.when(jnp.logical_not(first))
        def _():
            outs[0, 0] = moved[1][...]
            outs[0, 1] = own[1][...]

    return run(name, body, meta, (own, moved), arr((1, 2, dims.length, dims.d), own[0].dtype), 8)


def body(
    tokens,
    cotangent,
    lengths,
    chain_type,
    qkv_weight,
    qkv_bias,
    out_weight,
    out_bias,
    ffn_in,
    ffn_in_bias,
    ffn_out,
    ffn_out_bias,
    norm_gain,
    norm_bias,
):
    dims = Dims()
    dims.per_chip, dims.length, dims.d = tokens.shape
    dims.slots = lax.axis_size("tensor")
    dims.dp = lax.axis_size("dp")
    dims.group = lengths.shape[0]
    dims.width = qkv_weight.shape[-1]
    dims.hidden = ffn_in.shape[-1]
    sections = lax.axis_size("section")
    assert dims.per_chip == sections == LAYERS and dims.slots & (dims.slots - 1) == 0
    assert dims.dp & (dims.dp - 1) == 0 and 4 * dims.width == dims.d == dims.hidden
    d, width, slots = dims.d, dims.width, dims.slots
    each = range(slots)
    section = lax.axis_index("section")
    meta = jnp.concatenate(
        [
            jnp.stack([section, lax.axis_index("tensor"), lax.axis_index("dp")]).astype(jnp.int32),
            chain_type,
            lengths,
        ]
    )

    own_rows = jnp.where(section == 0, tokens[0], tokens[1])
    rows = gather(own_rows, slots)

    qkv_own = qkv_weight[0].transpose(0, 2, 3, 1).reshape(TYPES, 3 * width, d)
    attn_own = [qkv_own, out_weight[0]]
    attn_other = [swap(w, "section", 1) for w in attn_own]
    biases = [qkv_bias, swap(qkv_bias, "section", 1)]
    packed = pack_params(
        dims, meta, (out_bias, ffn_out_bias, norm_gain, norm_bias, ffn_in_bias, qkv_bias)
    )
    small = order_params(dims, meta, packed, swap(packed, "section", 1))
    ffn_own = [ffn_in[0], ffn_out[0]]
    rows[0], small = tied(rows[0], small)

    def moved(value, layer):
        return lax.ppermute(value, "section", [(1 - layer, layer)])

    saved = []
    acts = []
    for layer in range(LAYERS):
        weight = fetch(dims, layer, meta, attn_own, attn_other, "attn")
        attn = [attention_forward(dims, layer, meta, k, rows[k], weight, biases) for k in each]
        parts, qkv, att = ([a[i] for a in attn] for i in range(3))
        parts = scatter(parts)
        if layer == 0:
            parts, ffn_sent = tied(parts, ffn_own)
            ffn_other = [swap(w, "section", 1) for w in ffn_sent]
        first = first_norm(dims, layer, meta, own_rows, parts, small[layer])
        normed = gather(first[0], slots)
        weight = fetch(dims, layer, meta, ffn_own, ffn_other, "ffn")
        ffn = [ffn_forward(dims, layer, meta, k, normed[k], weight, small[layer]) for k in each]
        parts, act, slope = ([f[i] for f in ffn] for i in range(3))
        parts = scatter(parts)
        if layer < LAYERS - 1:
            second = second_norm(dims, layer, meta, first[1], parts, small[layer])
        else:
            second = last_norm(dims, layer, meta, first[1], parts, small[layer], cotangent)
        saved.append((rows, qkv, att, first, normed, act, slope, second))
        own_rows = second[0]
        acts.append(own_rows)
        if layer < LAYERS - 1:
            rows = gather(own_rows, slots)

    share = d // dims.dp
    ffn_shapes = [(TYPES, share, dims.hidden)]
    attn_shapes = [
        (TYPES, 3, share, width),
        (TYPES, width, share),
        (1, TYPES, 2, width),
        (1, TYPES, d),
        (1, TYPES, dims.hidden),
        (1, TYPES, d),
        (1, TYPES, 2, d),
        (1, TYPES, 2, d),
    ]

    def put_ffn(outs, totals, small):
        for index, total in enumerate(totals):
            outs[index // TYPES][index % TYPES] = total

    def put_attn(outs, totals, small):
        qkv_out, out_out, qkv_b, out_b, in_b, back_b, gains, shifts = outs
        for kind, total in enumerate(totals):
            for i in range(3):
                qkv_out[kind, i] = total[:, i * width : (i + 1) * width]
            out_out[kind] = total[:, 3 * width :].T
            qkv_b[0, kind, 0:1, :] = small[QKV_SUMS + kind : QKV_SUMS + kind + 1, :width]
            qkv_b[0, kind, 1:2, :] = small[QKV_SUMS + kind : QKV_SUMS + kind + 1, 2 * width : 3 * width]
            in_b[0, kind : kind + 1, :] = small[IN_SUMS + kind : IN_SUMS + kind + 1, :]
            for norm, (base, bias) in enumerate(((FIRST_SUMS, out_b), (SECOND_SUMS, back_b))):
                row = base + 3 * kind
                gains[0, kind, norm : norm + 1, :] = small[row : row + 1, :]
                shifts[0, kind, norm : norm + 1, :] = small[row + 1 : row + 2, :]
                bias[0, kind : kind + 1, :] = small[row + 2 : row + 3, :]

    second_grad, low = second[1:]
    input_grads = [None] * LAYERS
    ffn_sums = [GradSum(dims, layer, meta, ("in", "back") if layer else ("ffn",), False) for layer in range(LAYERS)]
    attn_sums = [GradSum(dims, layer, meta, ("attn",), True) for layer in range(LAYERS)]
    for layer in reversed(range(LAYERS)):
        rows, qkv, att, first, normed, act, slope, second = saved[layer]
        top = layer == LAYERS - 1
        grads = gather(low, slots)
        weight = fetch(dims, layer, meta, ffn_own, ffn_other, "ffn_back")
        if top:
            acts_moved = [moved(acts[i], i) for i in range(LAYERS)]
        else:
            ffn_up, attn_up = ffn_sums[layer + 1], attn_sums[layer + 1]
            grads, near, ffn_up.pieces[1], ffn_far = tied(
                grads, attn_up.near_sum(), ffn_up.pieces[1], ffn_far
            )
            attn_sums[layer + 1].near_send(near)
            ffn_sums[layer + 1].far_send(ffn_far, 0)
        back = [ffn_backward(dims, layer, meta, k, grads[k], slope[k], weight) for k in each]
        parts, dpre = ([b[i] for b in back] for i in range(2))
        parts = scatter(parts)
        ffn_grad, below = ffn_weights(dims, layer, meta, normed, dpre, grads, act)
        if top:
            acts_out = both_chains(dims, meta, acts, acts_moved, "acts_out")
            parts, ffn_grad, acts_out = tied(parts, ffn_grad, acts_out)
        else:
            far = attn_up.far_sum()
            parts, ffn_grad, far, ffn_up.pieces[0] = tied(parts, ffn_grad, far, ffn_up.pieces[0])
            attn_sums[layer + 1].far_send(far, 0)
        ffn_sums[layer].start(ffn_grad)
        first_grad, low = first_back(
            dims, layer, meta, parts, second_grad, first[1], first[2], small[layer]
        )
        grads = gather(low, slots)
        weight = fetch(dims, layer, meta, attn_own, attn_other, "attn_back")
        near = ffn_sums[layer].near_sum()
        grads, _ = tied(grads, near)
        if not top:
            grads, attn_up.pieces[0] = tied(grads, attn_up.pieces[0])
        ffn_sums[layer].near_send(near)
        back = [attention_backward(dims, layer, meta, k, grads[k], qkv[k], weight) for k in each]
        parts, dqkv = ([b[i] for b in back] for i in range(2))
        parts = scatter(parts)
        attn_grad = attention_weights(dims, layer, meta, rows, dqkv, grads, att, below)
        if top:
            parts, attn_grad, ffn_far = tied(parts, attn_grad, ffn_sums[layer].far_sum())
            ffn_sums[layer].far_send(ffn_far, 1)
        attn_sums[layer].start(attn_grad)
        if layer > 0:
            second = saved[layer - 1][-1]
            input_grads[layer], second_grad, low = between_layers(
                dims, layer, meta, parts, first_grad, second[1], second[2], small[layer - 1]
            )
        else:
            input_grads[layer] = input_gradient(dims, layer, meta, parts, first_grad)

    back_done = ffn_up.finish(1, ffn_shapes, put_ffn)
    in_done = ffn_up.finish(0, ffn_shapes, put_ffn)
    attn_done = attn_up.finish(0, attn_shapes, put_attn)
    ffn_far = ffn_sums[0].far_sum()
    attn_sums[0].other, _ = tied(attn_sums[0].other, ffn_far)
    ffn_sums[0].far_send(ffn_far, 0)
    attn_sums[0].near_send(attn_sums[0].near_sum())
    attn_sums[0].far_send(attn_sums[0].far_sum(), 0)
    in_total, back_total = ffn_sums[0].finish(0, ffn_shapes * 2, put_ffn, in_done + back_done)
    grads_moved = [moved(input_grads[layer], layer) for layer in range(LAYERS)]
    grads_out = both_chains(dims, meta, input_grads, grads_moved, "grads_out")
    qkv_total, out_total, *small_grads = attn_sums[0].finish(0, attn_shapes, put_attn, attn_done)
    qkv_bias_out, out_bias_out, in_bias_out, back_bias_out, gain_out, shift_out = small_grads
    return (
        acts_out,
        grads_out,
        qkv_total.transpose(0, 2, 1, 3)[None],
        qkv_bias_out,
        out_total[None],
        out_bias_out,
        in_total[None],
        in_bias_out,
        back_total.transpose(0, 2, 1)[None],
        back_bias_out,
        gain_out,
        shift_out,
    )


def solution(mesh):
    placed = (
        P(("dp", "tensor"), None, None),
        P(("dp", "tensor"), None, None),
        P("dp"),
        P("dp"),
        P("section", None, None, None, "tensor"),
        P("section", None, None, "tensor"),
        P("section", None, "tensor", None),
        P("section", None, None),
        P("section", None, None, "tensor"),
        P("section", None, "tensor"),
        P("section", None, "tensor", None),
        P("section", None, None),
        P("section", None, None, None),
        P("section", None, None, None),
    )
    return jax.shard_map(
        body,
        mesh=mesh,
        in_specs=placed,
        out_specs=(
            P("section", ("dp", "tensor"), None, None),
            P("section", ("dp", "tensor"), None, None),
            P("section", None, "dp", None, "tensor"),
            P("section", None, None, "tensor"),
            P("section", None, "tensor", "dp"),
            P("section", None, None),
            P("section", None, "dp", "tensor"),
            P("section", None, "tensor"),
            P("section", None, "tensor", "dp"),
            P("section", None, None),
            P("section", None, None, None),
            P("section", None, None, None),
        ),
        check_vma=False,
    )
```
